32 devices in a mesh: rep: 2 (over core), mp: 16 (over z, y, x).
Axes of the slice: x: 2, y: 2, z: 4, core: 2. Of those that a mesh axis runs over, the one named last changes fastest.
Arguments:
- lookup_block: int32 [2, 2048, 16, 4], P(None, ('rep', 'mp')), may hold values from 0 to 9
- lookup_offset: int32 [2, 2048, 16, 4], P(None, ('rep', 'mp')), may hold values from 0 to 63
- interaction_grad: bfloat16 [2, 2048, 16, 16], P(None, ('rep', 'mp')), may hold values from -4 to 4
- table: bfloat16 [49152, 256], P('mp'), may hold values from -0.3125 to 0.3125
- adagrad_state: float32 [49152], P('mp'), may hold values from 0.05 to 2
- touched_blocks: int32 [16, 10], P('mp'), may hold values from 0 to 47, as said below
- dither: int32 [16, 640, 256], P('mp'), may hold values from 0 to 32767
Outputs:
- new_table: bfloat16 [49152, 256], P('mp')
- new_state: float32 [49152], P('mp')
The draws below stay inside these ranges and needn't reach their ends.
Inputs may be any that keep to these rules, and one draw needn't show every extreme that they name: `touched_blocks`: each row names 10 different row blocks.
All inputs are finite; a program needn't handle non-finite values.
Results may differ from the reference program's by a relative error of at most 0.00055.
The reference program's roundings to bfloat16 on the way count: a program that leaves them out, or rounds other values in their place, can miss the bound.
Values may be sent and summed in bfloat16 or wider, within the bound.
A program may use at most 128 MiB of HBM per device.

```python
import math
import jax
import jax.numpy as jnp
import numpy as np
from jax import lax

E = 256
MICRO = 2
BAG = 4
BLOCK = 64
TOUCH = 10
NBLK = 48
FEATURES = 16
SAMPLES = 2048
ROWS = 49152
N_MP = 16


def draw_touched_blocks(key, part):
    feature_keys = jax.random.split(jax.random.fold_in(key, 17), N_MP)

    def one_table(table_key):
        return jax.random.permutation(table_key, NBLK)[:TOUCH]
    return jax.vmap(one_table)(feature_keys).astype(jnp.int32)


def set_ends(values, stream_key, least, largest):
    extent = values.shape
    index_at = [jax.random.randint(jax.random.fold_in(stream_key, axis), (), 0, extent[axis]) for axis in range(len(extent))]
    values = values.at[tuple(index_at)].set(least)
    longest = extent.index(max(extent))
    index_at[longest] = (index_at[longest] + 1) % extent[longest]
    return values.at[tuple(index_at)].set(largest)


def block_scale(stream_key, shape, cuts, least, largest):
    level = 1.0
    for axis_at, parts in cuts:
        heights = jax.random.uniform(jax.random.fold_in(jax.random.fold_in(stream_key, 6), axis_at), (parts,), jnp.float32, least / len(cuts), largest / len(cuts))
        level = level * jnp.repeat(jnp.exp(heights), shape[axis_at] // parts).reshape((-1,) + (1,) * (len(shape) - 1 - axis_at))
    return level


def rank_table(number_of, skew):
    loads = [(1 << 20) // math.isqrt(grade ** skew) + 1 for grade in range(1, number_of + 1)]
    scale = 1 + sum(loads) // (1 << 30)
    return np.cumsum(np.array([max(1, weight // scale) for weight in loads]))


def ranked(key, shape, number_of, skew):
    grid = rank_table(number_of, skew)
    lot = jax.random.randint(jax.random.fold_in(key, 1), shape, 0, int(grid[number_of - 1]))
    grade = jnp.searchsorted(jnp.asarray(grid, jnp.int32), lot, side="right")
    return jax.random.permutation(jax.random.fold_in(key, 2), number_of)[grade].astype(jnp.int32)


def scatter_about(own_key, dims, scale, most, shards=(), held_as=jnp.bfloat16):
    loudness = block_scale(own_key, dims, shards, -0.22, 0.18) if shards else 1.0
    array = jax.random.normal(own_key, dims, jnp.float32) * scale * loudness
    return jnp.minimum(jnp.maximum(array, -most), most).astype(held_as)


def setup_inputs(seed: int = 0) -> dict:
    splits = jax.random.split(jax.random.key(seed), 8)
    return {
        "lookup_block": set_ends(ranked(splits[0], (MICRO, SAMPLES, FEATURES, BAG), TOUCH, 1), jax.random.fold_in(splits[0], 3), 0, TOUCH - 1).astype(jnp.int32),
        "lookup_offset": set_ends(jax.random.randint(splits[1], (MICRO, SAMPLES, FEATURES, BAG), 0, BLOCK), jax.random.fold_in(splits[1], 1), 0, BLOCK - 1).astype(jnp.int32),
        "interaction_grad": scatter_about(splits[2], (MICRO, SAMPLES, FEATURES, FEATURES), (FEATURES ** -0.5), 4.0, ((1, 32),)),
        "table": scatter_about(splits[3], (ROWS, E), 0.02, 0.3125, ((0, 16),)),
        "adagrad_state": jnp.clip(jnp.exp(math.log(2.0) - 3.6888794 * jax.random.uniform(splits[4], (ROWS,), jnp.float32) ** block_scale(splits[4], (ROWS,), ((0, 16),), -0.2, 0.2)), 0.05, 2.0),
        "touched_blocks": draw_touched_blocks(jax.random.fold_in(splits[7], 71), 0),
        "dither": set_ends(jax.random.randint(splits[6], (FEATURES, TOUCH * BLOCK, E), 0, 32768), jax.random.fold_in(splits[6], 1), 0, 32767).astype(jnp.int32),
    }


LEARN_RATE = 0.1
POOL_DECAY = 0.5
DITHER_UNIT = 2.0 ** (-15)
SMALLEST = 2.0 ** (-14)

def dither_round(weights, dither_bits):
    magnitude = jnp.maximum(jnp.abs(weights), SMALLEST)
    spacing = jnp.exp2(jnp.floor(jnp.log2(magnitude)) - 7.0)
    grid_level = jnp.floor(weights / spacing + dither_bits.astype(jnp.float32) * DITHER_UNIT)
    return (grid_level * spacing).astype(jnp.bfloat16)

def pairwise(pooled_rows, cotangent):
    pooled_wide = pooled_rows.astype(jnp.float32)
    cot_wide = cotangent.astype(jnp.float32)
    forward = jnp.einsum('bfg,bge->bfe', cot_wide, pooled_wide)
    backward = jnp.einsum('bgf,bge->bfe', cot_wide, pooled_wide)
    return (forward + backward + POOL_DECAY * pooled_wide).astype(jnp.bfloat16)

def reference(lookup_block, lookup_offset, interaction_grad, table, adagrad_state, touched_blocks, dither):
    slab_size = TOUCH * BLOCK
    table_blocks = table.reshape(N_MP, NBLK, BLOCK, E)
    feature_ids = jnp.arange(N_MP, dtype=jnp.int32)[:, None]
    chosen = table_blocks[feature_ids, touched_blocks]
    slab_table = chosen.reshape(N_MP * slab_size, E)
    feature_base = (jnp.arange(N_MP, dtype=jnp.int32) * slab_size)[None, None, :, None]
    slab_index = (lookup_block * BLOCK + lookup_offset + feature_base).astype(jnp.int32)
    sample_block = math.gcd(256, SAMPLES)
    steps_count = MICRO * SAMPLES // sample_block
    blocked_index = slab_index.reshape(steps_count, sample_block, N_MP, BAG)
    blocked_cot = interaction_grad.reshape(steps_count, sample_block, N_MP, N_MP)

    def accumulate(carry, pieces):
        index_piece, cot_piece = pieces
        gathered = slab_table[index_piece].astype(jnp.float32)
        pooled_rows = lax.optimization_barrier(jnp.sum(gathered, axis=2)).astype(jnp.bfloat16)
        back_rows = pairwise(pooled_rows, cot_piece).astype(jnp.float32)
        spread = jnp.broadcast_to(back_rows[:, :, None, :], gathered.shape).reshape(-1, E)
        carry = carry + jax.ops.segment_sum(spread, index_piece.reshape(-1), num_segments=N_MP * slab_size)
        return (carry, None)
    start_grad = jnp.zeros((N_MP * slab_size, E), jnp.float32)
    slab_grad, _ = lax.scan(accumulate, start_grad, (blocked_index, blocked_cot))
    state_blocks = adagrad_state.reshape(N_MP, NBLK, BLOCK)
    state_slab = state_blocks[feature_ids, touched_blocks].reshape(N_MP * slab_size)
    state_next = state_slab + lax.optimization_barrier(jnp.mean(slab_grad * slab_grad, axis=-1))
    moved = slab_table.astype(jnp.float32) - LEARN_RATE * slab_grad / (jnp.sqrt(state_next) + 1e-08)[:, None]
    rounded = dither_round(moved, dither.reshape(N_MP * slab_size, E))
    new_table = table_blocks.at[feature_ids, touched_blocks].set(rounded.reshape(N_MP, TOUCH, BLOCK, E))
    new_state = state_blocks.at[feature_ids, touched_blocks].set(state_next.reshape(N_MP, TOUCH, BLOCK))
    return (new_table.reshape(ROWS, E), new_state.reshape(ROWS))
```

```python
import functools
import math

import jax
import jax.numpy as jnp
from jax import lax
from jax.experimental import pallas as pl
from jax.experimental.pallas import tpu as pltpu
from jax.sharding import PartitionSpec as P

BLOCK = 64
PLANES = 4
PARTS = 2
LEARN_RATE = 0.1
POOL_DECAY = 0.5
DITHER_UNIT = 2.0 ** (-15)
SMALLEST = 2.0 ** (-14)
KEEP_BYTES = 8 << 20
MESH = pl.DeviceIdType.MESH


def dither_round(weights, dither_bits):
    magnitude = jnp.maximum(jnp.abs(weights), SMALLEST)
    spacing = jnp.exp2(jnp.floor(jnp.log2(magnitude)) - 7.0)
    grid_level = jnp.floor(weights / spacing + dither_bits.astype(jnp.float32) * DITHER_UNIT)
    return (grid_level * spacing).astype(jnp.bfloat16)


def plane_order(planes, plane, step):
    picked = jnp.int32(0)
    for own in range(planes):
        near_first = sorted(range(planes), key=lambda q: (abs(q - own), (q - own) * (2 * own - planes)))
        picked = jnp.where(plane == own, near_first[step], picked)
    return picked


def step_kernel(
    n,
    block_hbm,
    offset_hbm,
    cot_ref,
    touched_ref,
    state_hbm,
    table_ref,
    dither_ref,
    out_ref,
    state_out_ref,
    table_in,
    block_ref,
    offset_ref,
    state_ref,
    rows_ref,
    cot_in,
    near,
    far,
    w_ref,
    dither_in,
    slab,
    slabs,
    pooled_out,
    pooled_in,
    grad_out,
    grad_in,
    kept,
    kept_own,
    total,
    total_in,
    state_col,
    local_sem,
    pair_sem,
    near_send,
    near_recv,
    far_send,
    far_recv,
    slab_send,
    slab_recv,
    half_send,
    half_recv,
    pooled_send,
    pooled_recv,
    grad_send,
    grad_recv,
):
    me = lax.axis_index("mp")
    rep = lax.axis_index("rep")
    planes, parts = slabs.shape[0], slabs.shape[1]
    m = n // planes
    plane = me // m
    local = lax.rem(me, m)
    samples = w_ref.shape[1]
    bags = rows_ref.shape[3]
    slab_size, width = slab.shape
    columns = width // parts
    touch_count = slab_size // BLOCK
    keeps = kept.shape[0] == planes

    def at(peer):
        return {"device_id": (rep, peer), "device_id_type": MESH}

    partner = {"device_id": (1 - rep, me), "device_id_type": MESH}

    def each(first, body):
        def run(step, carry):
            body(lax.rem(local + step, m))
            return carry

        lax.fori_loop(first, m, run, 0)

    def others(body):
        def run(step, carry):
            body(lax.rem(me + step, n))
            return carry

        lax.fori_loop(1, n, run, 0)

    def outside(body, first=0, last=n - m):
        def run(step, carry):
            body(lax.rem(plane + 1 + step // m, planes), lax.rem(local + step, m))
            return carry

        lax.fori_loop(first, last, run, 0)

    def nearest(step):
        return plane_order(planes, plane, step)

    barrier = pltpu.get_barrier_semaphore()
    others(lambda peer: pl.semaphore_signal(barrier, inc=1, **at(peer)))
    pl.semaphore_signal(barrier, inc=1, **partner)
    table_copy = pltpu.make_async_copy(table_ref, table_in, local_sem.at[0])
    table_copy.start()
    block_copy = pltpu.make_async_copy(block_hbm, block_ref, local_sem.at[1])
    block_copy.start()
    offset_copy = pltpu.make_async_copy(offset_hbm, offset_ref, local_sem.at[2])
    offset_copy.start()
    state_copy = pltpu.make_async_copy(state_hbm, state_ref, local_sem.at[3])
    state_copy.start()
    dither_copy = pltpu.make_async_copy(dither_ref, dither_in, local_sem.at[4])
    dither_copy.start()
    block_copy.wait()
    offset_copy.wait()
    rows_ref[...] = block_ref[...] * BLOCK + offset_ref[...]
    near[local] = rows_ref[:, :, local]
    table_copy.wait()
    for block in range(touch_count):
        slab[block * BLOCK : (block + 1) * BLOCK, :] = table_in[touched_ref[0, block]]
    for part in range(parts):
        turned = slab[:, part * columns : (part + 1) * columns].astype(jnp.float32).T
        slabs[plane, part] = turned.astype(jnp.bfloat16).reshape(slabs.shape[2:])
    pl.semaphore_wait(barrier, n)

    def near_copy(j, slot):
        return pltpu.make_async_remote_copy(
            rows_ref.at[:, :, j],
            near.at[slot],
            near_send.at[j],
            near_recv.at[slot],
            **at(plane * m + j),
        )

    def far_copy(q, j, slot):
        return pltpu.make_async_remote_copy(
            rows_ref.at[:, q, j],
            far.at[slot],
            far_send.at[q * m + j],
            far_recv.at[slot],
            **at(q * m + j),
        )

    def slab_copy(part, q, way, peer):
        return pltpu.make_async_remote_copy(
            slabs.at[q, part, rep],
            slabs.at[q, part, rep],
            slab_send.at[way, part, q],
            slab_recv.at[part, q],
            **at(peer),
        )

    def half_copy(part, q, which):
        return pltpu.make_async_remote_copy(
            slabs.at[q, part, which],
            slabs.at[q, part, which],
            half_send.at[part, q],
            half_recv.at[part, q],
            **partner,
        )

    has_up, has_down = plane + 1 < planes, plane > 0
    inner = jnp.logical_and(has_up, has_down)
    outer = jnp.logical_not(inner)
    up, down = lax.rem(me + m, n), lax.rem(me + n - m, n)

    def own_slab(part, act):
        @pl.when(has_up)
        def _():
            act(slab_copy(part, plane, 0, up))

        @pl.when(has_down)
        def _():
            act(slab_copy(part, plane, 1, down))

    def passed_slab(part, q, act):
        @pl.when(jnp.logical_and(q < plane, has_up))
        def _():
            act(slab_copy(part, q, 0, up))

        @pl.when(jnp.logical_and(q > plane, has_down))
        def _():
            act(slab_copy(part, q, 1, down))

    each(1, lambda j: near_copy(j, local).start())
    own_slab(0, lambda copy: copy.start())
    outside(lambda q, j: far_copy(q, j, me).start())
    for part in range(1, parts):
        own_slab(part, lambda copy: copy.start())
    cot_size = cot_in.shape[1]

    def spread(chunk, carry):
        cot_copy = pltpu.make_async_copy(
            cot_ref.at[:, pl.ds(chunk * cot_size, cot_size)], cot_in, local_sem.at[5]
        )
        cot_copy.start()
        cot_copy.wait()
        for i in range(cot_size):
            pieces = [cot_in[micro, i].astype(jnp.float32) for micro in range(cot_in.shape[0])]
            at_row = pl.multiple_of((chunk * cot_size + i) * n, n)
            w_ref[pl.ds(at_row, n), :] = jnp.concatenate(pieces, axis=-1)
        return carry

    lax.fori_loop(0, n // cot_size, spread, 0)
    place = lax.broadcasted_iota(jnp.int32, (n, samples), 0)

    def fold(f, carry):
        along = pl.ds(pl.multiple_of(f * n, n), n)
        across = pl.ds(f, n, stride=n)
        row, column = w_ref[along, :], w_ref[across, :]
        both = row + column + jnp.where(place == f, POOL_DECAY, 0.0)
        w_ref[along, :] = jnp.where(place >= f, both, row)
        w_ref[across, :] = jnp.where(place >= f, both, column)
        return carry

    lax.fori_loop(0, n, fold, 0)
    total[...] = jnp.zeros_like(total)

    offset_in_block = lax.broadcasted_iota(jnp.int32, (BLOCK, samples), 0)
    offset_in_block = offset_in_block.astype(jnp.float32).astype(jnp.bfloat16)
    one = jnp.ones((BLOCK, samples), jnp.bfloat16)

    def hits(micros):
        rows = jnp.concatenate([micros[i] for i in range(micros.shape[0])], axis=-1)
        blocks = []
        block_of, offset_of = rows // BLOCK, lax.rem(rows, BLOCK)
        for block in range(slab_size // BLOCK):
            wanted = jnp.where(block_of == block, offset_of, -1).astype(jnp.float32)
            counted = jnp.zeros((BLOCK, samples), jnp.bfloat16)
            for lookup in range(bags):
                row = jnp.broadcast_to(wanted[lookup : lookup + 1, :], (BLOCK, samples))
                same = row.astype(jnp.bfloat16) == offset_in_block
                counted = counted + jnp.where(same, one, jnp.zeros_like(one))
            blocks.append(counted)
        return jnp.concatenate(blocks, axis=0)

    def pooled_copy(part, q, j, slot):
        return pltpu.make_async_remote_copy(
            pooled_out.at[part, q, j],
            pooled_in.at[part, q * m + slot],
            pooled_send.at[part, q, j],
            pooled_recv.at[part, q * m + slot],
            **at(plane * m + j),
        )

    def grad_copy(part, peer, slot):
        return pltpu.make_async_remote_copy(
            grad_out.at[part, peer],
            grad_in.at[part, slot],
            grad_send.at[part, peer],
            grad_recv.at[part, slot],
            **at(peer),
        )

    def pool(part, q):
        rows_of = slabs[q, part].reshape(columns, slab_size)

        def pooled(j):
            if keeps and part > 0:
                counted = kept[q, j]
            else:
                counted = hits(near[j, :, q])
                if keeps:
                    kept[q, j] = counted
            summed = jnp.dot(rows_of, counted, preferred_element_type=jnp.float32)
            return summed.astype(jnp.bfloat16)

        def send(j):
            pooled_out[part, q, j] = pooled(j)
            pooled_copy(part, q, j, local).start()

        each(1, send)
        pooled_in[part, q * m + local] = pooled(local)

    def relay(part, step):
        q = nearest(step)
        slab_copy(part, q, 0, up).wait_recv()
        passed_slab(part, q, lambda copy: copy.start())
        half_copy(part, q, rep).start()

    def pool_from(part, step):
        q = nearest(step)
        half_copy(part, q, 1 - rep).wait_recv()
        pool(part, q)

    def arrive(part):
        def take(j):
            for q in range(planes):
                pooled_copy(part, q, j, j).wait_recv()

        each(1, take)

    def interact(part):
        def mixed(feature):
            def add(other, carry):
                weight = w_ref[pl.ds(feature * n + other, 1), :]
                return carry + weight * pooled_in[part, other].astype(jnp.float32)

            start = jnp.zeros((columns, samples), jnp.float32)
            return lax.fori_loop(0, n, add, start, unroll=4).astype(jnp.bfloat16)

        def send(peer):
            grad_out[part, peer] = mixed(peer)
            grad_copy(part, peer, me).start()

        for step in range(planes - 1, 0, -1):
            q = nearest(step)
            each(0, lambda j: send(q * m + j))
        each(1, lambda j: send(plane * m + j))
        grad_in[part, me] = mixed(me)

    def keep_far(first, last):
        def take(q, j):
            peer = q * m + j
            far_copy(q, j, peer).wait_recv()
            if keeps:
                kept_own[peer] = hits(far[peer])

        outside(take, first, last)

    def collect(part):
        def add(peer, counted):
            total[part] += lax.dot_general(
                counted,
                grad_in[part, peer],
                (((1,), (1,)), ((), ())),
                preferred_element_type=jnp.float32,
            )

        def near_hits(j):
            return kept[plane, j] if keeps else hits(near[j, :, plane])

        def take_near(j):
            grad_copy(part, plane * m + j, plane * m + j).wait_recv()
            add(plane * m + j, near_hits(j))

        def take_far(q, j):
            peer = q * m + j
            grad_copy(part, peer, peer).wait_recv()
            add(peer, kept_own[peer] if keeps else hits(far[peer]))

        add(me, near_hits(local))
        each(1, take_near)
        for step in range(1, planes):
            q = nearest(step)
            each(0, lambda j: take_far(q, j))

    each(1, lambda j: near_copy(j, j).wait_recv())
    pool(0, plane)
    relay(0, 1)
    pl.when(inner)(lambda: relay(0, 2))
    pool_from(0, 1)
    relay(1, 1)
    pl.when(inner)(lambda: relay(1, 2))
    pool(1, plane)
    pl.when(inner)(lambda: relay(0, 3))
    pool_from(1, 1)
    pl.when(outer)(lambda: relay(0, 2))
    pool_from(0, 2)
    pl.when(inner)(lambda: relay(1, 3))
    pl.when(outer)(lambda: relay(1, 2))
    pool_from(1, 2)
    pl.when(outer)(lambda: relay(0, 3))
    pool_from(0, 3)
    pl.when(outer)(lambda: relay(1, 3))
    pool_from(1, 3)
    early = jnp.where(inner, 0, n - m)
    keep_far(0, early)
    arrive(0)
    pl.when(outer)(lambda: arrive(1))
    interact(0)
    keep_far(early, n - m)
    pl.when(inner)(lambda: arrive(1))
    interact(1)
    state_copy.wait()
    pieces = []
    for block in range(touch_count):
        at_block = touched_ref[0, block]
        pair = state_ref[pl.ds(at_block // 2, 1), :]
        pieces.append(jnp.where(lax.rem(at_block, 2) == 0, pair[:, :BLOCK], pair[:, BLOCK:]))
    state_row = jnp.concatenate(pieces, axis=1)
    state_col[...] = jnp.broadcast_to(state_row, (state_col.shape[1], slab_size)).T
    def total_copy(part):
        return pltpu.make_async_remote_copy(
            total.at[part], total_in.at[part], pair_sem.at[0, part], pair_sem.at[1, part], **partner
        )

    collect(0)
    total_copy(0).start()
    each(1, lambda j: near_copy(j, j).wait_send())
    outside(lambda q, j: far_copy(q, j, me).wait_send())
    for part in range(parts):
        own_slab(part, lambda copy: copy.wait_send())
        for step in range(1, planes):
            q = nearest(step)
            passed_slab(part, q, lambda copy: copy.wait_send())
            half_copy(part, q, rep).wait_send()
        for q in range(planes):
            each(1, lambda j: pooled_copy(part, q, j, j).wait_send())
    others(lambda peer: grad_copy(0, peer, me).wait_send())
    dither_copy.wait()
    collect(1)
    total_copy(1).start()
    others(lambda peer: grad_copy(1, peer, me).wait_send())
    for part in range(parts):
        total_copy(part).wait_recv()

    def update(block, carry):
        at_rows = pl.ds(pl.multiple_of(block * BLOCK, BLOCK), BLOCK)
        grad = [total[part, at_rows, :] + total_in[part, at_rows, :] for part in range(parts)]
        grad = jnp.concatenate(grad, axis=1)
        state_next = state_col[at_rows, :] + jnp.sum(grad * grad, axis=1, keepdims=True) / width
        state_col[at_rows, :] = state_next
        divisor = jnp.sqrt(state_next) + 1e-08
        divisor = jnp.concatenate([divisor] * (width // divisor.shape[1]), axis=1)
        moved = slab[at_rows, :].astype(jnp.float32) - LEARN_RATE * grad / divisor
        out_ref[at_rows, :] = dither_round(moved, dither_in[at_rows, :])
        return carry

    lax.fori_loop(0, touch_count, update, 0, unroll=2)
    state_all = state_ref[...]
    block_at = 2 * lax.broadcasted_iota(jnp.int32, state_all.shape, 0)
    block_at = block_at + lax.broadcasted_iota(jnp.int32, state_all.shape, 1) // BLOCK
    state_row = state_col[...].T[:1, :]
    for block in range(touch_count):
        piece = state_row[:, block * BLOCK : (block + 1) * BLOCK]
        piece = jnp.broadcast_to(jnp.concatenate([piece, piece], axis=1), state_all.shape)
        state_all = jnp.where(block_at == touched_ref[0, block], piece, state_all)
    state_out_ref[...] = state_all
    for part in range(parts):
        total_copy(part).wait_send()


def fused_step(n, blocks, offsets, cot, touched, state, table, dither):
    micros, planes, m = blocks.shape[0], blocks.shape[1], blocks.shape[2]
    sample_count = blocks.shape[-1]
    samples = micros * sample_count
    cot_size = math.gcd(n, 16)
    slab_size, width = dither.shape
    columns = width // PARTS
    keeps = 2 * n * slab_size * samples <= KEEP_BYTES
    dma = pltpu.SemaphoreType.DMA
    block = (PARTS, n, columns, samples)
    vmem = pl.BlockSpec(memory_space=pltpu.VMEM)
    smem = pl.BlockSpec(memory_space=pltpu.SMEM)
    hbm = pl.BlockSpec(memory_space=pltpu.HBM)
    return pl.pallas_call(
        functools.partial(step_kernel, n),
        out_shape=(
            pltpu.VMEM((slab_size, width), jnp.bfloat16),
            pltpu.VMEM(state.shape, jnp.float32),
            pltpu.VMEM(table.shape, jnp.bfloat16),
        ),
        in_specs=[hbm, hbm, hbm, smem, hbm, hbm, hbm],
        out_specs=(vmem, vmem, vmem),
        scratch_shapes=[
            pltpu.VMEM(blocks.shape, jnp.int32),
            pltpu.VMEM(blocks.shape, jnp.int32),
            pltpu.VMEM(state.shape, jnp.float32),
            pltpu.VMEM(blocks.shape, jnp.int32),
            pltpu.VMEM((micros, cot_size, n, sample_count), jnp.bfloat16),
            pltpu.VMEM((m, micros, planes) + blocks.shape[3:], jnp.int32),
            pltpu.VMEM((n, micros) + blocks.shape[3:], jnp.int32),
            pltpu.VMEM((n * n, samples), jnp.float32),
            pltpu.VMEM((slab_size, width), jnp.int32),
            pltpu.VMEM((slab_size, width), jnp.bfloat16),
            pltpu.VMEM((planes, PARTS, 2, columns // 2, slab_size), jnp.bfloat16),
            pltpu.VMEM((PARTS, planes, m, columns, samples), jnp.bfloat16),
            pltpu.VMEM(block, jnp.bfloat16),
            pltpu.VMEM(block, jnp.bfloat16),
            pltpu.VMEM(block, jnp.bfloat16),
            pltpu.VMEM((planes if keeps else 1, m if keeps else 1, slab_size, samples), jnp.bfloat16),
            pltpu.VMEM((n if keeps else 1, slab_size, samples), jnp.bfloat16),
            pltpu.VMEM((PARTS, slab_size, columns), jnp.float32),
            pltpu.VMEM((PARTS, slab_size, columns), jnp.float32),
            pltpu.VMEM((slab_size, 128), jnp.float32),
            dma((6,)),
            dma((2, PARTS)),
            dma((m,)),
            dma((m,)),
            dma((n,)),
            dma((n,)),
            dma((2, PARTS, planes)),
            dma((PARTS, planes)),
            dma((PARTS, planes)),
            dma((PARTS, planes)),
            dma((PARTS, planes, m)),
            dma((PARTS, n)),
            dma((PARTS, n)),
            dma((PARTS, n)),
        ],
        compiler_params=pltpu.CompilerParams(collective_id=0, has_side_effects=True),
        name="fused_step",
    )(blocks, offsets, cot, touched, state, table, dither)


def write_kernel(touched_ref, new_ref, state_ref, table_ref, out_ref, state_out_ref, place, sem):
    state_copy = pltpu.make_async_copy(state_ref, state_out_ref, sem.at[1])
    state_copy.start()
    blocks, touch_count = table_ref.shape[0], touched_ref.shape[1]

    def clear(block, carry):
        place[block] = -1
        return carry

    lax.fori_loop(0, blocks, clear, 0, unroll=8)
    for i in range(touch_count):
        place[touched_ref[0, i]] = i

    def write(block, carry):
        new = place[block]

        @pl.when(new >= 0)
        def _():
            pltpu.make_async_copy(new_ref.at[new], out_ref.at[block], sem.at[0]).start()

        @pl.when(new < 0)
        def _():
            pltpu.make_async_copy(table_ref.at[block], out_ref.at[block], sem.at[0]).start()

        return carry

    lax.fori_loop(0, blocks, write, 0)
    pltpu.make_async_copy(table_ref, out_ref, sem.at[0]).wait()
    state_copy.wait()


def write_table(touched, new_rows, state, table):
    vmem = pl.BlockSpec(memory_space=pltpu.VMEM)
    hbm = pl.BlockSpec(memory_space=pltpu.HBM)
    held = [pltpu.with_memory_space_constraint(x, pltpu.VMEM) for x in (new_rows, state, table)]
    return pl.pallas_call(
        write_kernel,
        out_shape=(
            jax.ShapeDtypeStruct(table.shape, table.dtype),
            jax.ShapeDtypeStruct(state.shape, state.dtype),
        ),
        in_specs=[pl.BlockSpec(memory_space=pltpu.SMEM), vmem, vmem, vmem],
        out_specs=(hbm, hbm),
        scratch_shapes=[pltpu.SMEM((table.shape[0],), jnp.int32), pltpu.SemaphoreType.DMA((2,))],
        compiler_params=pltpu.CompilerParams(vmem_limit_bytes=4 << 20),
        name="write_table",
    )(touched, *held)


def per_device(
    lookup_block, lookup_offset, interaction_grad, table, adagrad_state, touched_blocks, dither
):
    micro_count, sample_count, feature_count, bag_count = lookup_block.shape
    n = lax.axis_size("mp")
    row_count, emb_width = table.shape
    touch_count = touched_blocks.shape[1]
    split = (micro_count, PLANES, feature_count // PLANES, bag_count, sample_count)
    blocks = lookup_block.transpose(0, 2, 3, 1).reshape(split)
    offsets = lookup_offset.transpose(0, 2, 3, 1).reshape(split)
    cot = interaction_grad.transpose(0, 2, 3, 1)
    table_blocks = table.reshape(row_count // BLOCK, BLOCK, emb_width)
    state = adagrad_state.reshape(row_count // (2 * BLOCK), 2 * BLOCK)
    new_rows, new_state, table_copy = fused_step(
        n, blocks, offsets, cot, touched_blocks, state, table_blocks, dither[0]
    )
    new_rows = new_rows.reshape(touch_count, BLOCK, emb_width)
    new_table, new_state = write_table(touched_blocks, new_rows, new_state, table_copy)
    return (new_table.reshape(row_count, emb_width), new_state.reshape(row_count))


def solution(mesh):
    return jax.shard_map(
        per_device,
        mesh=mesh,
        in_specs=(
            P(None, ("rep", "mp"), None, None),
            P(None, ("rep", "mp"), None, None),
            P(None, ("rep", "mp"), None, None),
            P("mp", None),
            P("mp"),
            P("mp", None),
            P("mp", None, None),
        ),
        out_specs=(P("mp", None), P("mp")),
        check_vma=False,
    )
```

```python
import functools
import math

import jax
import jax.numpy as jnp
from jax import lax
from jax.experimental import pallas as pl
from jax.experimental.pallas import tpu as pltpu
from jax.sharding import PartitionSpec as P

BLOCK = 64
PLANES = 4
PARTS = 2
LEARN_RATE = 0.1
POOL_DECAY = 0.5
DITHER_UNIT = 2.0 ** (-15)
SMALLEST = 2.0 ** (-14)
KEEP_BYTES = 8 << 20
MESH = pl.DeviceIdType.MESH


def dither_round(weights, dither_bits):
    magnitude = jnp.maximum(jnp.abs(weights), SMALLEST)
    spacing = jnp.exp2(jnp.floor(jnp.log2(magnitude)) - 7.0)
    grid_level = jnp.floor(weights / spacing + dither_bits.astype(jnp.float32) * DITHER_UNIT)
    return (grid_level * spacing).astype(jnp.bfloat16)


def plane_order(planes, plane, step):
    picked = jnp.int32(0)
    for own in range(planes):
        near_first = sorted(range(planes), key=lambda q: (abs(q - own), (q - own) * (2 * own - planes)))
        picked = jnp.where(plane == own, near_first[step], picked)
    return picked


def step_kernel(
    n,
    block_hbm,
    offset_hbm,
    cot_ref,
    touched_ref,
    state_hbm,
    table_ref,
    dither_ref,
    out_ref,
    state_out_ref,
    table_in,
    block_ref,
    offset_ref,
    state_ref,
    rows_ref,
    cot_in,
    near,
    far,
    w_ref,
    dither_in,
    slab,
    slabs,
    pooled_out,
    pooled_in,
    grad_out,
    grad_in,
    kept,
    kept_own,
    total,
    total_in,
    state_col,
    local_sem,
    pair_sem,
    near_send,
    near_recv,
    far_send,
    far_recv,
    slab_send,
    slab_recv,
    half_send,
    half_recv,
    pooled_send,
    pooled_recv,
    grad_send,
    grad_recv,
):
    me = lax.axis_index("mp")
    rep = lax.axis_index("rep")
    planes, parts = slabs.shape[0], slabs.shape[1]
    m = n // planes
    plane = me // m
    local = lax.rem(me, m)
    samples = w_ref.shape[1]
    bags = rows_ref.shape[3]
    slab_size, width = slab.shape
    columns = width // parts
    touch_count = slab_size // BLOCK
    keeps = kept.shape[0] == planes

    def at(peer):
        return {"device_id": (rep, peer), "device_id_type": MESH}

    partner = {"device_id": (1 - rep, me), "device_id_type": MESH}

    def each(first, body):
        def run(step, carry):
            body(lax.rem(local + step, m))
            return carry

        lax.fori_loop(first, m, run, 0)

    def others(body):
        def run(step, carry):
            body(lax.rem(me + step, n))
            return carry

        lax.fori_loop(1, n, run, 0)

    def outside(body, first=0, last=n - m):
        def run(step, carry):
            body(lax.rem(plane + 1 + step // m, planes), lax.rem(local + step, m))
            return carry

        lax.fori_loop(first, last, run, 0)

    def nearest(step):
        return plane_order(planes, plane, step)

    barrier = pltpu.get_barrier_semaphore()
    others(lambda peer: pl.semaphore_signal(barrier, inc=1, **at(peer)))
    pl.semaphore_signal(barrier, inc=1, **partner)
    table_copy = pltpu.make_async_copy(table_ref, table_in, local_sem.at[0])
    table_copy.start()
    block_copy = pltpu.make_async_copy(block_hbm, block_ref, local_sem.at[1])
    block_copy.start()
    offset_copy = pltpu.make_async_copy(offset_hbm, offset_ref, local_sem.at[2])
    offset_copy.start()
    state_copy = pltpu.make_async_copy(state_hbm, state_ref, local_sem.at[3])
    state_copy.start()
    dither_copy = pltpu.make_async_copy(dither_ref, dither_in, local_sem.at[4])
    dither_copy.start()
    block_copy.wait()
    offset_copy.wait()
    rows_ref[...] = block_ref[...] * BLOCK + offset_ref[...]
    near[local] = rows_ref[:, :, local]
    table_copy.wait()
    for block in range(touch_count):
        slab[block * BLOCK : (block + 1) * BLOCK, :] = table_in[touched_ref[0, block]]
    for part in range(parts):
        turned = slab[:, part * columns : (part + 1) * columns].astype(jnp.float32).T
        slabs[plane, part] = turned.astype(jnp.bfloat16).reshape(slabs.shape[2:])
    pl.semaphore_wait(barrier, n)

    def near_copy(j, slot):
        return pltpu.make_async_remote_copy(
            rows_ref.at[:, :, j],
            near.at[slot],
            near_send,
            near_recv,
            **at(plane * m + j),
        )

    def far_copy(q, j, slot):
        return pltpu.make_async_remote_copy(
            rows_ref.at[:, q, j],
            far.at[slot],
            far_send,
            far_recv,
            **at(q * m + j),
        )

    def slab_copy(part, q, way, peer):
        return pltpu.make_async_remote_copy(
            slabs.at[q, part, rep],
            slabs.at[q, part, rep],
            slab_send.at[way, part, q],
            slab_recv.at[part, q],
            **at(peer),
        )

    def half_copy(part, q, which):
        return pltpu.make_async_remote_copy(
            slabs.at[q, part, which],
            slabs.at[q, part, which],
            half_send,
            half_recv.at[part, q],
            **partner,
        )

    has_up, has_down = plane + 1 < planes, plane > 0
    inner = jnp.logical_and(has_up, has_down)
    outer = jnp.logical_not(inner)
    up, down = lax.rem(me + m, n), lax.rem(me + n - m, n)

    def own_slab(part, act):
        @pl.when(has_up)
        def _():
            act(slab_copy(part, plane, 0, up))

        @pl.when(has_down)
        def _():
            act(slab_copy(part, plane, 1, down))

    def passed_slab(part, q, act):
        @pl.when(jnp.logical_and(q < plane, has_up))
        def _():
            act(slab_copy(part, q, 0, up))

        @pl.when(jnp.logical_and(q > plane, has_down))
        def _():
            act(slab_copy(part, q, 1, down))

    each(1, lambda j: near_copy(j, local).start())
    own_slab(0, lambda copy: copy.start())
    outside(lambda q, j: far_copy(q, j, me).start())

    @pl.when(outer)
    def _():
        own_slab(1, lambda copy: copy.start())

    cot_size = cot_in.shape[1]

    def spread(chunk, carry):
        cot_copy = pltpu.make_async_copy(
            cot_ref.at[:, pl.ds(chunk * cot_size, cot_size)], cot_in, local_sem.at[5]
        )
        cot_copy.start()
        cot_copy.wait()
        for i in range(cot_size):
            pieces = [cot_in[micro, i].astype(jnp.float32) for micro in range(cot_in.shape[0])]
            at_row = pl.multiple_of((chunk * cot_size + i) * n, n)
            w_ref[pl.ds(at_row, n), :] = jnp.concatenate(pieces, axis=-1)
        return carry

    lax.fori_loop(0, n // cot_size, spread, 0)
    place = lax.broadcasted_iota(jnp.int32, (n, samples), 0)

    def fold(f, carry):
        along = pl.ds(pl.multiple_of(f * n, n), n)
        across = pl.ds(f, n, stride=n)
        row, column = w_ref[along, :], w_ref[across, :]
        both = row + column + jnp.where(place == f, POOL_DECAY, 0.0)
        w_ref[along, :] = jnp.where(place >= f, both, row)
        w_ref[across, :] = jnp.where(place >= f, both, column)
        return carry

    lax.fori_loop(0, n, fold, 0)
    total[...] = jnp.zeros_like(total)

    offset_in_block = lax.broadcasted_iota(jnp.int32, (BLOCK, samples), 0)
    offset_in_block = offset_in_block.astype(jnp.float32).astype(jnp.bfloat16)
    one = jnp.ones((BLOCK, samples), jnp.bfloat16)

    def hits(micros):
        rows = jnp.concatenate([micros[i] for i in range(micros.shape[0])], axis=-1)
        blocks = []
        block_of, offset_of = rows // BLOCK, lax.rem(rows, BLOCK)
        for block in range(slab_size // BLOCK):
            wanted = jnp.where(block_of == block, offset_of, -1).astype(jnp.float32)
            counted = jnp.zeros((BLOCK, samples), jnp.bfloat16)
            for lookup in range(bags):
                row = jnp.broadcast_to(wanted[lookup : lookup + 1, :], (BLOCK, samples))
                same = row.astype(jnp.bfloat16) == offset_in_block
                counted = counted + jnp.where(same, one, jnp.zeros_like(one))
            blocks.append(counted)
        return jnp.concatenate(blocks, axis=0)

    def pooled_copy(part, q, j, slot):
        return pltpu.make_async_remote_copy(
            pooled_out.at[part, q, j],
            pooled_in.at[part, q * m + slot],
            pooled_send.at[part],
            pooled_recv.at[part],
            **at(plane * m + j),
        )

    def grad_copy(part, peer, slot):
        return pltpu.make_async_remote_copy(
            grad_out.at[part, peer],
            grad_in.at[part, slot],
            grad_send.at[part],
            grad_recv.at[part, slot],
            **at(peer),
        )

    def pool(part, q):
        rows_of = slabs[q, part].reshape(columns, slab_size)

        def pooled(j):
            if keeps and part > 0:
                counted = kept[q, j]
            else:
                counted = hits(near[j, :, q])
                if keeps:
                    kept[q, j] = counted
            summed = jnp.dot(rows_of, counted, preferred_element_type=jnp.float32)
            return summed.astype(jnp.bfloat16)

        def send(j):
            pooled_out[part, q, j] = pooled(j)
            pooled_copy(part, q, j, local).start()

        each(1, send)
        pooled_in[part, q * m + local] = pooled(local)

    def relay(part, step):
        q = nearest(step)
        slab_copy(part, q, 0, up).wait_recv()
        passed_slab(part, q, lambda copy: copy.start())
        half_copy(part, q, rep).start()

    def pool_from(part, step):
        q = nearest(step)
        half_copy(part, q, 1 - rep).wait_recv()
        pool(part, q)

    def batch(ref, send_sem, recv_sem):
        return pltpu.make_async_remote_copy(ref, ref, send_sem, recv_sem, **partner)

    def arrive(part):
        arrived = pooled_in.at[part, pl.ds(0, planes * (m - 1))]
        batch(arrived, pooled_send.at[part], pooled_recv.at[part]).wait_recv()

    def interact(part):
        def mixed(feature):
            def add(other, carry):
                weight = w_ref[pl.ds(feature * n + other, 1), :]
                return carry + weight * pooled_in[part, other].astype(jnp.float32)

            start = jnp.zeros((columns, samples), jnp.float32)
            return lax.fori_loop(0, n, add, start, unroll=4).astype(jnp.bfloat16)

        def send(peer):
            grad_out[part, peer] = mixed(peer)
            grad_copy(part, peer, me).start()

        for step in range(planes - 1, 0, -1):
            q = nearest(step)
            each(0, lambda j: send(q * m + j))
        each(1, lambda j: send(plane * m + j))
        grad_in[part, me] = mixed(me)

    def keep_far(first, last):
        def take(q, j):
            peer = q * m + j
            kept_own[peer] = hits(far[peer])

        if keeps:
            outside(take, first, last)

    def collect(part):
        def add(peer, counted):
            total[part] += lax.dot_general(
                counted,
                grad_in[part, peer],
                (((1,), (1,)), ((), ())),
                preferred_element_type=jnp.float32,
            )

        def near_hits(j):
            return kept[plane, j] if keeps else hits(near[j, :, plane])

        def take_near(j):
            grad_copy(part, plane * m + j, plane * m + j).wait_recv()
            add(plane * m + j, near_hits(j))

        def take_far(q, j):
            peer = q * m + j
            grad_copy(part, peer, peer).wait_recv()
            add(peer, kept_own[peer] if keeps else hits(far[peer]))

        add(me, near_hits(local))
        each(1, take_near)
        for step in range(1, planes):
            q = nearest(step)
            each(0, lambda j: take_far(q, j))

    batch(near.at[pl.ds(0, m - 1)], near_send, near_recv).wait_recv()
    pool(0, plane)
    relay(0, 1)

    @pl.when(inner)
    def _():
        relay(0, 2)
        own_slab(1, lambda copy: copy.start())
        pool(1, plane)
        pool_from(0, 1)
        pool_from(0, 2)
        relay(0, 3)
        relay(1, 1)
        relay(1, 2)
        pool_from(0, 3)
        pool_from(1, 1)
        pool_from(1, 2)
        relay(1, 3)
        pool_from(1, 3)

    @pl.when(outer)
    def _():
        pool(1, plane)
        pool_from(0, 1)
        relay(1, 1)
        relay(0, 2)
        pool_from(1, 1)
        pool_from(0, 2)
        relay(1, 2)
        relay(0, 3)
        pool_from(1, 2)
        pool_from(0, 3)
        relay(1, 3)
        pool_from(1, 3)

    arrive(0)
    interact(0)
    arrive(1)
    interact(1)
    batch(far.at[pl.ds(0, n - m)], far_send, far_recv).wait_recv()
    keep_far(0, n - m)
    state_copy.wait()
    pieces = []
    for block in range(touch_count):
        at_block = touched_ref[0, block]
        pair = state_ref[pl.ds(at_block // 2, 1), :]
        pieces.append(jnp.where(lax.rem(at_block, 2) == 0, pair[:, :BLOCK], pair[:, BLOCK:]))
    state_row = jnp.concatenate(pieces, axis=1)
    state_col[...] = jnp.broadcast_to(state_row, (state_col.shape[1], slab_size)).T
    def total_copy(part):
        return pltpu.make_async_remote_copy(
            total.at[part], total_in.at[part], pair_sem.at[0, part], pair_sem.at[1, part], **partner
        )

    collect(0)
    total_copy(0).start()
    batch(near.at[pl.ds(0, m - 1)], near_send, near_recv).wait_send()
    batch(far.at[pl.ds(0, n - m)], far_send, far_recv).wait_send()
    batch(slabs.at[pl.ds(0, planes - 1), :, 0], half_send, half_recv.at[0, 0]).wait_send()
    for part in range(parts):
        own_slab(part, lambda copy: copy.wait_send())
        for step in range(1, planes):
            passed_slab(part, nearest(step), lambda copy: copy.wait_send())
        sent = pooled_out.at[part, :, pl.ds(0, m - 1)]
        batch(sent, pooled_send.at[part], pooled_recv.at[part]).wait_send()

    def grads_sent(part):
        sent = grad_out.at[part, pl.ds(0, n - 1)]
        batch(sent, grad_send.at[part], grad_recv.at[part, 0]).wait_send()

    grads_sent(0)
    dither_copy.wait()
    collect(1)
    total_copy(1).start()
    grads_sent(1)
    for part in range(parts):
        total_copy(part).wait_recv()

    def update(block, carry):
        at_rows = pl.ds(pl.multiple_of(block * BLOCK, BLOCK), BLOCK)
        grad = [total[part, at_rows, :] + total_in[part, at_rows, :] for part in range(parts)]
        grad = jnp.concatenate(grad, axis=1)
        state_next = state_col[at_rows, :] + jnp.sum(grad * grad, axis=1, keepdims=True) / width
        state_col[at_rows, :] = state_next
        divisor = jnp.sqrt(state_next) + 1e-08
        divisor = jnp.concatenate([divisor] * (width // divisor.shape[1]), axis=1)
        moved = slab[at_rows, :].astype(jnp.float32) - LEARN_RATE * grad / divisor
        out_ref[at_rows, :] = dither_round(moved, dither_in[at_rows, :])
        return carry

    lax.fori_loop(0, touch_count, update, 0, unroll=2)
    state_all = state_ref[...]
    block_at = 2 * lax.broadcasted_iota(jnp.int32, state_all.shape, 0)
    block_at = block_at + lax.broadcasted_iota(jnp.int32, state_all.shape, 1) // BLOCK
    state_row = state_col[...].T[:1, :]
    for block in range(touch_count):
        piece = state_row[:, block * BLOCK : (block + 1) * BLOCK]
        piece = jnp.broadcast_to(jnp.concatenate([piece, piece], axis=1), state_all.shape)
        state_all = jnp.where(block_at == touched_ref[0, block], piece, state_all)
    state_out_ref[...] = state_all
    for part in range(parts):
        total_copy(part).wait_send()


def fused_step(n, blocks, offsets, cot, touched, state, table, dither):
    micros, planes, m = blocks.shape[0], blocks.shape[1], blocks.shape[2]
    sample_count = blocks.shape[-1]
    samples = micros * sample_count
    cot_size = math.gcd(n, 16)
    slab_size, width = dither.shape
    columns = width // PARTS
    keeps = 2 * n * slab_size * samples <= KEEP_BYTES
    dma = pltpu.SemaphoreType.DMA
    block = (PARTS, n, columns, samples)
    vmem = pl.BlockSpec(memory_space=pltpu.VMEM)
    smem = pl.BlockSpec(memory_space=pltpu.SMEM)
    hbm = pl.BlockSpec(memory_space=pltpu.HBM)
    return pl.pallas_call(
        functools.partial(step_kernel, n),
        out_shape=(
            pltpu.VMEM((slab_size, width), jnp.bfloat16),
            pltpu.VMEM(state.shape, jnp.float32),
            pltpu.VMEM(table.shape, jnp.bfloat16),
        ),
        in_specs=[hbm, hbm, hbm, smem, hbm, hbm, hbm],
        out_specs=(vmem, vmem, vmem),
        scratch_shapes=[
            pltpu.VMEM(blocks.shape, jnp.int32),
            pltpu.VMEM(blocks.shape, jnp.int32),
            pltpu.VMEM(state.shape, jnp.float32),
            pltpu.VMEM(blocks.shape, jnp.int32),
            pltpu.VMEM((micros, cot_size, n, sample_count), jnp.bfloat16),
            pltpu.VMEM((m, micros, planes) + blocks.shape[3:], jnp.int32),
            pltpu.VMEM((n, micros) + blocks.shape[3:], jnp.int32),
            pltpu.VMEM((n * n, samples), jnp.float32),
            pltpu.VMEM((slab_size, width), jnp.int32),
            pltpu.VMEM((slab_size, width), jnp.bfloat16),
            pltpu.VMEM((planes, PARTS, 2, columns // 2, slab_size), jnp.bfloat16),
            pltpu.VMEM((PARTS, planes, m, columns, samples), jnp.bfloat16),
            pltpu.VMEM(block, jnp.bfloat16),
            pltpu.VMEM(block, jnp.bfloat16),
            pltpu.VMEM(block, jnp.bfloat16),
            pltpu.VMEM((planes if keeps else 1, m if keeps else 1, slab_size, samples), jnp.bfloat16),
            pltpu.VMEM((n if keeps else 1, slab_size, samples), jnp.bfloat16),
            pltpu.VMEM((PARTS, slab_size, columns), jnp.float32),
            pltpu.VMEM((PARTS, slab_size, columns), jnp.float32),
            pltpu.VMEM((slab_size, 128), jnp.float32),
            dma((6,)),
            dma((2, PARTS)),
            dma(()),
            dma(()),
            dma(()),
            dma(()),
            dma((2, PARTS, planes)),
            dma((PARTS, planes)),
            dma(()),
            dma((PARTS, planes)),
            dma((PARTS,)),
            dma((PARTS,)),
            dma((PARTS,)),
            dma((PARTS, n)),
        ],
        compiler_params=pltpu.CompilerParams(collective_id=0, has_side_effects=True),
        name="fused_step",
    )(blocks, offsets, cot, touched, state, table, dither)


def write_kernel(touched_ref, new_ref, state_ref, table_ref, out_ref, state_out_ref, place, sem):
    state_copy = pltpu.make_async_copy(state_ref, state_out_ref, sem.at[1])
    state_copy.start()
    blocks, touch_count = table_ref.shape[0], touched_ref.shape[1]

    def clear(block, carry):
        place[block] = -1
        return carry

    lax.fori_loop(0, blocks, clear, 0, unroll=8)
    for i in range(touch_count):
        place[touched_ref[0, i]] = i

    def write(block, carry):
        new = place[block]

        @pl.when(new >= 0)
        def _():
            pltpu.make_async_copy(new_ref.at[new], out_ref.at[block], sem.at[0]).start()

        @pl.when(new < 0)
        def _():
            pltpu.make_async_copy(table_ref.at[block], out_ref.at[block], sem.at[0]).start()

        return carry

    lax.fori_loop(0, blocks, write, 0)
    pltpu.make_async_copy(table_ref, out_ref, sem.at[0]).wait()
    state_copy.wait()


def write_table(touched, new_rows, state, table):
    vmem = pl.BlockSpec(memory_space=pltpu.VMEM)
    hbm = pl.BlockSpec(memory_space=pltpu.HBM)
    held = [pltpu.with_memory_space_constraint(x, pltpu.VMEM) for x in (new_rows, state, table)]
    return pl.pallas_call(
        write_kernel,
        out_shape=(
            jax.ShapeDtypeStruct(table.shape, table.dtype),
            jax.ShapeDtypeStruct(state.shape, state.dtype),
        ),
        in_specs=[pl.BlockSpec(memory_space=pltpu.SMEM), vmem, vmem, vmem],
        out_specs=(hbm, hbm),
        scratch_shapes=[pltpu.SMEM((table.shape[0],), jnp.int32), pltpu.SemaphoreType.DMA((2,))],
        compiler_params=pltpu.CompilerParams(vmem_limit_bytes=4 << 20),
        name="write_table",
    )(touched, *held)


def per_device(
    lookup_block, lookup_offset, interaction_grad, table, adagrad_state, touched_blocks, dither
):
    micro_count, sample_count, feature_count, bag_count = lookup_block.shape
    n = lax.axis_size("mp")
    row_count, emb_width = table.shape
    touch_count = touched_blocks.shape[1]
    split = (micro_count, PLANES, feature_count // PLANES, bag_count, sample_count)
    blocks = lookup_block.transpose(0, 2, 3, 1).reshape(split)
    offsets = lookup_offset.transpose(0, 2, 3, 1).reshape(split)
    cot = interaction_grad.transpose(0, 2, 3, 1)
    table_blocks = table.reshape(row_count // BLOCK, BLOCK, emb_width)
    state = adagrad_state.reshape(row_count // (2 * BLOCK), 2 * BLOCK)
    new_rows, new_state, table_copy = fused_step(
        n, blocks, offsets, cot, touched_blocks, state, table_blocks, dither[0]
    )
    new_rows = new_rows.reshape(touch_count, BLOCK, emb_width)
    new_table, new_state = write_table(touched_blocks, new_rows, new_state, table_copy)
    return (new_table.reshape(row_count, emb_width), new_state.reshape(row_count))


def solution(mesh):
    return jax.shard_map(
        per_device,
        mesh=mesh,
        in_specs=(
            P(None, ("rep", "mp"), None, None),
            P(None, ("rep", "mp"), None, None),
            P(None, ("rep", "mp"), None, None),
            P("mp", None),
            P("mp"),
            P("mp", None),
            P("mp", None, None),
        ),
        out_specs=(P("mp", None), P("mp")),
        check_vma=False,
    )
```

```python
import functools
import math

import jax
import jax.numpy as jnp
from jax import lax
from jax.experimental import pallas as pl
from jax.experimental.pallas import tpu as pltpu
from jax.sharding import PartitionSpec as P

BLOCK = 64
PLANES = 4
PARTS = 2
LEARN_RATE = 0.1
POOL_DECAY = 0.5
DITHER_UNIT = 2.0 ** (-15)
SMALLEST = 2.0 ** (-14)
KEEP_BYTES = 8 << 20
MESH = pl.DeviceIdType.MESH


def dither_round(weights, dither_bits):
    magnitude = jnp.maximum(jnp.abs(weights), SMALLEST)
    spacing = jnp.exp2(jnp.floor(jnp.log2(magnitude)) - 7.0)
    grid_level = jnp.floor(weights / spacing + dither_bits.astype(jnp.float32) * DITHER_UNIT)
    return (grid_level * spacing).astype(jnp.bfloat16)


def plane_order(planes, plane, step):
    picked = jnp.int32(0)
    for own in range(planes):
        near_first = sorted(range(planes), key=lambda q: (abs(q - own), (q - own) * (2 * own - planes)))
        picked = jnp.where(plane == own, near_first[step], picked)
    return picked


def step_kernel(
    n,
    block_hbm,
    offset_hbm,
    cot_ref,
    touched_ref,
    state_hbm,
    table_ref,
    dither_ref,
    out_ref,
    state_out_ref,
    table_in,
    block_ref,
    offset_ref,
    state_ref,
    rows_ref,
    cot_in,
    near,
    far,
    w_ref,
    dither_in,
    slab,
    slabs,
    pooled_out,
    pooled_in,
    grad_out,
    grad_in,
    kept,
    kept_own,
    total,
    total_in,
    state_col,
    local_sem,
    pair_sem,
    near_send,
    near_recv,
    far_send,
    far_recv,
    slab_send,
    slab_recv,
    half_send,
    half_recv,
    pooled_send,
    pooled_recv,
    grad_send,
    grad_recv,
):
    me = lax.axis_index("mp")
    rep = lax.axis_index("rep")
    planes, parts = slabs.shape[0], slabs.shape[1]
    m = n // planes
    plane = me // m
    local = lax.rem(me, m)
    samples = w_ref.shape[1]
    bags = rows_ref.shape[3]
    slab_size, width = slab.shape
    columns = width // parts
    touch_count = slab_size // BLOCK
    keeps = kept.shape[0] == planes

    def at(peer):
        return {"device_id": (rep, peer), "device_id_type": MESH}

    partner = {"device_id": (1 - rep, me), "device_id_type": MESH}

    def each(first, body):
        def run(step, carry):
            body(lax.rem(local + step, m))
            return carry

        lax.fori_loop(first, m, run, 0)

    def others(body):
        def run(step, carry):
            body(lax.rem(me + step, n))
            return carry

        lax.fori_loop(1, n, run, 0)

    def outside(body, first=0, last=n - m):
        def run(step, carry):
            body(lax.rem(plane + 1 + step // m, planes), lax.rem(local + step, m))
            return carry

        lax.fori_loop(first, last, run, 0)

    def nearest(step):
        return plane_order(planes, plane, step)

    barrier = pltpu.get_barrier_semaphore()
    others(lambda peer: pl.semaphore_signal(barrier, inc=1, **at(peer)))
    pl.semaphore_signal(barrier, inc=1, **partner)
    table_copy = pltpu.make_async_copy(table_ref, table_in, local_sem.at[0])
    table_copy.start()
    block_copy = pltpu.make_async_copy(block_hbm, block_ref, local_sem.at[1])
    block_copy.start()
    offset_copy = pltpu.make_async_copy(offset_hbm, offset_ref, local_sem.at[2])
    offset_copy.start()
    state_copy = pltpu.make_async_copy(state_hbm, state_ref, local_sem.at[3])
    state_copy.start()
    dither_copy = pltpu.make_async_copy(dither_ref, dither_in, local_sem.at[4])
    dither_copy.start()
    block_copy.wait()
    offset_copy.wait()
    rows_ref[...] = block_ref[...] * BLOCK + offset_ref[...]
    near[local] = rows_ref[:, :, local]
    table_copy.wait()
    for block in range(touch_count):
        slab[block * BLOCK : (block + 1) * BLOCK, :] = table_in[touched_ref[0, block]]
    for part in range(parts):
        turned = slab[:, part * columns : (part + 1) * columns].astype(jnp.float32).T
        slabs[plane, part] = turned.astype(jnp.bfloat16).reshape(slabs.shape[2:])
    pl.semaphore_wait(barrier, n)

    def near_copy(j, slot):
        return pltpu.make_async_remote_copy(
            rows_ref.at[:, :, j],
            near.at[slot],
            near_send,
            near_recv,
            **at(plane * m + j),
        )

    def far_copy(q, j, slot):
        return pltpu.make_async_remote_copy(
            rows_ref.at[:, q, j],
            far.at[slot],
            far_send,
            far_recv,
            **at(q * m + j),
        )

    def slab_copy(part, q, way, peer):
        return pltpu.make_async_remote_copy(
            slabs.at[q, part, rep],
            slabs.at[q, part, rep],
            slab_send.at[way, part, q],
            slab_recv.at[part, q],
            **at(peer),
        )

    def half_copy(part, q, which):
        return pltpu.make_async_remote_copy(
            slabs.at[q, part, which],
            slabs.at[q, part, which],
            half_send,
            half_recv.at[part, q],
            **partner,
        )

    has_up, has_down = plane + 1 < planes, plane > 0
    inner = jnp.logical_and(has_up, has_down)
    outer = jnp.logical_not(inner)
    up, down = lax.rem(me + m, n), lax.rem(me + n - m, n)

    def own_slab(part, act):
        @pl.when(has_up)
        def _():
            act(slab_copy(part, plane, 0, up))

        @pl.when(has_down)
        def _():
            act(slab_copy(part, plane, 1, down))

    def passed_slab(part, q, act):
        @pl.when(jnp.logical_and(q < plane, has_up))
        def _():
            act(slab_copy(part, q, 0, up))

        @pl.when(jnp.logical_and(q > plane, has_down))
        def _():
            act(slab_copy(part, q, 1, down))

    each(1, lambda j: near_copy(j, local).start())
    own_slab(0, lambda copy: copy.start())
    outside(lambda q, j: far_copy(q, j, me).start())
    cot_size = cot_in.shape[1]

    def spread(chunk, carry):
        cot_copy = pltpu.make_async_copy(
            cot_ref.at[:, pl.ds(chunk * cot_size, cot_size)], cot_in, local_sem.at[5]
        )
        cot_copy.start()
        cot_copy.wait()
        for i in range(cot_size):
            pieces = [cot_in[micro, i].astype(jnp.float32) for micro in range(cot_in.shape[0])]
            at_row = pl.multiple_of((chunk * cot_size + i) * n, n)
            w_ref[pl.ds(at_row, n), :] = jnp.concatenate(pieces, axis=-1)
        return carry

    lax.fori_loop(0, n // cot_size, spread, 0)
    place = lax.broadcasted_iota(jnp.int32, (n, samples), 0)

    def fold(f, carry):
        along = pl.ds(pl.multiple_of(f * n, n), n)
        across = pl.ds(f, n, stride=n)
        row, column = w_ref[along, :], w_ref[across, :]
        both = row + column + jnp.where(place == f, POOL_DECAY, 0.0)
        w_ref[along, :] = jnp.where(place >= f, both, row)
        w_ref[across, :] = jnp.where(place >= f, both, column)
        return carry

    lax.fori_loop(0, n, fold, 0)
    own_slab(1, lambda copy: copy.start())
    total[...] = jnp.zeros_like(total)

    offset_in_block = lax.broadcasted_iota(jnp.int32, (BLOCK, samples), 0)
    offset_in_block = offset_in_block.astype(jnp.float32).astype(jnp.bfloat16)
    one = jnp.ones((BLOCK, samples), jnp.bfloat16)

    def hits(micros):
        rows = jnp.concatenate([micros[i] for i in range(micros.shape[0])], axis=-1)
        blocks = []
        block_of, offset_of = rows // BLOCK, lax.rem(rows, BLOCK)
        for block in range(slab_size // BLOCK):
            wanted = jnp.where(block_of == block, offset_of, -1).astype(jnp.float32)
            counted = jnp.zeros((BLOCK, samples), jnp.bfloat16)
            for lookup in range(bags):
                row = jnp.broadcast_to(wanted[lookup : lookup + 1, :], (BLOCK, samples))
                same = row.astype(jnp.bfloat16) == offset_in_block
                counted = counted + jnp.where(same, one, jnp.zeros_like(one))
            blocks.append(counted)
        return jnp.concatenate(blocks, axis=0)

    def pooled_copy(part, q, j, slot):
        return pltpu.make_async_remote_copy(
            pooled_out.at[part, q, j],
            pooled_in.at[part, q * m + slot],
            pooled_send.at[part],
            pooled_recv.at[part],
            **at(plane * m + j),
        )

    def grad_copy(part, peer, slot):
        return pltpu.make_async_remote_copy(
            grad_out.at[part, peer],
            grad_in.at[part, slot],
            grad_send.at[part],
            grad_recv.at[part, slot],
            **at(peer),
        )

    def pool(part, q):
        rows_of = slabs[q, part].reshape(columns, slab_size)

        def pooled(j):
            if keeps and part > 0:
                counted = kept[q, j]
            else:
                counted = hits(near[j, :, q])
                if keeps:
                    kept[q, j] = counted
            summed = jnp.dot(rows_of, counted, preferred_element_type=jnp.float32)
            return summed.astype(jnp.bfloat16)

        def send(j):
            pooled_out[part, q, j] = pooled(j)
            pooled_copy(part, q, j, local).start()

        each(1, send)
        pooled_in[part, q * m + local] = pooled(local)

    def relay(part, step):
        q = nearest(step)
        slab_copy(part, q, 0, up).wait_recv()
        passed_slab(part, q, lambda copy: copy.start())
        half_copy(part, q, rep).start()

    def pool_from(part, step):
        q = nearest(step)
        half_copy(part, q, 1 - rep).wait_recv()
        pool(part, q)

    def batch(ref, send_sem, recv_sem):
        return pltpu.make_async_remote_copy(ref, ref, send_sem, recv_sem, **partner)

    def arrive(part):
        arrived = pooled_in.at[part, pl.ds(0, planes * (m - 1))]
        batch(arrived, pooled_send.at[part], pooled_recv.at[part]).wait_recv()

    def interact(part):
        def mixed(feature):
            def add(other, carry):
                weight = w_ref[pl.ds(feature * n + other, 1), :]
                return carry + weight * pooled_in[part, other].astype(jnp.float32)

            start = jnp.zeros((columns, samples), jnp.float32)
            return lax.fori_loop(0, n, add, start, unroll=4).astype(jnp.bfloat16)

        def send(peer):
            grad_out[part, peer] = mixed(peer)
            grad_copy(part, peer, me).start()

        for step in range(planes - 1, 0, -1):
            q = nearest(step)
            each(0, lambda j: send(q * m + j))
        each(1, lambda j: send(plane * m + j))
        grad_in[part, me] = mixed(me)

    def keep_far(first, last):
        def take(q, j):
            peer = q * m + j
            kept_own[peer] = hits(far[peer])

        if keeps:
            outside(take, first, last)

    def collect(part):
        def add(peer, counted):
            total[part] += lax.dot_general(
                counted,
                grad_in[part, peer],
                (((1,), (1,)), ((), ())),
                preferred_element_type=jnp.float32,
            )

        def near_hits(j):
            return kept[plane, j] if keeps else hits(near[j, :, plane])

        def take_near(j):
            grad_copy(part, plane * m + j, plane * m + j).wait_recv()
            add(plane * m + j, near_hits(j))

        def take_far(q, j):
            peer = q * m + j
            grad_copy(part, peer, peer).wait_recv()
            add(peer, kept_own[peer] if keeps else hits(far[peer]))

        add(me, near_hits(local))
        each(1, take_near)
        for step in range(1, planes):
            q = nearest(step)
            each(0, lambda j: take_far(q, j))

    batch(near.at[pl.ds(0, m - 1)], near_send, near_recv).wait_recv()
    pool(0, plane)
    relay(0, 1)

    @pl.when(inner)
    def _():
        relay(0, 2)
        pool(1, plane)
        relay(1, 1)
        relay(1, 2)
        pool_from(0, 1)
        relay(0, 3)
        pool_from(0, 2)
        pool_from(0, 3)
        relay(1, 3)
        pool_from(1, 1)
        pool_from(1, 2)

    @pl.when(outer)
    def _():
        pool(1, plane)
        relay(1, 1)
        pool_from(0, 1)
        relay(0, 2)
        pool_from(1, 1)
        pool_from(0, 2)
        relay(1, 2)
        relay(0, 3)
        pool_from(1, 2)
        pool_from(0, 3)
        relay(1, 3)

    pool_from(1, 3)
    arrive(0)
    interact(0)
    arrive(1)
    interact(1)
    batch(far.at[pl.ds(0, n - m)], far_send, far_recv).wait_recv()
    keep_far(0, n - m)
    state_copy.wait()
    pieces = []
    for block in range(touch_count):
        at_block = touched_ref[0, block]
        pair = state_ref[pl.ds(at_block // 2, 1), :]
        pieces.append(jnp.where(lax.rem(at_block, 2) == 0, pair[:, :BLOCK], pair[:, BLOCK:]))
    state_row = jnp.concatenate(pieces, axis=1)
    state_col[...] = jnp.broadcast_to(state_row, (state_col.shape[1], slab_size)).T
    def total_copy(part):
        return pltpu.make_async_remote_copy(
            total.at[part], total_in.at[part], pair_sem.at[0, part], pair_sem.at[1, part], **partner
        )

    collect(0)
    total_copy(0).start()
    batch(near.at[pl.ds(0, m - 1)], near_send, near_recv).wait_send()
    batch(far.at[pl.ds(0, n - m)], far_send, far_recv).wait_send()
    batch(slabs.at[pl.ds(0, planes - 1), :, 0], half_send, half_recv.at[0, 0]).wait_send()
    for part in range(parts):
        own_slab(part, lambda copy: copy.wait_send())
        for step in range(1, planes):
            passed_slab(part, nearest(step), lambda copy: copy.wait_send())
        sent = pooled_out.at[part, :, pl.ds(0, m - 1)]
        batch(sent, pooled_send.at[part], pooled_recv.at[part]).wait_send()

    def grads_sent(part):
        sent = grad_out.at[part, pl.ds(0, n - 1)]
        batch(sent, grad_send.at[part], grad_recv.at[part, 0]).wait_send()

    grads_sent(0)
    dither_copy.wait()
    collect(1)
    total_copy(1).start()
    grads_sent(1)
    for part in range(parts):
        total_copy(part).wait_recv()

    def update(block, carry):
        at_rows = pl.ds(pl.multiple_of(block * BLOCK, BLOCK), BLOCK)
        grad = [total[part, at_rows, :] + total_in[part, at_rows, :] for part in range(parts)]
        grad = jnp.concatenate(grad, axis=1)
        state_next = state_col[at_rows, :] + jnp.sum(grad * grad, axis=1, keepdims=True) / width
        state_col[at_rows, :] = state_next
        divisor = jnp.sqrt(state_next) + 1e-08
        divisor = jnp.concatenate([divisor] * (width // divisor.shape[1]), axis=1)
        moved = slab[at_rows, :].astype(jnp.float32) - LEARN_RATE * grad / divisor
        out_ref[at_rows, :] = dither_round(moved, dither_in[at_rows, :])
        return carry

    lax.fori_loop(0, touch_count, update, 0, unroll=2)
    state_all = state_ref[...]
    block_at = 2 * lax.broadcasted_iota(jnp.int32, state_all.shape, 0)
    block_at = block_at + lax.broadcasted_iota(jnp.int32, state_all.shape, 1) // BLOCK
    state_row = state_col[...].T[:1, :]
    for block in range(touch_count):
        piece = state_row[:, block * BLOCK : (block + 1) * BLOCK]
        piece = jnp.broadcast_to(jnp.concatenate([piece, piece], axis=1), state_all.shape)
        state_all = jnp.where(block_at == touched_ref[0, block], piece, state_all)
    state_out_ref[...] = state_all
    for part in range(parts):
        total_copy(part).wait_send()


def fused_step(n, blocks, offsets, cot, touched, state, table, dither):
    micros, planes, m = blocks.shape[0], blocks.shape[1], blocks.shape[2]
    sample_count = blocks.shape[-1]
    samples = micros * sample_count
    cot_size = math.gcd(n, 16)
    slab_size, width = dither.shape
    columns = width // PARTS
    keeps = 2 * n * slab_size * samples <= KEEP_BYTES
    dma = pltpu.SemaphoreType.DMA
    block = (PARTS, n, columns, samples)
    vmem = pl.BlockSpec(memory_space=pltpu.VMEM)
    smem = pl.BlockSpec(memory_space=pltpu.SMEM)
    hbm = pl.BlockSpec(memory_space=pltpu.HBM)
    return pl.pallas_call(
        functools.partial(step_kernel, n),
        out_shape=(
            pltpu.VMEM((slab_size, width), jnp.bfloat16),
            pltpu.VMEM(state.shape, jnp.float32),
            pltpu.VMEM(table.shape, jnp.bfloat16),
        ),
        in_specs=[hbm, hbm, hbm, smem, hbm, hbm, hbm],
        out_specs=(vmem, vmem, vmem),
        scratch_shapes=[
            pltpu.VMEM(blocks.shape, jnp.int32),
            pltpu.VMEM(blocks.shape, jnp.int32),
            pltpu.VMEM(state.shape, jnp.float32),
            pltpu.VMEM(blocks.shape, jnp.int32),
            pltpu.VMEM((micros, cot_size, n, sample_count), jnp.bfloat16),
            pltpu.VMEM((m, micros, planes) + blocks.shape[3:], jnp.int32),
            pltpu.VMEM((n, micros) + blocks.shape[3:], jnp.int32),
            pltpu.VMEM((n * n, samples), jnp.float32),
            pltpu.VMEM((slab_size, width), jnp.int32),
            pltpu.VMEM((slab_size, width), jnp.bfloat16),
            pltpu.VMEM((planes, PARTS, 2, columns // 2, slab_size), jnp.bfloat16),
            pltpu.VMEM((PARTS, planes, m, columns, samples), jnp.bfloat16),
            pltpu.VMEM(block, jnp.bfloat16),
            pltpu.VMEM(block, jnp.bfloat16),
            pltpu.VMEM(block, jnp.bfloat16),
            pltpu.VMEM((planes if keeps else 1, m if keeps else 1, slab_size, samples), jnp.bfloat16),
            pltpu.VMEM((n if keeps else 1, slab_size, samples), jnp.bfloat16),
            pltpu.VMEM((PARTS, slab_size, columns), jnp.float32),
            pltpu.VMEM((PARTS, slab_size, columns), jnp.float32),
            pltpu.VMEM((slab_size, 128), jnp.float32),
            dma((6,)),
            dma((2, PARTS)),
            dma(()),
            dma(()),
            dma(()),
            dma(()),
            dma((2, PARTS, planes)),
            dma((PARTS, planes)),
            dma(()),
            dma((PARTS, planes)),
            dma((PARTS,)),
            dma((PARTS,)),
            dma((PARTS,)),
            dma((PARTS, n)),
        ],
        compiler_params=pltpu.CompilerParams(collective_id=0, has_side_effects=True),
        name="fused_step",
    )(blocks, offsets, cot, touched, state, table, dither)


def write_kernel(touched_ref, new_ref, state_ref, table_ref, out_ref, state_out_ref, place, sem):
    state_copy = pltpu.make_async_copy(state_ref, state_out_ref, sem.at[1])
    state_copy.start()
    blocks, touch_count = table_ref.shape[0], touched_ref.shape[1]

    def clear(block, carry):
        place[block] = -1
        return carry

    lax.fori_loop(0, blocks, clear, 0, unroll=8)
    for i in range(touch_count):
        place[touched_ref[0, i]] = i

    def write(block, carry):
        new = place[block]

        @pl.when(new >= 0)
        def _():
            pltpu.make_async_copy(new_ref.at[new], out_ref.at[block], sem.at[0]).start()

        @pl.when(new < 0)
        def _():
            pltpu.make_async_copy(table_ref.at[block], out_ref.at[block], sem.at[0]).start()

        return carry

    lax.fori_loop(0, blocks, write, 0)
    pltpu.make_async_copy(table_ref, out_ref, sem.at[0]).wait()
    state_copy.wait()


def write_table(touched, new_rows, state, table):
    vmem = pl.BlockSpec(memory_space=pltpu.VMEM)
    hbm = pl.BlockSpec(memory_space=pltpu.HBM)
    held = [pltpu.with_memory_space_constraint(x, pltpu.VMEM) for x in (new_rows, state, table)]
    return pl.pallas_call(
        write_kernel,
        out_shape=(
            jax.ShapeDtypeStruct(table.shape, table.dtype),
            jax.ShapeDtypeStruct(state.shape, state.dtype),
        ),
        in_specs=[pl.BlockSpec(memory_space=pltpu.SMEM), vmem, vmem, vmem],
        out_specs=(hbm, hbm),
        scratch_shapes=[pltpu.SMEM((table.shape[0],), jnp.int32), pltpu.SemaphoreType.DMA((2,))],
        compiler_params=pltpu.CompilerParams(vmem_limit_bytes=4 << 20),
        name="write_table",
    )(touched, *held)


def per_device(
    lookup_block, lookup_offset, interaction_grad, table, adagrad_state, touched_blocks, dither
):
    micro_count, sample_count, feature_count, bag_count = lookup_block.shape
    n = lax.axis_size("mp")
    row_count, emb_width = table.shape
    touch_count = touched_blocks.shape[1]
    split = (micro_count, PLANES, feature_count // PLANES, bag_count, sample_count)
    blocks = lookup_block.transpose(0, 2, 3, 1).reshape(split)
    offsets = lookup_offset.transpose(0, 2, 3, 1).reshape(split)
    cot = interaction_grad.transpose(0, 2, 3, 1)
    table_blocks = table.reshape(row_count // BLOCK, BLOCK, emb_width)
    state = adagrad_state.reshape(row_count // (2 * BLOCK), 2 * BLOCK)
    new_rows, new_state, table_copy = fused_step(
        n, blocks, offsets, cot, touched_blocks, state, table_blocks, dither[0]
    )
    new_rows = new_rows.reshape(touch_count, BLOCK, emb_width)
    new_table, new_state = write_table(touched_blocks, new_rows, new_state, table_copy)
    return (new_table.reshape(row_count, emb_width), new_state.reshape(row_count))


def solution(mesh):
    return jax.shard_map(
        per_device,
        mesh=mesh,
        in_specs=(
            P(None, ("rep", "mp"), None, None),
            P(None, ("rep", "mp"), None, None),
            P(None, ("rep", "mp"), None, None),
            P("mp", None),
            P("mp"),
            P("mp", None),
            P("mp", None, None),
        ),
        out_specs=(P("mp", None), P("mp")),
        check_vma=False,
    )
```

```python
import functools
import math

import jax
import jax.numpy as jnp
from jax import lax
from jax.experimental import pallas as pl
from jax.experimental.pallas import tpu as pltpu
from jax.sharding import PartitionSpec as P

BLOCK = 64
PLANES = 4
PARTS = 2
LEARN_RATE = 0.1
POOL_DECAY = 0.5
DITHER_UNIT = 2.0 ** (-15)
SMALLEST = 2.0 ** (-14)
KEEP_BYTES = 8 << 20
MESH = pl.DeviceIdType.MESH


def dither_round(weights, dither_bits):
    magnitude = jnp.maximum(jnp.abs(weights), SMALLEST)
    spacing = jnp.exp2(jnp.floor(jnp.log2(magnitude)) - 7.0)
    grid_level = jnp.floor(weights / spacing + dither_bits.astype(jnp.float32) * DITHER_UNIT)
    return (grid_level * spacing).astype(jnp.bfloat16)


def plane_order(planes, plane, step):
    picked = jnp.int32(0)
    for own in range(planes):
        near_first = sorted(range(planes), key=lambda q: (abs(q - own), (q - own) * (2 * own - planes)))
        picked = jnp.where(plane == own, near_first[step], picked)
    return picked


def step_kernel(
    n,
    block_hbm,
    offset_hbm,
    cot_ref,
    touched_ref,
    state_hbm,
    table_ref,
    dither_ref,
    out_ref,
    state_out_ref,
    table_in,
    block_ref,
    offset_ref,
    state_ref,
    rows_ref,
    cot_in,
    near,
    far,
    w_ref,
    dither_in,
    slab,
    slabs,
    pooled_out,
    pooled_in,
    grad_out,
    grad_in,
    kept,
    kept_own,
    total,
    total_in,
    state_col,
    local_sem,
    pair_sem,
    near_send,
    near_recv,
    far_send,
    far_recv,
    slab_send,
    slab_recv,
    half_send,
    half_recv,
    pooled_send,
    pooled_recv,
    grad_send,
    grad_recv,
):
    me = lax.axis_index("mp")
    rep = lax.axis_index("rep")
    planes, parts = slabs.shape[0], slabs.shape[1]
    m = n // planes
    plane = me // m
    local = lax.rem(me, m)
    samples = w_ref.shape[1]
    bags = rows_ref.shape[3]
    slab_size, width = slab.shape
    columns = width // parts
    touch_count = slab_size // BLOCK
    keeps = kept.shape[0] == planes

    def at(peer):
        return {"device_id": (rep, peer), "device_id_type": MESH}

    partner = {"device_id": (1 - rep, me), "device_id_type": MESH}

    def each(first, body):
        def run(step, carry):
            body(lax.rem(local + step, m))
            return carry

        lax.fori_loop(first, m, run, 0)

    def others(body):
        def run(step, carry):
            body(lax.rem(me + step, n))
            return carry

        lax.fori_loop(1, n, run, 0)

    def outside(body, first=0, last=n - m):
        def run(step, carry):
            body(lax.rem(plane + 1 + step // m, planes), lax.rem(local + step, m))
            return carry

        lax.fori_loop(first, last, run, 0)

    def nearest(step):
        return plane_order(planes, plane, step)

    barrier = pltpu.get_barrier_semaphore()
    others(lambda peer: pl.semaphore_signal(barrier, inc=1, **at(peer)))
    pl.semaphore_signal(barrier, inc=1, **partner)
    table_copy = pltpu.make_async_copy(table_ref, table_in, local_sem.at[0])
    table_copy.start()
    block_copy = pltpu.make_async_copy(block_hbm, block_ref, local_sem.at[1])
    block_copy.start()
    offset_copy = pltpu.make_async_copy(offset_hbm, offset_ref, local_sem.at[2])
    offset_copy.start()
    state_copy = pltpu.make_async_copy(state_hbm, state_ref, local_sem.at[3])
    state_copy.start()
    dither_copy = pltpu.make_async_copy(dither_ref, dither_in, local_sem.at[4])
    dither_copy.start()
    block_copy.wait()
    offset_copy.wait()
    rows_ref[...] = block_ref[...] * BLOCK + offset_ref[...]
    near[local] = rows_ref[:, :, local]
    table_copy.wait()
    for block in range(touch_count):
        slab[block * BLOCK : (block + 1) * BLOCK, :] = table_in[touched_ref[0, block]]
    for part in range(parts):
        turned = slab[:, part * columns : (part + 1) * columns].astype(jnp.float32).T
        slabs[plane, part] = turned.astype(jnp.bfloat16).reshape(slabs.shape[2:])
    pl.semaphore_wait(barrier, n)

    def near_copy(j, slot):
        return pltpu.make_async_remote_copy(
            rows_ref.at[:, :, j],
            near.at[slot],
            near_send,
            near_recv,
            **at(plane * m + j),
        )

    def far_copy(q, j, slot):
        return pltpu.make_async_remote_copy(
            rows_ref.at[:, q, j],
            far.at[slot],
            far_send,
            far_recv,
            **at(q * m + j),
        )

    def slab_copy(part, q, way, peer):
        return pltpu.make_async_remote_copy(
            slabs.at[q, part, rep],
            slabs.at[q, part, rep],
            slab_send.at[way, part, q],
            slab_recv.at[part, q],
            **at(peer),
        )

    def half_copy(part, q, which):
        return pltpu.make_async_remote_copy(
            slabs.at[q, part, which],
            slabs.at[q, part, which],
            half_send,
            half_recv.at[part, q],
            **partner,
        )

    has_up, has_down = plane + 1 < planes, plane > 0
    inner = jnp.logical_and(has_up, has_down)
    outer = jnp.logical_not(inner)
    up, down = lax.rem(me + m, n), lax.rem(me + n - m, n)

    def own_slab(part, act):
        @pl.when(has_up)
        def _():
            act(slab_copy(part, plane, 0, up))

        @pl.when(has_down)
        def _():
            act(slab_copy(part, plane, 1, down))

    def passed_slab(part, q, act):
        @pl.when(jnp.logical_and(q < plane, has_up))
        def _():
            act(slab_copy(part, q, 0, up))

        @pl.when(jnp.logical_and(q > plane, has_down))
        def _():
            act(slab_copy(part, q, 1, down))

    each(1, lambda j: near_copy(j, local).start())
    own_slab(0, lambda copy: copy.start())
    outside(lambda q, j: far_copy(q, j, me).start())
    cot_size = cot_in.shape[1]

    def spread(chunk, carry):
        cot_copy = pltpu.make_async_copy(
            cot_ref.at[:, pl.ds(chunk * cot_size, cot_size)], cot_in, local_sem.at[5]
        )
        cot_copy.start()
        cot_copy.wait()
        for i in range(cot_size):
            pieces = [cot_in[micro, i].astype(jnp.float32) for micro in range(cot_in.shape[0])]
            at_row = pl.multiple_of((chunk * cot_size + i) * n, n)
            w_ref[pl.ds(at_row, n), :] = jnp.concatenate(pieces, axis=-1)
        return carry

    lax.fori_loop(0, n // cot_size, spread, 0)
    place = lax.broadcasted_iota(jnp.int32, (n, samples), 0)

    def fold(f, carry):
        along = pl.ds(pl.multiple_of(f * n, n), n)
        across = pl.ds(f, n, stride=n)
        row, column = w_ref[along, :], w_ref[across, :]
        both = row + column + jnp.where(place == f, POOL_DECAY, 0.0)
        w_ref[along, :] = jnp.where(place >= f, both, row)
        w_ref[across, :] = jnp.where(place >= f, both, column)
        return carry

    lax.fori_loop(0, n, fold, 0)
    own_slab(1, lambda copy: copy.start())
    total[...] = jnp.zeros_like(total)

    sublanes = 16
    place_of = lax.broadcasted_iota(jnp.int32, (BLOCK, samples), 0)
    place_of = place_of.astype(jnp.float32).astype(jnp.bfloat16)
    one = jnp.ones((sublanes, samples), jnp.bfloat16)
    none = jnp.zeros_like(one)

    def hits(micros):
        rows = jnp.concatenate([micros[i] for i in range(micros.shape[0])], axis=-1)
        block_of = (rows // BLOCK).astype(jnp.float32)
        offset_of = lax.rem(rows, BLOCK).astype(jnp.float32)

        def wide(values, lookup):
            row = jnp.broadcast_to(values[lookup : lookup + 1, :], (sublanes, samples))
            return row.astype(jnp.bfloat16)

        spans = [slice(at, at + sublanes) for at in range(0, BLOCK, sublanes)]
        offsets = [wide(offset_of, lookup) for lookup in range(bags)]
        same = [[jnp.where(offset == place_of[span], one, none) for span in spans] for offset in offsets]
        in_block = [wide(block_of, lookup) for lookup in range(bags)]
        pieces = []
        for block in range(slab_size // BLOCK):
            chosen = [row == jnp.full_like(row, block) for row in in_block]
            for at in range(len(spans)):
                terms = [jnp.where(chosen[k], same[k][at], none) for k in range(bags)]
                while len(terms) > 1:
                    terms = [sum(terms[k + 1 : k + 2], terms[k]) for k in range(0, len(terms), 2)]
                pieces.append(terms[0])
        return jnp.concatenate(pieces, axis=0)

    def pooled_copy(part, q, j, slot):
        return pltpu.make_async_remote_copy(
            pooled_out.at[part, q, j],
            pooled_in.at[part, q * m + slot],
            pooled_send.at[part],
            pooled_recv.at[part],
            **at(plane * m + j),
        )

    def grad_copy(part, peer, slot):
        return pltpu.make_async_remote_copy(
            grad_out.at[part, peer],
            grad_in.at[part, slot],
            grad_send.at[part],
            grad_recv.at[part, slot],
            **at(peer),
        )

    def member(at):
        return lax.rem(local + at, m)

    def pairs(body):
        def run(pair, carry):
            body(pair)
            return carry

        lax.fori_loop(0, m // 2, run, 0)

    def near_pair(q, pair):
        return [hits(near[member(2 * pair + k), :, q]) for k in (1, 2)]

    def pool(part, q):
        rows_of = slabs[q, part].reshape(columns, slab_size)

        def both(pair):
            if keeps and part > 0:
                counted = kept[q, pair]
            else:
                counted = jnp.concatenate(near_pair(q, pair), axis=1)
                if keeps:
                    kept[q, pair] = counted
            summed = jnp.dot(rows_of, counted, preferred_element_type=jnp.float32)
            summed = summed.astype(jnp.bfloat16)
            first, second = member(2 * pair + 1), member(2 * pair + 2)
            pooled_out[part, q, first] = summed[:, :samples]
            pooled_copy(part, q, first, local).start()
            pooled_out[part, q, second] = summed[:, samples:]

            @pl.when(2 * pair + 2 < m)
            def _():
                pooled_copy(part, q, second, local).start()

        pairs(both)
        pooled_in[part, q * m + local] = pooled_out[part, q, local]

    def relay(part, step):
        q = nearest(step)
        slab_copy(part, q, 0, up).wait_recv()
        passed_slab(part, q, lambda copy: copy.start())
        half_copy(part, q, rep).start()

    def pool_from(part, step):
        q = nearest(step)
        half_copy(part, q, 1 - rep).wait_recv()
        pool(part, q)

    def batch(ref, send_sem, recv_sem):
        return pltpu.make_async_remote_copy(ref, ref, send_sem, recv_sem, **partner)

    def arrive(part):
        arrived = pooled_in.at[part, pl.ds(0, planes * (m - 1))]
        batch(arrived, pooled_send.at[part], pooled_recv.at[part]).wait_recv()

    def interact(part, first=True, rest=True):
        def mixed(feature):
            def add(other, carry):
                weight = w_ref[pl.ds(feature * n + other, 1), :]
                return carry + weight * pooled_in[part, other].astype(jnp.float32)

            start = jnp.zeros((columns, samples), jnp.float32)
            return lax.fori_loop(0, n, add, start, unroll=4).astype(jnp.bfloat16)

        def send(peer):
            grad_out[part, peer] = mixed(peer)
            grad_copy(part, peer, me).start()

        for step in range(planes - 1, 0, -1):
            if first if step > 1 else rest:
                q = nearest(step)
                each(0, lambda j: send(q * m + j))
        if rest:
            each(1, lambda j: send(plane * m + j))
            grad_in[part, me] = mixed(me)

    def far_pair(q, pair):
        counted = [hits(far[q * m + member(2 * pair + k)]) for k in (0, 1)]
        return jnp.concatenate(counted, axis=1)

    def keep_far():
        for step in range(1, planes):
            q = nearest(step)

            def take(pair):
                kept_own[q, pair] = far_pair(q, pair)

            if keeps:
                pairs(take)

    def collect(part):
        def add(first, second, counted):
            grads = jnp.concatenate([grad_in[part, first], grad_in[part, second]], axis=1)
            total[part] += lax.dot_general(
                counted, grads, (((1,), (1,)), ((), ())), preferred_element_type=jnp.float32
            )

        def ready(peer):
            grad_copy(part, peer, peer).wait_recv()

        def take_near(pair):
            first, second = (plane * m + member(2 * pair + k) for k in (1, 2))
            ready(first)
            pl.when(2 * pair + 2 < m)(lambda: ready(second))
            if keeps:
                add(first, second, kept[plane, pair])
            else:
                add(first, second, jnp.concatenate(near_pair(plane, pair), axis=1))

        def take_far(q, pair):
            first, second = (q * m + member(2 * pair + k) for k in (0, 1))
            ready(first)
            ready(second)
            add(first, second, kept_own[q, pair] if keeps else far_pair(q, pair))

        pairs(take_near)
        for step in range(1, planes):
            q = nearest(step)
            pairs(lambda pair: take_far(q, pair))

    batch(near.at[pl.ds(0, m - 1)], near_send, near_recv).wait_recv()
    pool(0, plane)
    relay(0, 1)

    @pl.when(inner)
    def _():
        relay(0, 2)
        pool(1, plane)
        pool_from(0, 1)
        relay(1, 1)
        relay(1, 2)
        pool_from(0, 2)
        relay(0, 3)
        pool_from(1, 1)
        pool_from(0, 3)
        relay(1, 3)
        pool_from(1, 2)
        arrive(0)
        interact(0, rest=False)
        pool_from(1, 3)
        interact(0, first=False)

    @pl.when(outer)
    def _():
        pool(1, plane)
        pool_from(0, 1)
        relay(1, 1)
        relay(0, 2)
        pool_from(1, 1)
        pool_from(0, 2)
        relay(1, 2)
        relay(0, 3)
        pool_from(1, 2)
        pool_from(0, 3)
        relay(1, 3)
        pool_from(1, 3)
        arrive(0)
        interact(0)

    arrive(1)
    interact(1)
    batch(far.at[pl.ds(0, n - m)], far_send, far_recv).wait_recv()
    keep_far()
    state_copy.wait()
    pieces = []
    for block in range(touch_count):
        at_block = touched_ref[0, block]
        pair = state_ref[pl.ds(at_block // 2, 1), :]
        pieces.append(jnp.where(lax.rem(at_block, 2) == 0, pair[:, :BLOCK], pair[:, BLOCK:]))
    state_row = jnp.concatenate(pieces, axis=1)
    state_col[...] = jnp.broadcast_to(state_row, (state_col.shape[1], slab_size)).T
    def total_copy(part):
        return pltpu.make_async_remote_copy(
            total.at[part], total_in.at[part], pair_sem.at[0, part], pair_sem.at[1, part], **partner
        )

    collect(0)
    total_copy(0).start()
    batch(near.at[pl.ds(0, m - 1)], near_send, near_recv).wait_send()
    batch(far.at[pl.ds(0, n - m)], far_send, far_recv).wait_send()
    batch(slabs.at[pl.ds(0, planes - 1), :, 0], half_send, half_recv.at[0, 0]).wait_send()
    for part in range(parts):
        own_slab(part, lambda copy: copy.wait_send())
        for step in range(1, planes):
            passed_slab(part, nearest(step), lambda copy: copy.wait_send())
        sent = pooled_out.at[part, :, pl.ds(0, m - 1)]
        batch(sent, pooled_send.at[part], pooled_recv.at[part]).wait_send()

    def grads_sent(part):
        sent = grad_out.at[part, pl.ds(0, n - 1)]
        batch(sent, grad_send.at[part], grad_recv.at[part, 0]).wait_send()

    grads_sent(0)
    dither_copy.wait()
    collect(1)
    total_copy(1).start()
    grads_sent(1)
    for part in range(parts):
        total_copy(part).wait_recv()

    def update(block, carry):
        at_rows = pl.ds(pl.multiple_of(block * BLOCK, BLOCK), BLOCK)
        grad = [total[part, at_rows, :] + total_in[part, at_rows, :] for part in range(parts)]
        grad = jnp.concatenate(grad, axis=1)
        state_next = state_col[at_rows, :] + jnp.sum(grad * grad, axis=1, keepdims=True) / width
        state_col[at_rows, :] = state_next
        divisor = jnp.sqrt(state_next) + 1e-08
        divisor = jnp.concatenate([divisor] * (width // divisor.shape[1]), axis=1)
        moved = slab[at_rows, :].astype(jnp.float32) - LEARN_RATE * grad / divisor
        out_ref[at_rows, :] = dither_round(moved, dither_in[at_rows, :])
        return carry

    lax.fori_loop(0, touch_count, update, 0, unroll=2)
    state_all = state_ref[...]
    block_at = 2 * lax.broadcasted_iota(jnp.int32, state_all.shape, 0)
    block_at = block_at + lax.broadcasted_iota(jnp.int32, state_all.shape, 1) // BLOCK
    state_row = state_col[...].T[:1, :]
    for block in range(touch_count):
        piece = state_row[:, block * BLOCK : (block + 1) * BLOCK]
        piece = jnp.broadcast_to(jnp.concatenate([piece, piece], axis=1), state_all.shape)
        state_all = jnp.where(block_at == touched_ref[0, block], piece, state_all)
    state_out_ref[...] = state_all
    for part in range(parts):
        total_copy(part).wait_send()


def fused_step(n, blocks, offsets, cot, touched, state, table, dither):
    micros, planes, m = blocks.shape[0], blocks.shape[1], blocks.shape[2]
    sample_count = blocks.shape[-1]
    samples = micros * sample_count
    cot_size = math.gcd(n, 16)
    slab_size, width = dither.shape
    columns = width // PARTS
    keeps = 2 * n * slab_size * samples <= KEEP_BYTES
    held = (planes, m // 2) if keeps else (1, 1)
    dma = pltpu.SemaphoreType.DMA
    block = (PARTS, n, columns, samples)
    vmem = pl.BlockSpec(memory_space=pltpu.VMEM)
    smem = pl.BlockSpec(memory_space=pltpu.SMEM)
    hbm = pl.BlockSpec(memory_space=pltpu.HBM)
    return pl.pallas_call(
        functools.partial(step_kernel, n),
        out_shape=(
            pltpu.VMEM((slab_size, width), jnp.bfloat16),
            pltpu.VMEM(state.shape, jnp.float32),
            pltpu.VMEM(table.shape, jnp.bfloat16),
        ),
        in_specs=[hbm, hbm, hbm, smem, hbm, hbm, hbm],
        out_specs=(vmem, vmem, vmem),
        scratch_shapes=[
            pltpu.VMEM(blocks.shape, jnp.int32),
            pltpu.VMEM(blocks.shape, jnp.int32),
            pltpu.VMEM(state.shape, jnp.float32),
            pltpu.VMEM(blocks.shape, jnp.int32),
            pltpu.VMEM((micros, cot_size, n, sample_count), jnp.bfloat16),
            pltpu.VMEM((m, micros, planes) + blocks.shape[3:], jnp.int32),
            pltpu.VMEM((n, micros) + blocks.shape[3:], jnp.int32),
            pltpu.VMEM((n * n, samples), jnp.float32),
            pltpu.VMEM((slab_size, width), jnp.int32),
            pltpu.VMEM((slab_size, width), jnp.bfloat16),
            pltpu.VMEM((planes, PARTS, 2, columns // 2, slab_size), jnp.bfloat16),
            pltpu.VMEM((PARTS, planes, m, columns, samples), jnp.bfloat16),
            pltpu.VMEM(block, jnp.bfloat16),
            pltpu.VMEM(block, jnp.bfloat16),
            pltpu.VMEM(block, jnp.bfloat16),
            pltpu.VMEM(held + (slab_size, 2 * samples), jnp.bfloat16),
            pltpu.VMEM(held + (slab_size, 2 * samples), jnp.bfloat16),
            pltpu.VMEM((PARTS, slab_size, columns), jnp.float32),
            pltpu.VMEM((PARTS, slab_size, columns), jnp.float32),
            pltpu.VMEM((slab_size, 128), jnp.float32),
            dma((6,)),
            dma((2, PARTS)),
            dma(()),
            dma(()),
            dma(()),
            dma(()),
            dma((2, PARTS, planes)),
            dma((PARTS, planes)),
            dma(()),
            dma((PARTS, planes)),
            dma((PARTS,)),
            dma((PARTS,)),
            dma((PARTS,)),
            dma((PARTS, n)),
        ],
        compiler_params=pltpu.CompilerParams(collective_id=0, has_side_effects=True),
        name="fused_step",
    )(blocks, offsets, cot, touched, state, table, dither)


def write_kernel(touched_ref, new_ref, state_ref, table_ref, out_ref, state_out_ref, place, sem):
    state_copy = pltpu.make_async_copy(state_ref, state_out_ref, sem.at[1])
    state_copy.start()
    blocks, touch_count = table_ref.shape[0], touched_ref.shape[1]

    def clear(block, carry):
        place[block] = -1
        return carry

    lax.fori_loop(0, blocks, clear, 0, unroll=8)
    for i in range(touch_count):
        place[touched_ref[0, i]] = i

    def write(block, carry):
        new = place[block]

        @pl.when(new >= 0)
        def _():
            pltpu.make_async_copy(new_ref.at[new], out_ref.at[block], sem.at[0]).start()

        @pl.when(new < 0)
        def _():
            pltpu.make_async_copy(table_ref.at[block], out_ref.at[block], sem.at[0]).start()

        return carry

    lax.fori_loop(0, blocks, write, 0)
    pltpu.make_async_copy(table_ref, out_ref, sem.at[0]).wait()
    state_copy.wait()


def write_table(touched, new_rows, state, table):
    vmem = pl.BlockSpec(memory_space=pltpu.VMEM)
    hbm = pl.BlockSpec(memory_space=pltpu.HBM)
    held = [pltpu.with_memory_space_constraint(x, pltpu.VMEM) for x in (new_rows, state, table)]
    return pl.pallas_call(
        write_kernel,
        out_shape=(
            jax.ShapeDtypeStruct(table.shape, table.dtype),
            jax.ShapeDtypeStruct(state.shape, state.dtype),
        ),
        in_specs=[pl.BlockSpec(memory_space=pltpu.SMEM), vmem, vmem, vmem],
        out_specs=(hbm, hbm),
        scratch_shapes=[pltpu.SMEM((table.shape[0],), jnp.int32), pltpu.SemaphoreType.DMA((2,))],
        compiler_params=pltpu.CompilerParams(vmem_limit_bytes=4 << 20),
        name="write_table",
    )(touched, *held)


def per_device(
    lookup_block, lookup_offset, interaction_grad, table, adagrad_state, touched_blocks, dither
):
    micro_count, sample_count, feature_count, bag_count = lookup_block.shape
    n = lax.axis_size("mp")
    row_count, emb_width = table.shape
    touch_count = touched_blocks.shape[1]
    split = (micro_count, PLANES, feature_count // PLANES, bag_count, sample_count)
    blocks = lookup_block.transpose(0, 2, 3, 1).reshape(split)
    offsets = lookup_offset.transpose(0, 2, 3, 1).reshape(split)
    cot = interaction_grad.transpose(0, 2, 3, 1)
    table_blocks = table.reshape(row_count // BLOCK, BLOCK, emb_width)
    state = adagrad_state.reshape(row_count // (2 * BLOCK), 2 * BLOCK)
    new_rows, new_state, table_copy = fused_step(
        n, blocks, offsets, cot, touched_blocks, state, table_blocks, dither[0]
    )
    new_rows = new_rows.reshape(touch_count, BLOCK, emb_width)
    new_table, new_state = write_table(touched_blocks, new_rows, new_state, table_copy)
    return (new_table.reshape(row_count, emb_width), new_state.reshape(row_count))


def solution(mesh):
    return jax.shard_map(
        per_device,
        mesh=mesh,
        in_specs=(
            P(None, ("rep", "mp"), None, None),
            P(None, ("rep", "mp"), None, None),
            P(None, ("rep", "mp"), None, None),
            P("mp", None),
            P("mp"),
            P("mp", None),
            P("mp", None, None),
        ),
        out_specs=(P("mp", None), P("mp")),
        check_vma=False,
    )
```

```python
import functools
import math

import jax
import jax.numpy as jnp
from jax import lax
from jax.experimental import pallas as pl
from jax.experimental.pallas import tpu as pltpu
from jax.sharding import PartitionSpec as P

BLOCK = 64
PLANES = 4
UNITS = 4
UNROLL = 4
PARTS = ((0, 1), (1, 1), (2, 2))
HALVES = ((0, 2, (0, 1)), (2, 2, (2,)))
LEARN_RATE = 0.1
POOL_DECAY = 0.5
DITHER_UNIT = 2.0 ** (-15)
SMALLEST = 2.0 ** (-14)
KEEP_BYTES = 8 << 20
MESH = pl.DeviceIdType.MESH


def dither_round(weights, dither_bits):
    magnitude = jnp.maximum(jnp.abs(weights), SMALLEST)
    spacing = jnp.exp2(jnp.floor(jnp.log2(magnitude)) - 7.0)
    grid_level = jnp.floor(weights / spacing + dither_bits.astype(jnp.float32) * DITHER_UNIT)
    return (grid_level * spacing).astype(jnp.bfloat16)


def plane_order(planes, plane, step):
    picked = jnp.int32(0)
    for own in range(planes):
        near_first = sorted(range(planes), key=lambda q: (abs(q - own), (q - own) * (2 * own - planes)))
        picked = jnp.where(plane == own, near_first[step], picked)
    return picked


def step_kernel(
    n,
    block_hbm,
    offset_hbm,
    cot_ref,
    touched_ref,
    state_hbm,
    table_ref,
    dither_ref,
    out_ref,
    state_out_ref,
    table_in,
    block_ref,
    offset_ref,
    state_ref,
    rows_ref,
    cot_in,
    near,
    far,
    w_ref,
    dither_in,
    slab,
    slabs,
    pooled_out,
    pooled_in,
    grad_out,
    grad_in,
    kept,
    kept_own,
    total,
    total_in,
    state_col,
    local_sem,
    pair_sem,
    near_send,
    near_recv,
    far_send,
    far_recv,
    slab_send,
    slab_recv,
    half_send,
    half_recv,
    pooled_send,
    pooled_recv,
    grad_send,
    grad_recv,
    grad_last,
):
    me = lax.axis_index("mp")
    rep = lax.axis_index("rep")
    planes, parts = slabs.shape[0], len(PARTS)
    m = n // planes
    plane = me // m
    local = lax.rem(me, m)
    samples = w_ref.shape[1]
    bags = rows_ref.shape[3]
    slab_size, width = slab.shape
    columns = width // UNITS
    touch_count = slab_size // BLOCK
    keeps = kept.shape[0] == planes

    def at(peer):
        return {"device_id": (rep, peer), "device_id_type": MESH}

    partner = {"device_id": (1 - rep, me), "device_id_type": MESH}

    def each(first, body):
        def run(step, carry):
            body(lax.rem(local + step, m))
            return carry

        lax.fori_loop(first, m, run, 0)

    def others(body):
        def run(step, carry):
            body(lax.rem(me + step, n))
            return carry

        lax.fori_loop(1, n, run, 0)

    def outside(body, first=0, last=n - m):
        def run(step, carry):
            body(lax.rem(plane + 1 + step // m, planes), lax.rem(local + step, m))
            return carry

        lax.fori_loop(first, last, run, 0)

    def nearest(step):
        return plane_order(planes, plane, step)

    def units(part):
        first, count = PARTS[part]
        return pl.ds(first, count)

    def tall(part):
        return PARTS[part][1] * columns

    barrier = pltpu.get_barrier_semaphore()
    others(lambda peer: pl.semaphore_signal(barrier, inc=1, **at(peer)))
    pl.semaphore_signal(barrier, inc=1, **partner)
    table_copy = pltpu.make_async_copy(table_ref, table_in, local_sem.at[0])
    table_copy.start()
    block_copy = pltpu.make_async_copy(block_hbm, block_ref, local_sem.at[1])
    block_copy.start()
    offset_copy = pltpu.make_async_copy(offset_hbm, offset_ref, local_sem.at[2])
    offset_copy.start()
    state_copy = pltpu.make_async_copy(state_hbm, state_ref, local_sem.at[3])
    state_copy.start()
    dither_copy = pltpu.make_async_copy(dither_ref, dither_in, local_sem.at[4])
    dither_copy.start()
    block_copy.wait()
    offset_copy.wait()
    rows_ref[...] = block_ref[...] * BLOCK + offset_ref[...]
    near[local] = rows_ref[:, :, local]
    table_copy.wait()
    for block in range(touch_count):
        slab[block * BLOCK : (block + 1) * BLOCK, :] = table_in[touched_ref[0, block]]
    turned = slab[...].astype(jnp.float32).T.astype(jnp.bfloat16)
    slabs[plane] = turned.reshape(slabs.shape[1:])
    pl.semaphore_wait(barrier, n)

    def near_copy(j, slot):
        return pltpu.make_async_remote_copy(
            rows_ref.at[:, :, j],
            near.at[slot],
            near_send,
            near_recv,
            **at(plane * m + j),
        )

    def far_copy(q, j, slot):
        return pltpu.make_async_remote_copy(
            rows_ref.at[:, q, j],
            far.at[slot],
            far_send,
            far_recv,
            **at(q * m + j),
        )

    def slab_copy(part, q, slot, peer):
        return pltpu.make_async_remote_copy(
            slabs.at[q, units(part), rep],
            slabs.at[q, units(part), rep],
            slab_send.at[part, slot],
            slab_recv.at[part, q],
            **at(peer),
        )

    def half_copy(part, q, which):
        return pltpu.make_async_remote_copy(
            slabs.at[q, units(part), which],
            slabs.at[q, units(part), which],
            half_send,
            half_recv.at[part, q],
            **partner,
        )

    has_up, has_down = plane + 1 < planes, plane > 0
    inner = jnp.logical_and(has_up, has_down)
    outer = jnp.logical_not(inner)
    up, down = lax.rem(me + m, n), lax.rem(me + n - m, n)

    def own_slab(part, act):
        @pl.when(has_up)
        def _():
            act(slab_copy(part, plane, plane, up))

        @pl.when(has_down)
        def _():
            act(slab_copy(part, plane, planes, down))

    def passed_slab(part, q, act):
        @pl.when(jnp.logical_and(q < plane, has_up))
        def _():
            act(slab_copy(part, q, q, up))

        @pl.when(jnp.logical_and(q > plane, has_down))
        def _():
            act(slab_copy(part, q, q, down))

    each(1, lambda j: near_copy(j, local).start())
    own_slab(0, lambda copy: copy.start())
    outside(lambda q, j: far_copy(q, j, me).start())
    cot_size = cot_in.shape[1]

    def spread(chunk, carry):
        cot_copy = pltpu.make_async_copy(
            cot_ref.at[:, pl.ds(chunk * cot_size, cot_size)], cot_in, local_sem.at[5]
        )
        cot_copy.start()
        cot_copy.wait()
        for i in range(cot_size):
            pieces = [cot_in[micro, i].astype(jnp.float32) for micro in range(cot_in.shape[0])]
            at_row = pl.multiple_of((chunk * cot_size + i) * n, n)
            w_ref[pl.ds(at_row, n), :] = jnp.concatenate(pieces, axis=-1)
        return carry

    lax.fori_loop(0, n // cot_size, spread, 0)
    place = lax.broadcasted_iota(jnp.int32, (n, samples), 0)

    def fold(f, carry):
        along = pl.ds(pl.multiple_of(f * n, n), n)
        across = pl.ds(f, n, stride=n)
        row, column = w_ref[along, :], w_ref[across, :]
        both = row + column + jnp.where(place == f, POOL_DECAY, 0.0)
        w_ref[along, :] = jnp.where(place >= f, both, row)
        w_ref[across, :] = jnp.where(place >= f, both, column)
        return carry

    lax.fori_loop(0, n, fold, 0)
    for part in range(1, parts):
        own_slab(part, lambda copy: copy.start())
    total[...] = jnp.zeros_like(total)

    sublanes = 16
    place_of = lax.broadcasted_iota(jnp.int32, (BLOCK, samples), 0)
    place_of = place_of.astype(jnp.float32).astype(jnp.bfloat16)
    one = jnp.ones((sublanes, samples), jnp.bfloat16)
    none = jnp.zeros_like(one)

    def hits(micros):
        rows = jnp.concatenate([micros[i] for i in range(micros.shape[0])], axis=-1)
        block_of = (rows // BLOCK).astype(jnp.float32)
        offset_of = lax.rem(rows, BLOCK).astype(jnp.float32)

        def wide(values, lookup):
            row = jnp.broadcast_to(values[lookup : lookup + 1, :], (sublanes, samples))
            return row.astype(jnp.bfloat16)

        spans = [slice(at, at + sublanes) for at in range(0, BLOCK, sublanes)]
        offsets = [wide(offset_of, lookup) for lookup in range(bags)]
        same = [[jnp.where(offset == place_of[span], one, none) for span in spans] for offset in offsets]
        in_block = [wide(block_of, lookup) for lookup in range(bags)]
        pieces = []
        for block in range(slab_size // BLOCK):
            chosen = [row == jnp.full_like(row, block) for row in in_block]
            for at in range(len(spans)):
                terms = [jnp.where(chosen[k], same[k][at], none) for k in range(bags)]
                while len(terms) > 1:
                    terms = [sum(terms[k + 1 : k + 2], terms[k]) for k in range(0, len(terms), 2)]
                pieces.append(terms[0])
        return jnp.concatenate(pieces, axis=0)

    def pooled_copy(part, q, j, slot):
        return pltpu.make_async_remote_copy(
            pooled_out.at[units(part), q, j],
            pooled_in.at[units(part), q * m + slot],
            pooled_send.at[part],
            pooled_recv.at[part],
            **at(plane * m + j),
        )

    def grad_copy(part, peer, slot):
        return pltpu.make_async_remote_copy(
            grad_out.at[units(part), peer],
            grad_in.at[units(part), slot],
            grad_send.at[part],
            grad_last.at[slot] if part == parts - 1 else grad_recv.at[part, slot // m],
            **at(peer),
        )

    def member(at):
        return lax.rem(local + at, m)

    def pairs(body):
        def run(pair, carry):
            body(pair)
            return carry

        lax.fori_loop(0, m // 2, run, 0)

    def near_pair(q, pair):
        return [hits(near[member(2 * pair + k), :, q]) for k in (1, 2)]

    def pool(part, q):
        rows_of = slabs[q, units(part)].reshape(tall(part), slab_size)

        def both(pair):
            if keeps and part > 0:
                counted = kept[q, pair]
            else:
                counted = jnp.concatenate(near_pair(q, pair), axis=1)
                if keeps:
                    kept[q, pair] = counted
            summed = jnp.dot(rows_of, counted, preferred_element_type=jnp.float32)
            summed = summed.astype(jnp.bfloat16).reshape(-1, columns, 2 * samples)
            first, second = member(2 * pair + 1), member(2 * pair + 2)
            pooled_out[units(part), q, first] = summed[:, :, :samples]
            pooled_copy(part, q, first, local).start()
            pooled_out[units(part), q, second] = summed[:, :, samples:]

            @pl.when(2 * pair + 2 < m)
            def _():
                pooled_copy(part, q, second, local).start()

        pairs(both)
        pooled_in[units(part), q * m + local] = pooled_out[units(part), q, local]

    def relay(part, step):
        q = nearest(step)
        slab_copy(part, q, q, up).wait_recv()
        passed_slab(part, q, lambda copy: copy.start())
        half_copy(part, q, rep).start()

    def pool_from(part, step):
        q = nearest(step)
        half_copy(part, q, 1 - rep).wait_recv()
        pool(part, q)

    def batch(ref, send_sem, recv_sem):
        return pltpu.make_async_remote_copy(ref, ref, send_sem, recv_sem, **partner)

    def arrive(part):
        arrived = pooled_in.at[units(part), pl.ds(0, planes * (m - 1))]
        batch(arrived, pooled_send.at[part], pooled_recv.at[part]).wait_recv()

    def interact(part, first=True, rest=True):
        def mixed(feature):
            def add(other, carry):
                weight = w_ref[pl.ds(feature * n + other, 1), :]
                seen = pooled_in[units(part), other].reshape(tall(part), samples)
                return carry + weight * seen.astype(jnp.float32)

            start = jnp.zeros((tall(part), samples), jnp.float32)
            mix = lax.fori_loop(0, n, add, start, unroll=UNROLL)
            return mix.astype(jnp.bfloat16).reshape(-1, columns, samples)

        def send(peer):
            grad_out[units(part), peer] = mixed(peer)
            grad_copy(part, peer, me).start()

        for step in range(planes - 1, 0, -1):
            if first if step > 1 else rest:
                q = nearest(step)
                each(0, lambda j: send(q * m + j))
        if rest:
            each(1, lambda j: send(plane * m + j))
            grad_in[units(part), me] = mixed(me)

    def far_pair(q, pair):
        counted = [hits(far[q * m + member(2 * pair + k)]) for k in (0, 1)]
        return jnp.concatenate(counted, axis=1)

    def keep_far():
        for step in range(1, planes):
            q = nearest(step)

            def take(pair):
                kept_own[q, pair] = far_pair(q, pair)

            if keeps:
                pairs(take)

    def collect(which):
        first_unit, count, members = HALVES[which]

        def add(first, second, counted):
            grads = [grad_in[pl.ds(first_unit, count), peer] for peer in (first, second)]
            grads = [piece.reshape(count * columns, samples) for piece in grads]
            total[which] += lax.dot_general(
                counted,
                jnp.concatenate(grads, axis=1),
                (((1,), (1,)), ((), ())),
                preferred_element_type=jnp.float32,
            )

        def plane_ready(q, blocks):
            for part in members:
                if part < parts - 1:
                    arrived = grad_in.at[units(part), pl.ds(0, blocks)]
                    batch(arrived, grad_send.at[part], grad_recv.at[part, q]).wait_recv()

        def ready(peer):
            if parts - 1 in members:
                grad_copy(parts - 1, peer, peer).wait_recv()

        def take_near(pair):
            first, second = (plane * m + member(2 * pair + k) for k in (1, 2))
            ready(first)
            pl.when(2 * pair + 2 < m)(lambda: ready(second))
            if keeps:
                add(first, second, kept[plane, pair])
            else:
                add(first, second, jnp.concatenate(near_pair(plane, pair), axis=1))

        def take_far(q, pair):
            first, second = (q * m + member(2 * pair + k) for k in (0, 1))
            ready(first)
            ready(second)
            add(first, second, kept_own[q, pair] if keeps else far_pair(q, pair))

        plane_ready(plane, m - 1)
        pairs(take_near)
        for step in range(1, planes):
            q = jnp.where(inner, nearest(step % (planes - 1) + 1), nearest(step))
            plane_ready(q, m)
            pairs(lambda pair: take_far(q, pair))

    batch(near.at[pl.ds(0, m - 1)], near_send, near_recv).wait_recv()
    pool(0, plane)
    relay(0, 1)

    @pl.when(inner)
    def _():
        relay(0, 2)
        pool(1, plane)
        relay(1, 1)
        relay(1, 2)
        pool_from(0, 1)
        pool_from(0, 2)
        relay(0, 3)
        relay(2, 1)
        relay(2, 2)
        pool_from(1, 1)
        relay(1, 3)
        pool_from(0, 3)
        pool_from(1, 2)
        pool_from(1, 3)
        pool(2, plane)
        relay(2, 3)
        arrive(0)
        interact(0)
        pool_from(2, 1)
        arrive(1)
        interact(1)
        pool_from(2, 2)
        pool_from(2, 3)

    @pl.when(outer)
    def _():
        pool(1, plane)
        relay(1, 1)
        pool_from(0, 1)
        relay(2, 1)
        pool_from(1, 1)
        relay(0, 2)
        relay(1, 2)
        pool_from(0, 2)
        pool_from(1, 2)
        pool(2, plane)
        relay(0, 3)
        relay(2, 2)
        relay(1, 3)
        pool_from(0, 3)
        pool_from(1, 3)
        pool_from(2, 1)
        pool_from(2, 2)
        arrive(0)
        interact(0)
        relay(2, 3)
        pool_from(2, 3)
        arrive(1)
        interact(1)

    arrive(2)
    interact(2)
    batch(far.at[pl.ds(0, n - m)], far_send, far_recv).wait_recv()
    keep_far()
    state_copy.wait()
    pieces = []
    for block in range(touch_count):
        at_block = touched_ref[0, block]
        pair = state_ref[pl.ds(at_block // 2, 1), :]
        pieces.append(jnp.where(lax.rem(at_block, 2) == 0, pair[:, :BLOCK], pair[:, BLOCK:]))
    state_row = jnp.concatenate(pieces, axis=1)
    state_col[...] = jnp.broadcast_to(state_row, (state_col.shape[1], slab_size)).T
    def total_copy(part):
        return pltpu.make_async_remote_copy(
            total.at[part], total_in.at[part], pair_sem.at[0, part], pair_sem.at[1, part], **partner
        )

    collect(0)
    total_copy(0).start()
    batch(near.at[pl.ds(0, m - 1)], near_send, near_recv).wait_send()
    batch(far.at[pl.ds(0, n - m)], far_send, far_recv).wait_send()
    batch(slabs.at[pl.ds(0, planes - 1), :, 0], half_send, half_recv.at[0, 0]).wait_send()
    for part in range(parts):
        own_slab(part, lambda copy: copy.wait_send())
        for step in range(1, planes):
            passed_slab(part, nearest(step), lambda copy: copy.wait_send())
        sent = pooled_out.at[units(part), :, pl.ds(0, m - 1)]
        batch(sent, pooled_send.at[part], pooled_recv.at[part]).wait_send()

    def grads_sent(part):
        sent = grad_out.at[units(part), pl.ds(0, n - 1)]
        batch(sent, grad_send.at[part], grad_last.at[0]).wait_send()

    grads_sent(0)
    grads_sent(1)
    dither_copy.wait()
    collect(1)
    total_copy(1).start()
    grads_sent(2)
    for which in range(len(HALVES)):
        total_copy(which).wait_recv()

    def update(block, carry):
        at_rows = pl.ds(pl.multiple_of(block * BLOCK, BLOCK), BLOCK)
        grad = [total[h, at_rows, :] + total_in[h, at_rows, :] for h in range(len(HALVES))]
        grad = jnp.concatenate(grad, axis=1)
        state_next = state_col[at_rows, :] + jnp.sum(grad * grad, axis=1, keepdims=True) / width
        state_col[at_rows, :] = state_next
        divisor = jnp.sqrt(state_next) + 1e-08
        divisor = jnp.concatenate([divisor] * (width // divisor.shape[1]), axis=1)
        moved = slab[at_rows, :].astype(jnp.float32) - LEARN_RATE * grad / divisor
        out_ref[at_rows, :] = dither_round(moved, dither_in[at_rows, :])
        return carry

    lax.fori_loop(0, touch_count, update, 0, unroll=2)
    state_all = state_ref[...]
    block_at = 2 * lax.broadcasted_iota(jnp.int32, state_all.shape, 0)
    block_at = block_at + lax.broadcasted_iota(jnp.int32, state_all.shape, 1) // BLOCK
    state_row = state_col[...].T[:1, :]
    for block in range(touch_count):
        piece = state_row[:, block * BLOCK : (block + 1) * BLOCK]
        piece = jnp.broadcast_to(jnp.concatenate([piece, piece], axis=1), state_all.shape)
        state_all = jnp.where(block_at == touched_ref[0, block], piece, state_all)
    state_out_ref[...] = state_all
    for which in range(len(HALVES)):
        total_copy(which).wait_send()


def fused_step(n, blocks, offsets, cot, touched, state, table, dither):
    micros, planes, m = blocks.shape[0], blocks.shape[1], blocks.shape[2]
    sample_count = blocks.shape[-1]
    samples = micros * sample_count
    cot_size = math.gcd(n, 16)
    slab_size, width = dither.shape
    columns, parts = width // UNITS, len(PARTS)
    keeps = 2 * n * slab_size * samples <= KEEP_BYTES
    held = (planes, m // 2) if keeps else (1, 1)
    dma = pltpu.SemaphoreType.DMA
    block = (UNITS, n, columns, samples)
    vmem = pl.BlockSpec(memory_space=pltpu.VMEM)
    smem = pl.BlockSpec(memory_space=pltpu.SMEM)
    hbm = pl.BlockSpec(memory_space=pltpu.HBM)
    return pl.pallas_call(
        functools.partial(step_kernel, n),
        out_shape=(
            pltpu.VMEM((slab_size, width), jnp.bfloat16),
            pltpu.VMEM(state.shape, jnp.float32),
            pltpu.VMEM(table.shape, jnp.bfloat16),
        ),
        in_specs=[hbm, hbm, hbm, smem, hbm, hbm, hbm],
        out_specs=(vmem, vmem, vmem),
        scratch_shapes=[
            pltpu.VMEM(blocks.shape, jnp.int32),
            pltpu.VMEM(blocks.shape, jnp.int32),
            pltpu.VMEM(state.shape, jnp.float32),
            pltpu.VMEM(blocks.shape, jnp.int32),
            pltpu.VMEM((micros, cot_size, n, sample_count), jnp.bfloat16),
            pltpu.VMEM((m, micros, planes) + blocks.shape[3:], jnp.int32),
            pltpu.VMEM((n, micros) + blocks.shape[3:], jnp.int32),
            pltpu.VMEM((n * n, samples), jnp.float32),
            pltpu.VMEM((slab_size, width), jnp.int32),
            pltpu.VMEM((slab_size, width), jnp.bfloat16),
            pltpu.VMEM((planes, UNITS, 2, columns // 2, slab_size), jnp.bfloat16),
            pltpu.VMEM((UNITS, planes, m, columns, samples), jnp.bfloat16),
            pltpu.VMEM(block, jnp.bfloat16),
            pltpu.VMEM(block, jnp.bfloat16),
            pltpu.VMEM(block, jnp.bfloat16),
            pltpu.VMEM(held + (slab_size, 2 * samples), jnp.bfloat16),
            pltpu.VMEM(held + (slab_size, 2 * samples), jnp.bfloat16),
            pltpu.VMEM((len(HALVES), slab_size, width // len(HALVES)), jnp.float32),
            pltpu.VMEM((len(HALVES), slab_size, width // len(HALVES)), jnp.float32),
            pltpu.VMEM((slab_size, 128), jnp.float32),
            dma((6,)),
            dma((2, len(HALVES))),
            dma(()),
            dma(()),
            dma(()),
            dma(()),
            dma((parts, planes + 1)),
            dma((parts, planes)),
            dma(()),
            dma((parts, planes)),
            dma((parts,)),
            dma((parts,)),
            dma((parts,)),
            dma((parts - 1, planes)),
            dma((n,)),
        ],
        compiler_params=pltpu.CompilerParams(collective_id=0, has_side_effects=True),
        name="fused_step",
    )(blocks, offsets, cot, touched, state, table, dither)


def write_kernel(touched_ref, new_ref, state_ref, table_ref, out_ref, state_out_ref, place, sem):
    state_copy = pltpu.make_async_copy(state_ref, state_out_ref, sem.at[1])
    state_copy.start()
    blocks, touch_count = table_ref.shape[0], touched_ref.shape[1]

    def clear(block, carry):
        place[block] = -1
        return carry

    lax.fori_loop(0, blocks, clear, 0, unroll=8)
    for i in range(touch_count):
        place[touched_ref[0, i]] = i

    def write(block, carry):
        new = place[block]

        @pl.when(new >= 0)
        def _():
            pltpu.make_async_copy(new_ref.at[new], out_ref.at[block], sem.at[0]).start()

        @pl.when(new < 0)
        def _():
            pltpu.make_async_copy(table_ref.at[block], out_ref.at[block], sem.at[0]).start()

        return carry

    lax.fori_loop(0, blocks, write, 0)
    pltpu.make_async_copy(table_ref, out_ref, sem.at[0]).wait()
    state_copy.wait()


def write_table(touched, new_rows, state, table):
    vmem = pl.BlockSpec(memory_space=pltpu.VMEM)
    hbm = pl.BlockSpec(memory_space=pltpu.HBM)
    held = [pltpu.with_memory_space_constraint(x, pltpu.VMEM) for x in (new_rows, state, table)]
    return pl.pallas_call(
        write_kernel,
        out_shape=(
            jax.ShapeDtypeStruct(table.shape, table.dtype),
            jax.ShapeDtypeStruct(state.shape, state.dtype),
        ),
        in_specs=[pl.BlockSpec(memory_space=pltpu.SMEM), vmem, vmem, vmem],
        out_specs=(hbm, hbm),
        scratch_shapes=[pltpu.SMEM((table.shape[0],), jnp.int32), pltpu.SemaphoreType.DMA((2,))],
        compiler_params=pltpu.CompilerParams(vmem_limit_bytes=4 << 20),
        name="write_table",
    )(touched, *held)


def per_device(
    lookup_block, lookup_offset, interaction_grad, table, adagrad_state, touched_blocks, dither
):
    micro_count, sample_count, feature_count, bag_count = lookup_block.shape
    n = lax.axis_size("mp")
    row_count, emb_width = table.shape
    touch_count = touched_blocks.shape[1]
    split = (micro_count, PLANES, feature_count // PLANES, bag_count, sample_count)
    blocks = lookup_block.transpose(0, 2, 3, 1).reshape(split)
    offsets = lookup_offset.transpose(0, 2, 3, 1).reshape(split)
    cot = interaction_grad.transpose(0, 2, 3, 1)
    table_blocks = table.reshape(row_count // BLOCK, BLOCK, emb_width)
    state = adagrad_state.reshape(row_count // (2 * BLOCK), 2 * BLOCK)
    new_rows, new_state, table_copy = fused_step(
        n, blocks, offsets, cot, touched_blocks, state, table_blocks, dither[0]
    )
    new_rows = new_rows.reshape(touch_count, BLOCK, emb_width)
    new_table, new_state = write_table(touched_blocks, new_rows, new_state, table_copy)
    return (new_table.reshape(row_count, emb_width), new_state.reshape(row_count))


def solution(mesh):
    return jax.shard_map(
        per_device,
        mesh=mesh,
        in_specs=(
            P(None, ("rep", "mp"), None, None),
            P(None, ("rep", "mp"), None, None),
            P(None, ("rep", "mp"), None, None),
            P("mp", None),
            P("mp"),
            P("mp", None),
            P("mp", None, None),
        ),
        out_specs=(P("mp", None), P("mp")),
        check_vma=False,
    )
```

```python
import functools
import math

import jax
import jax.numpy as jnp
from jax import lax
from jax.experimental import pallas as pl
from jax.experimental.pallas import tpu as pltpu
from jax.sharding import PartitionSpec as P

BLOCK = 64
PLANES = 4
UNITS = 4
UNROLL = 4
CHUNKS = 2
PARTS = ((0, 1), (1, 1), (2, 2))
HALVES = ((0, 2, (0, 1)), (2, 2, (2,)))
LEARN_RATE = 0.1
POOL_DECAY = 0.5
DITHER_UNIT = 2.0 ** (-15)
SMALLEST = 2.0 ** (-14)
KEEP_BYTES = 8 << 20
MESH = pl.DeviceIdType.MESH


def dither_round(weights, dither_bits):
    magnitude = jnp.maximum(jnp.abs(weights), SMALLEST)
    exponent = jnp.floor(jnp.log2(magnitude)) - 7.0
    spacing, per_spacing = jnp.exp2(exponent), jnp.exp2(-exponent)
    grid_level = jnp.floor(weights * per_spacing + dither_bits.astype(jnp.float32) * DITHER_UNIT)
    return (grid_level * spacing).astype(jnp.bfloat16)


def plane_order(planes, plane, step):
    picked = jnp.int32(0)
    for own in range(planes):
        near_first = sorted(range(planes), key=lambda q: (abs(q - own), (q - own) * (2 * own - planes)))
        picked = jnp.where(plane == own, near_first[step], picked)
    return picked


def step_kernel(
    n,
    block_hbm,
    offset_hbm,
    cot_ref,
    touched_ref,
    state_hbm,
    table_ref,
    dither_ref,
    state_out_ref,
    table_in,
    block_ref,
    offset_ref,
    state_ref,
    rows_ref,
    cot_in,
    near,
    far,
    w_ref,
    dither_in,
    slab,
    slabs,
    pooled_out,
    pooled_in,
    wide,
    grad_out,
    grad_in,
    kept,
    kept_own,
    total,
    total_in,
    state_col,
    local_sem,
    pair_sem,
    near_send,
    near_recv,
    far_send,
    far_recv,
    slab_send,
    slab_recv,
    half_send,
    half_recv,
    pooled_send,
    pooled_recv,
    grad_send,
    grad_recv,
    grad_last,
):
    me = lax.axis_index("mp")
    rep = lax.axis_index("rep")
    planes, parts = slabs.shape[0], len(PARTS)
    m = n // planes
    plane = me // m
    local = lax.rem(me, m)
    samples = w_ref.shape[1]
    bags = rows_ref.shape[3]
    slab_size, width = slab.shape
    columns = width // UNITS
    touch_count = slab_size // BLOCK
    keeps = kept.shape[0] == planes

    def at(peer):
        return {"device_id": (rep, peer), "device_id_type": MESH}

    partner = {"device_id": (1 - rep, me), "device_id_type": MESH}

    def each(first, body):
        def run(step, carry):
            body(lax.rem(local + step, m))
            return carry

        lax.fori_loop(first, m, run, 0)

    def others(body):
        def run(step, carry):
            body(lax.rem(me + step, n))
            return carry

        lax.fori_loop(1, n, run, 0)

    def outside(body, first=0, last=n - m):
        def run(step, carry):
            body(lax.rem(plane + 1 + step // m, planes), lax.rem(local + step, m))
            return carry

        lax.fori_loop(first, last, run, 0)

    def nearest(step):
        return plane_order(planes, plane, step)

    def units(part):
        first, count = PARTS[part]
        return pl.ds(first, count)

    def tall(part):
        return PARTS[part][1] * columns

    barrier = pltpu.get_barrier_semaphore()
    others(lambda peer: pl.semaphore_signal(barrier, inc=1, **at(peer)))
    pl.semaphore_signal(barrier, inc=1, **partner)
    table_blocks = table_ref.shape[0]
    held_table = table_in.at[pl.ds(0, table_blocks)]
    table_copy = pltpu.make_async_copy(table_ref, held_table, local_sem.at[0])
    table_copy.start()
    block_copy = pltpu.make_async_copy(block_hbm, block_ref, local_sem.at[1])
    block_copy.start()
    offset_copy = pltpu.make_async_copy(offset_hbm, offset_ref, local_sem.at[2])
    offset_copy.start()
    state_copy = pltpu.make_async_copy(state_hbm, state_ref, local_sem.at[3])
    state_copy.start()
    dither_copy = pltpu.make_async_copy(dither_ref, dither_in, local_sem.at[4])
    dither_copy.start()
    block_copy.wait()
    offset_copy.wait()
    rows_ref[...] = block_ref[...] * BLOCK + offset_ref[...]
    near[local] = rows_ref[:, :, local]
    table_copy.wait()
    for block in range(touch_count):
        slab[block * BLOCK : (block + 1) * BLOCK, :] = table_in[touched_ref[0, block]]
    turned = slab[...].astype(jnp.float32).T.astype(jnp.bfloat16)
    slabs[plane] = turned.reshape(slabs.shape[1:])
    pl.semaphore_wait(barrier, n)

    def near_copy(j, slot):
        return pltpu.make_async_remote_copy(
            rows_ref.at[:, :, j],
            near.at[slot],
            near_send,
            near_recv,
            **at(plane * m + j),
        )

    def far_copy(q, j, slot):
        return pltpu.make_async_remote_copy(
            rows_ref.at[:, q, j],
            far.at[slot],
            far_send,
            far_recv,
            **at(q * m + j),
        )

    def slab_copy(part, q, slot, peer):
        return pltpu.make_async_remote_copy(
            slabs.at[q, units(part), rep],
            slabs.at[q, units(part), rep],
            slab_send.at[slot],
            slab_recv.at[part, q],
            **at(peer),
        )

    def half_copy(part, q, which):
        return pltpu.make_async_remote_copy(
            slabs.at[q, units(part), which],
            slabs.at[q, units(part), which],
            half_send,
            half_recv.at[part, q],
            **partner,
        )

    has_up, has_down = plane + 1 < planes, plane > 0
    inner = jnp.logical_and(has_up, has_down)
    outer = jnp.logical_not(inner)
    up, down = lax.rem(me + m, n), lax.rem(me + n - m, n)

    def own_slab(part, act):
        @pl.when(has_up)
        def _():
            act(slab_copy(part, plane, 0, up))

        @pl.when(has_down)
        def _():
            act(slab_copy(part, plane, 0, down))

    def passed_slab(part, q, act):
        @pl.when(jnp.logical_and(q < plane, has_up))
        def _():
            act(slab_copy(part, q, 1, up))

        @pl.when(jnp.logical_and(q > plane, has_down))
        def _():
            act(slab_copy(part, q, 1, down))

    each(1, lambda j: near_copy(j, local).start())
    own_slab(0, lambda copy: copy.start())
    outside(lambda q, j: far_copy(q, j, me).start())
    cot_size = cot_in.shape[1]

    def spread(chunk, carry):
        cot_copy = pltpu.make_async_copy(
            cot_ref.at[:, pl.ds(chunk * cot_size, cot_size)], cot_in, local_sem.at[5]
        )
        cot_copy.start()
        cot_copy.wait()
        for i in range(cot_size):
            pieces = [cot_in[micro, i].astype(jnp.float32) for micro in range(cot_in.shape[0])]
            at_row = pl.multiple_of((chunk * cot_size + i) * n, n)
            w_ref[pl.ds(at_row, n), :] = jnp.concatenate(pieces, axis=-1)
        return carry

    lax.fori_loop(0, n // cot_size, spread, 0)
    place = lax.broadcasted_iota(jnp.int32, (n, samples), 0)

    def fold(f, carry):
        along = pl.ds(pl.multiple_of(f * n, n), n)
        across = pl.ds(f, n, stride=n)
        row, column = w_ref[along, :], w_ref[across, :]
        both = row + column + jnp.where(place == f, POOL_DECAY, 0.0)
        w_ref[along, :] = jnp.where(place >= f, both, row)
        w_ref[across, :] = jnp.where(place >= f, both, column)
        return carry

    lax.fori_loop(0, n, fold, 0)
    for part in range(1, parts):
        own_slab(part, lambda copy: copy.start())
    total[...] = jnp.zeros_like(total)

    sublanes = 16
    place_of = lax.broadcasted_iota(jnp.int32, (BLOCK, samples), 0)
    place_of = place_of.astype(jnp.float32).astype(jnp.bfloat16)
    one = jnp.ones((sublanes, samples), jnp.bfloat16)
    none = jnp.zeros_like(one)

    def hits(micros):
        rows = jnp.concatenate([micros[i] for i in range(micros.shape[0])], axis=-1)
        block_of = (rows // BLOCK).astype(jnp.float32)
        offset_of = lax.rem(rows, BLOCK).astype(jnp.float32)

        def wide(values, lookup):
            row = jnp.broadcast_to(values[lookup : lookup + 1, :], (sublanes, samples))
            return row.astype(jnp.bfloat16)

        spans = [slice(at, at + sublanes) for at in range(0, BLOCK, sublanes)]
        offsets = [wide(offset_of, lookup) for lookup in range(bags)]
        same = [[jnp.where(offset == place_of[span], one, none) for span in spans] for offset in offsets]
        in_block = [wide(block_of, lookup) for lookup in range(bags)]
        pieces = []
        for block in range(slab_size // BLOCK):
            chosen = [row == jnp.full_like(row, block) for row in in_block]
            for at in range(len(spans)):
                terms = [jnp.where(chosen[k], same[k][at], none) for k in range(bags)]
                while len(terms) > 1:
                    terms = [sum(terms[k + 1 : k + 2], terms[k]) for k in range(0, len(terms), 2)]
                pieces.append(terms[0])
        return jnp.concatenate(pieces, axis=0)

    def pooled_copy(part, q, j, slot):
        return pltpu.make_async_remote_copy(
            pooled_out.at[units(part), q, j],
            pooled_in.at[units(part), q * m + slot],
            pooled_send.at[part],
            pooled_recv.at[part],
            **at(plane * m + j),
        )

    def grad_copy(part, peer, slot):
        return pltpu.make_async_remote_copy(
            grad_out.at[units(part), peer],
            grad_in.at[units(part), slot],
            grad_send.at[part],
            grad_last.at[slot] if part == parts - 1 else grad_recv.at[part, slot // m],
            **at(peer),
        )

    def member(at):
        return lax.rem(local + at, m)

    def pairs(body):
        def run(pair, carry):
            body(pair)
            return carry

        lax.fori_loop(0, m // 2, run, 0)

    def near_pair(q, pair):
        return [hits(near[member(2 * pair + k), :, q]) for k in (1, 2)]

    def pool(part, q):
        rows_of = slabs[q, units(part)].reshape(tall(part), slab_size)

        def both(pair):
            if keeps and part > 0:
                counted = kept[q, pair]
            else:
                counted = jnp.concatenate(near_pair(q, pair), axis=1)
                if keeps:
                    kept[q, pair] = counted
            summed = jnp.dot(rows_of, counted, preferred_element_type=jnp.float32)
            summed = summed.astype(jnp.bfloat16).reshape(-1, columns, 2 * samples)
            first, second = member(2 * pair + 1), member(2 * pair + 2)
            pooled_out[units(part), q, first] = summed[:, :, :samples]
            pooled_copy(part, q, first, local).start()
            pooled_out[units(part), q, second] = summed[:, :, samples:]

            @pl.when(2 * pair + 2 < m)
            def _():
                pooled_copy(part, q, second, local).start()

        pairs(both)
        pooled_in[units(part), q * m + local] = pooled_out[units(part), q, local]

    def relay(part, step):
        q = nearest(step)
        slab_copy(part, q, 1, up).wait_recv()
        passed_slab(part, q, lambda copy: copy.start())
        half_copy(part, q, rep).start()

    def pool_from(part, step):
        q = nearest(step)
        half_copy(part, q, 1 - rep).wait_recv()
        pool(part, q)

    def batch(ref, send_sem, recv_sem):
        return pltpu.make_async_remote_copy(ref, ref, send_sem, recv_sem, **partner)

    def arrive(part):
        arrived = pooled_in.at[units(part), pl.ds(0, planes * (m - 1))]
        batch(arrived, pooled_send.at[part], pooled_recv.at[part]).wait_recv()
        widen(part)

    def widen(part):
        if wide.shape[0] == n:

            def run(other, carry):
                seen = pooled_in[units(part), other].reshape(tall(part), samples)
                wide[other, : tall(part)] = seen.astype(jnp.float32)
                return carry

            lax.fori_loop(0, n, run, 0, unroll=4)

    def interact(part, first=True, rest=True):
        def mixed(feature):
            def add(other, carry):
                weight = w_ref[pl.ds(feature * n + other, 1), :]
                if wide.shape[0] == n:
                    return carry + weight * wide[other, : tall(part)]
                seen = pooled_in[units(part), other].reshape(tall(part), samples)
                return carry + weight * seen.astype(jnp.float32)

            start = jnp.zeros((tall(part), samples), jnp.float32)
            mix = lax.fori_loop(0, n, add, start, unroll=UNROLL)
            return mix.astype(jnp.bfloat16).reshape(-1, columns, samples)

        def send(peer):
            grad_out[units(part), peer] = mixed(peer)
            grad_copy(part, peer, me).start()

        for step in range(planes - 1, 0, -1):
            if first if step > 1 else rest:
                q = nearest(step)
                each(0, lambda j: send(q * m + j))
        if rest:
            each(1, lambda j: send(plane * m + j))
            grad_in[units(part), me] = mixed(me)

    def far_pair(q, pair):
        counted = [hits(far[q * m + member(2 * pair + k)]) for k in (0, 1)]
        return jnp.concatenate(counted, axis=1)

    def keep_far():
        for step in range(1, planes):
            q = nearest(step)

            def take(pair):
                kept_own[q, pair] = far_pair(q, pair)

            if keeps:
                pairs(take)

    def collect(which):
        first_unit, count, members = HALVES[which]

        def add(first, second, counted):
            grads = [grad_in[pl.ds(first_unit, count), peer] for peer in (first, second)]
            grads = [piece.reshape(count * columns, samples) for piece in grads]
            total[which] += lax.dot_general(
                counted,
                jnp.concatenate(grads, axis=1),
                (((1,), (1,)), ((), ())),
                preferred_element_type=jnp.float32,
            )

        def plane_ready(q, blocks):
            for part in members:
                if part < parts - 1:
                    arrived = grad_in.at[units(part), pl.ds(0, blocks)]
                    batch(arrived, grad_send.at[part], grad_recv.at[part, q]).wait_recv()

        def ready(peer):
            if parts - 1 in members:
                grad_copy(parts - 1, peer, peer).wait_recv()

        def take_near(pair):
            first, second = (plane * m + member(2 * pair + k) for k in (1, 2))
            ready(first)
            pl.when(2 * pair + 2 < m)(lambda: ready(second))
            if keeps:
                add(first, second, kept[plane, pair])
            else:
                add(first, second, jnp.concatenate(near_pair(plane, pair), axis=1))

        def take_far(q, pair):
            first, second = (q * m + member(2 * pair + k) for k in (0, 1))
            ready(first)
            ready(second)
            add(first, second, kept_own[q, pair] if keeps else far_pair(q, pair))

        plane_ready(plane, m - 1)
        pairs(take_near)
        for step in range(1, planes):
            q = jnp.where(inner, nearest(step % (planes - 1) + 1), nearest(step))
            plane_ready(q, m)
            pairs(lambda pair: take_far(q, pair))

    batch(near.at[pl.ds(0, m - 1)], near_send, near_recv).wait_recv()
    pool(0, plane)
    relay(0, 1)

    @pl.when(inner)
    def _():
        relay(0, 2)
        pool(1, plane)
        relay(1, 1)
        relay(1, 2)
        pool_from(0, 1)
        pool_from(0, 2)
        relay(0, 3)
        relay(2, 1)
        relay(2, 2)
        pool_from(1, 1)
        relay(1, 3)
        pool_from(0, 3)
        pool_from(1, 2)
        pool_from(1, 3)
        pool(2, plane)
        relay(2, 3)
        arrive(0)
        interact(0)
        pool_from(2, 1)
        arrive(1)
        interact(1)
        pool_from(2, 2)
        pool_from(2, 3)

    @pl.when(outer)
    def _():
        pool(1, plane)
        relay(1, 1)
        pool_from(0, 1)
        relay(2, 1)
        pool_from(1, 1)
        relay(0, 2)
        relay(1, 2)
        pool_from(0, 2)
        pool_from(1, 2)
        pool(2, plane)
        relay(0, 3)
        relay(2, 2)
        relay(1, 3)
        pool_from(0, 3)
        pool_from(1, 3)
        pool_from(2, 1)
        pool_from(2, 2)
        arrive(0)
        interact(0)
        relay(2, 3)
        pool_from(2, 3)
        arrive(1)
        interact(1)

    arrive(2)
    interact(2)
    batch(far.at[pl.ds(0, n - m)], far_send, far_recv).wait_recv()
    keep_far()
    state_copy.wait()
    pieces = []
    for block in range(touch_count):
        at_block = touched_ref[0, block]
        pair = state_ref[pl.ds(at_block // 2, 1), :]
        pieces.append(jnp.where(lax.rem(at_block, 2) == 0, pair[:, :BLOCK], pair[:, BLOCK:]))
    state_row = jnp.concatenate(pieces, axis=1)
    state_col[...] = jnp.broadcast_to(state_row, (state_col.shape[1], slab_size)).T
    chunk = touch_count // CHUNKS * BLOCK

    def total_copy(which, at):
        span = pl.ds(at * chunk, chunk)
        return pltpu.make_async_remote_copy(
            total.at[which, span],
            total_in.at[which, span],
            pair_sem.at[0, which, at],
            pair_sem.at[1, which, at],
            **partner,
        )

    collect(0)
    for at_chunk in range(CHUNKS):
        total_copy(0, at_chunk).start()
    batch(near.at[pl.ds(0, m - 1)], near_send, near_recv).wait_send()
    batch(far.at[pl.ds(0, n - m)], far_send, far_recv).wait_send()
    batch(slabs.at[pl.ds(0, planes - 1), :, 0], half_send, half_recv.at[0, 0]).wait_send()
    any_slab = slab_recv.at[0, 0]

    @pl.when(inner)
    def _():
        batch(slabs.at[pl.ds(0, 2), :, 0], slab_send.at[0], any_slab).wait_send()
        batch(slabs.at[pl.ds(0, planes - 1), :, 0], slab_send.at[1], any_slab).wait_send()

    @pl.when(outer)
    def _():
        batch(slabs.at[0, :, 0], slab_send.at[0], any_slab).wait_send()

    for part in range(parts):
        sent = pooled_out.at[units(part), :, pl.ds(0, m - 1)]
        batch(sent, pooled_send.at[part], pooled_recv.at[part]).wait_send()

    def grads_sent(part):
        sent = grad_out.at[units(part), pl.ds(0, n - 1)]
        batch(sent, grad_send.at[part], grad_last.at[0]).wait_send()

    grads_sent(0)
    grads_sent(1)
    dither_copy.wait()
    collect(1)
    for at_chunk in range(CHUNKS):
        total_copy(1, at_chunk).start()
    grads_sent(2)
    def update(block, carry):
        at_rows = pl.ds(pl.multiple_of(block * BLOCK, BLOCK), BLOCK)
        grad = [total[h, at_rows, :] + total_in[h, at_rows, :] for h in range(len(HALVES))]
        grad = jnp.concatenate(grad, axis=1)
        state_next = state_col[at_rows, :] + jnp.sum(grad * grad, axis=1, keepdims=True) / width
        state_col[at_rows, :] = state_next
        rate = LEARN_RATE / (jnp.sqrt(state_next) + 1e-08)
        rate = jnp.concatenate([rate] * (width // rate.shape[1]), axis=1)
        moved = slab[at_rows, :].astype(jnp.float32) - grad * rate
        table_in[table_blocks + block] = dither_round(moved, dither_in[at_rows, :])
        return carry

    per_chunk = touch_count // CHUNKS
    for at_chunk in range(CHUNKS):
        for which in range(len(HALVES)):
            total_copy(which, at_chunk).wait_recv()
        lax.fori_loop(at_chunk * per_chunk, (at_chunk + 1) * per_chunk, update, 0, unroll=True)
    state_all = state_ref[...]
    block_at = 2 * lax.broadcasted_iota(jnp.int32, state_all.shape, 0)
    block_at = block_at + lax.broadcasted_iota(jnp.int32, state_all.shape, 1) // BLOCK
    state_row = state_col[...].T[:1, :]
    for block in range(touch_count):
        piece = state_row[:, block * BLOCK : (block + 1) * BLOCK]
        piece = jnp.broadcast_to(jnp.concatenate([piece, piece], axis=1), state_all.shape)
        state_all = jnp.where(block_at == touched_ref[0, block], piece, state_all)
    state_out_ref[...] = state_all
    for which in range(len(HALVES)):
        for at_chunk in range(CHUNKS):
            total_copy(which, at_chunk).wait_send()


def fused_step(n, blocks, offsets, cot, touched, state, table, dither):
    micros, planes, m = blocks.shape[0], blocks.shape[1], blocks.shape[2]
    sample_count = blocks.shape[-1]
    samples = micros * sample_count
    cot_size = math.gcd(n, 16)
    slab_size, width = dither.shape
    columns, parts = width // UNITS, len(PARTS)
    keeps = 2 * n * slab_size * samples <= KEEP_BYTES
    held = (planes, m // 2) if keeps else (1, 1)
    dma = pltpu.SemaphoreType.DMA
    block = (UNITS, n, columns, samples)
    vmem = pl.BlockSpec(memory_space=pltpu.VMEM)
    smem = pl.BlockSpec(memory_space=pltpu.SMEM)
    hbm = pl.BlockSpec(memory_space=pltpu.HBM)
    return pl.pallas_call(
        functools.partial(step_kernel, n),
        out_shape=(
            pltpu.VMEM(state.shape, jnp.float32),
            pltpu.VMEM((table.shape[0] + slab_size // BLOCK,) + table.shape[1:], jnp.bfloat16),
        ),
        in_specs=[hbm, hbm, hbm, smem, hbm, hbm, hbm],
        out_specs=(vmem, vmem),
        scratch_shapes=[
            pltpu.VMEM(blocks.shape, jnp.int32),
            pltpu.VMEM(blocks.shape, jnp.int32),
            pltpu.VMEM(state.shape, jnp.float32),
            pltpu.VMEM(blocks.shape, jnp.int32),
            pltpu.VMEM((micros, cot_size, n, sample_count), jnp.bfloat16),
            pltpu.VMEM((m, micros, planes) + blocks.shape[3:], jnp.int32),
            pltpu.VMEM((n, micros) + blocks.shape[3:], jnp.int32),
            pltpu.VMEM((n * n, samples), jnp.float32),
            pltpu.VMEM((slab_size, width), jnp.int32),
            pltpu.VMEM((slab_size, width), jnp.bfloat16),
            pltpu.VMEM((planes, UNITS, 2, columns // 2, slab_size), jnp.bfloat16),
            pltpu.VMEM((UNITS, planes, m, columns, samples), jnp.bfloat16),
            pltpu.VMEM(block, jnp.bfloat16),
            pltpu.VMEM((n if keeps else 1, 2 * columns, samples), jnp.float32),
            pltpu.VMEM(block, jnp.bfloat16),
            pltpu.VMEM(block, jnp.bfloat16),
            pltpu.VMEM(held + (slab_size, 2 * samples), jnp.bfloat16),
            pltpu.VMEM(held + (slab_size, 2 * samples), jnp.bfloat16),
            pltpu.VMEM((len(HALVES), slab_size, width // len(HALVES)), jnp.float32),
            pltpu.VMEM((len(HALVES), slab_size, width // len(HALVES)), jnp.float32),
            pltpu.VMEM((slab_size, 128), jnp.float32),
            dma((6,)),
            dma((2, len(HALVES), CHUNKS)),
            dma(()),
            dma(()),
            dma(()),
            dma(()),
            dma((2,)),
            dma((parts, planes)),
            dma(()),
            dma((parts, planes)),
            dma((parts,)),
            dma((parts,)),
            dma((parts,)),
            dma((parts - 1, planes)),
            dma((n,)),
        ],
        compiler_params=pltpu.CompilerParams(collective_id=0, has_side_effects=True),
        name="fused_step",
    )(blocks, offsets, cot, touched, state, table, dither)


def write_kernel(touched_ref, state_ref, blocks_ref, out_ref, state_out_ref, place, sem):
    state_copy = pltpu.make_async_copy(state_ref, state_out_ref, sem.at[1])
    state_copy.start()
    blocks, touch_count = out_ref.shape[0], touched_ref.shape[1]
    for block in range(blocks):
        place[block] = block
    for i in range(touch_count):
        place[touched_ref[0, i]] = blocks + i
    for block in range(blocks):
        source = blocks_ref.at[place[block]]
        pltpu.make_async_copy(source, out_ref.at[block], sem.at[0]).start()
    pltpu.make_async_copy(blocks_ref.at[pl.ds(0, blocks)], out_ref, sem.at[0]).wait()
    state_copy.wait()


def write_table(touched, state, blocks, table):
    vmem = pl.BlockSpec(memory_space=pltpu.VMEM)
    hbm = pl.BlockSpec(memory_space=pltpu.HBM)
    held = [pltpu.with_memory_space_constraint(x, pltpu.VMEM) for x in (state, blocks)]
    return pl.pallas_call(
        write_kernel,
        out_shape=(
            jax.ShapeDtypeStruct(table.shape, table.dtype),
            jax.ShapeDtypeStruct(state.shape, state.dtype),
        ),
        in_specs=[pl.BlockSpec(memory_space=pltpu.SMEM), vmem, vmem],
        out_specs=(hbm, hbm),
        scratch_shapes=[pltpu.SMEM((table.shape[0],), jnp.int32), pltpu.SemaphoreType.DMA((2,))],
        compiler_params=pltpu.CompilerParams(vmem_limit_bytes=4 << 20),
        name="write_table",
    )(touched, *held)


def per_device(
    lookup_block, lookup_offset, interaction_grad, table, adagrad_state, touched_blocks, dither
):
    micro_count, sample_count, feature_count, bag_count = lookup_block.shape
    n = lax.axis_size("mp")
    row_count, emb_width = table.shape
    split = (micro_count, PLANES, feature_count // PLANES, bag_count, sample_count)
    blocks = lookup_block.transpose(0, 2, 3, 1).reshape(split)
    offsets = lookup_offset.transpose(0, 2, 3, 1).reshape(split)
    cot = interaction_grad.transpose(0, 2, 3, 1)
    table_blocks = table.reshape(row_count // BLOCK, BLOCK, emb_width)
    state = adagrad_state.reshape(row_count // (2 * BLOCK), 2 * BLOCK)
    new_state, held_blocks = fused_step(
        n, blocks, offsets, cot, touched_blocks, state, table_blocks, dither[0]
    )
    new_table, new_state = write_table(touched_blocks, new_state, held_blocks, table_blocks)
    return (new_table.reshape(row_count, emb_width), new_state.reshape(row_count))


def solution(mesh):
    return jax.shard_map(
        per_device,
        mesh=mesh,
        in_specs=(
            P(None, ("rep", "mp"), None, None),
            P(None, ("rep", "mp"), None, None),
            P(None, ("rep", "mp"), None, None),
            P("mp", None),
            P("mp"),
            P("mp", None),
            P("mp", None, None),
        ),
        out_specs=(P("mp", None), P("mp")),
        check_vma=False,
    )
```

```python
import functools
import math

import jax
import jax.numpy as jnp
from jax import lax
from jax.experimental import pallas as pl
from jax.experimental.pallas import tpu as pltpu
from jax.sharding import PartitionSpec as P

BLOCK = 64
PLANES = 4
UNITS = 4
UNROLL = 4
CHUNKS = 2
PARTS = ((0, 1), (1, 1), (2, 2))
HALVES = ((0, 2, (0, 1)), (2, 2, (2,)))
LEARN_RATE = 0.1
POOL_DECAY = 0.5
DITHER_UNIT = 2.0 ** (-15)
SMALLEST = 2.0 ** (-14)
KEEP_BYTES = 8 << 20
MESH = pl.DeviceIdType.MESH


def dither_round(weights, dither_bits):
    magnitude = jnp.maximum(jnp.abs(weights), SMALLEST)
    exponent = jnp.floor(jnp.log2(magnitude)) - 7.0
    spacing, per_spacing = jnp.exp2(exponent), jnp.exp2(-exponent)
    grid_level = jnp.floor(weights * per_spacing + dither_bits.astype(jnp.float32) * DITHER_UNIT)
    return (grid_level * spacing).astype(jnp.bfloat16)


def plane_order(planes, plane, step):
    picked = jnp.int32(0)
    for own in range(planes):
        near_first = sorted(range(planes), key=lambda q: (abs(q - own), (q - own) * (2 * own - planes)))
        picked = jnp.where(plane == own, near_first[step], picked)
    return picked


def step_kernel(
    n,
    block_hbm,
    offset_hbm,
    cot_ref,
    touched_ref,
    state_hbm,
    table_ref,
    dither_ref,
    state_out_ref,
    table_in,
    block_ref,
    offset_ref,
    state_ref,
    rows_ref,
    cot_in,
    near,
    far,
    w_ref,
    dither_in,
    slab,
    slabs,
    pooled_out,
    pooled_in,
    wide,
    grad_out,
    grad_in,
    kept,
    kept_own,
    total,
    total_in,
    state_col,
    local_sem,
    pair_sem,
    near_send,
    near_recv,
    far_send,
    far_recv,
    slab_send,
    slab_recv,
    half_send,
    half_recv,
    pooled_send,
    pooled_recv,
    grad_send,
    grad_recv,
    grad_last,
):
    me = lax.axis_index("mp")
    rep = lax.axis_index("rep")
    planes, parts = slabs.shape[0], len(PARTS)
    m = n // planes
    plane = me // m
    local = lax.rem(me, m)
    samples = w_ref.shape[1]
    bags = rows_ref.shape[3]
    slab_size, width = slab.shape
    columns = width // UNITS
    touch_count = slab_size // BLOCK
    keeps = kept.shape[0] == planes

    def at(peer):
        return {"device_id": (rep, peer), "device_id_type": MESH}

    partner = {"device_id": (1 - rep, me), "device_id_type": MESH}

    def each(first, body):
        def run(step, carry):
            body(lax.rem(local + step, m))
            return carry

        lax.fori_loop(first, m, run, 0)

    def others(body):
        def run(step, carry):
            body(lax.rem(me + step, n))
            return carry

        lax.fori_loop(1, n, run, 0)

    def outside(body, first=0, last=n - m):
        def run(step, carry):
            body(lax.rem(plane + 1 + step // m, planes), lax.rem(local + step, m))
            return carry

        lax.fori_loop(first, last, run, 0)

    def nearest(step):
        return plane_order(planes, plane, step)

    def units(part):
        first, count = PARTS[part]
        return pl.ds(first, count)

    def tall(part):
        return PARTS[part][1] * columns

    barrier = pltpu.get_barrier_semaphore()
    others(lambda peer: pl.semaphore_signal(barrier, inc=1, **at(peer)))
    pl.semaphore_signal(barrier, inc=1, **partner)
    table_blocks = table_ref.shape[0]
    held_table = table_in.at[pl.ds(0, table_blocks)]
    table_copy = pltpu.make_async_copy(table_ref, held_table, local_sem.at[0])
    table_copy.start()
    block_copy = pltpu.make_async_copy(block_hbm, block_ref, local_sem.at[1])
    block_copy.start()
    offset_copy = pltpu.make_async_copy(offset_hbm, offset_ref, local_sem.at[2])
    offset_copy.start()
    state_copy = pltpu.make_async_copy(state_hbm, state_ref, local_sem.at[3])
    state_copy.start()
    dither_copy = pltpu.make_async_copy(dither_ref, dither_in, local_sem.at[4])
    dither_copy.start()
    block_copy.wait()
    offset_copy.wait()
    rows_ref[...] = block_ref[...] * BLOCK + offset_ref[...]
    near[local] = rows_ref[:, :, local]
    table_copy.wait()
    for block in range(touch_count):
        slab[block * BLOCK : (block + 1) * BLOCK, :] = table_in[touched_ref[0, block]]
    turned = slab[...].astype(jnp.float32).T.astype(jnp.bfloat16)
    slabs[plane] = turned.reshape(slabs.shape[1:])
    pl.semaphore_wait(barrier, n)

    def near_copy(j, slot):
        return pltpu.make_async_remote_copy(
            rows_ref.at[:, :, j],
            near.at[slot],
            near_send,
            near_recv,
            **at(plane * m + j),
        )

    def far_copy(q, j, slot):
        return pltpu.make_async_remote_copy(
            rows_ref.at[:, q, j],
            far.at[slot],
            far_send,
            far_recv,
            **at(q * m + j),
        )

    def slab_copy(part, q, slot, peer):
        return pltpu.make_async_remote_copy(
            slabs.at[q, units(part), rep],
            slabs.at[q, units(part), rep],
            slab_send.at[slot],
            slab_recv.at[part, q],
            **at(peer),
        )

    def half_copy(part, q, which):
        return pltpu.make_async_remote_copy(
            slabs.at[q, units(part), which],
            slabs.at[q, units(part), which],
            half_send,
            half_recv.at[part, q],
            **partner,
        )

    has_up, has_down = plane + 1 < planes, plane > 0
    inner = jnp.logical_and(has_up, has_down)
    outer = jnp.logical_not(inner)
    up, down = lax.rem(me + m, n), lax.rem(me + n - m, n)

    def own_slab(part, act):
        @pl.when(has_up)
        def _():
            act(slab_copy(part, plane, 0, up))

        @pl.when(has_down)
        def _():
            act(slab_copy(part, plane, 0, down))

    def passed_slab(part, q, act):
        @pl.when(jnp.logical_and(q < plane, has_up))
        def _():
            act(slab_copy(part, q, 1, up))

        @pl.when(jnp.logical_and(q > plane, has_down))
        def _():
            act(slab_copy(part, q, 1, down))

    each(1, lambda j: near_copy(j, local).start())
    own_slab(0, lambda copy: copy.start())
    outside(lambda q, j: far_copy(q, j, me).start())
    cot_size = cot_in.shape[1]

    def spread(chunk, carry):
        cot_copy = pltpu.make_async_copy(
            cot_ref.at[:, pl.ds(chunk * cot_size, cot_size)], cot_in, local_sem.at[5]
        )
        cot_copy.start()
        cot_copy.wait()
        for i in range(cot_size):
            pieces = [cot_in[micro, i].astype(jnp.float32) for micro in range(cot_in.shape[0])]
            at_row = pl.multiple_of((chunk * cot_size + i) * n, n)
            w_ref[pl.ds(at_row, n), :] = jnp.concatenate(pieces, axis=-1)
        return carry

    lax.fori_loop(0, n // cot_size, spread, 0)
    place = lax.broadcasted_iota(jnp.int32, (n, samples), 0)

    def fold(f, carry):
        along = pl.ds(pl.multiple_of(f * n, n), n)
        across = pl.ds(f, n, stride=n)
        row, column = w_ref[along, :], w_ref[across, :]
        both = row + column + jnp.where(place == f, POOL_DECAY, 0.0)
        w_ref[along, :] = jnp.where(place >= f, both, row)
        w_ref[across, :] = jnp.where(place >= f, both, column)
        return carry

    lax.fori_loop(0, n, fold, 0)
    for part in range(1, parts):
        own_slab(part, lambda copy: copy.start())
    total[...] = jnp.zeros_like(total)

    sublanes = 16
    place_of = lax.broadcasted_iota(jnp.int32, (BLOCK, samples), 0)
    place_of = place_of.astype(jnp.float32).astype(jnp.bfloat16)
    one = jnp.ones((sublanes, samples), jnp.bfloat16)
    none = jnp.zeros_like(one)

    def hits(micros):
        rows = jnp.concatenate([micros[i] for i in range(micros.shape[0])], axis=-1)
        block_of = (rows // BLOCK).astype(jnp.float32)
        offset_of = lax.rem(rows, BLOCK).astype(jnp.float32)

        def wide(values, lookup):
            row = jnp.broadcast_to(values[lookup : lookup + 1, :], (sublanes, samples))
            return row.astype(jnp.bfloat16)

        spans = [slice(at, at + sublanes) for at in range(0, BLOCK, sublanes)]
        offsets = [wide(offset_of, lookup) for lookup in range(bags)]
        same = [[jnp.where(offset == place_of[span], one, none) for span in spans] for offset in offsets]
        in_block = [wide(block_of, lookup) for lookup in range(bags)]
        pieces = []
        for block in range(slab_size // BLOCK):
            chosen = [row == jnp.full_like(row, block) for row in in_block]
            for at in range(len(spans)):
                terms = [jnp.where(chosen[k], same[k][at], none) for k in range(bags)]
                while len(terms) > 1:
                    terms = [sum(terms[k + 1 : k + 2], terms[k]) for k in range(0, len(terms), 2)]
                pieces.append(terms[0])
        return jnp.concatenate(pieces, axis=0)

    def pooled_copy(part, q, j, slot):
        return pltpu.make_async_remote_copy(
            pooled_out.at[units(part), q, j],
            pooled_in.at[units(part), q * m + slot],
            pooled_send.at[part],
            pooled_recv.at[part],
            **at(plane * m + j),
        )

    def grad_copy(part, peer, slot):
        return pltpu.make_async_remote_copy(
            grad_out.at[units(part), peer],
            grad_in.at[units(part), slot],
            grad_send.at[part],
            grad_last.at[slot] if part == parts - 1 else grad_recv.at[part, slot // m],
            **at(peer),
        )

    def member(at):
        return lax.rem(local + at, m)

    def pairs(body):
        def run(pair, carry):
            body(pair)
            return carry

        lax.fori_loop(0, m // 2, run, 0)

    def near_pair(q, pair):
        return [hits(near[member(2 * pair + k), :, q]) for k in (1, 2)]

    def pool(part, q):
        rows_of = slabs[q, units(part)].reshape(tall(part), slab_size)

        def both(pair):
            if keeps and part > 0:
                counted = kept[q, pair]
            else:
                counted = jnp.concatenate(near_pair(q, pair), axis=1)
                if keeps:
                    kept[q, pair] = counted
            summed = jnp.dot(rows_of, counted, preferred_element_type=jnp.float32)
            summed = summed.astype(jnp.bfloat16).reshape(-1, columns, 2 * samples)
            first, second = member(2 * pair + 1), member(2 * pair + 2)
            pooled_out[units(part), q, first] = summed[:, :, :samples]
            pooled_copy(part, q, first, local).start()
            pooled_out[units(part), q, second] = summed[:, :, samples:]

            @pl.when(2 * pair + 2 < m)
            def _():
                pooled_copy(part, q, second, local).start()

        pairs(both)
        pooled_in[units(part), q * m + local] = pooled_out[units(part), q, local]

    def relay(part, step):
        q = nearest(step)
        slab_copy(part, q, 1, up).wait_recv()
        passed_slab(part, q, lambda copy: copy.start())
        half_copy(part, q, rep).start()

    def pool_from(part, step):
        q = nearest(step)
        half_copy(part, q, 1 - rep).wait_recv()
        pool(part, q)

    def batch(ref, send_sem, recv_sem):
        return pltpu.make_async_remote_copy(ref, ref, send_sem, recv_sem, **partner)

    def arrive(part):
        arrived = pooled_in.at[units(part), pl.ds(0, planes * (m - 1))]
        batch(arrived, pooled_send.at[part], pooled_recv.at[part]).wait_recv()
        widen(part)

    def wide_rows(part):
        start = PARTS[part][0] * columns % wide.shape[1]
        return slice(start, start + tall(part))

    def widen(part):
        if wide.shape[0] == n:

            def run(other, carry):
                seen = pooled_in[units(part), other].reshape(tall(part), samples)
                wide[other, wide_rows(part)] = seen.astype(jnp.float32)
                return carry

            lax.fori_loop(0, n, run, 0, unroll=4)

    def interact(part, first=True, rest=True):
        def mixed(feature):
            def add(other, carry):
                weight = w_ref[pl.ds(feature * n + other, 1), :]
                if wide.shape[0] == n:
                    return carry + weight * wide[other, wide_rows(part)]
                seen = pooled_in[units(part), other].reshape(tall(part), samples)
                return carry + weight * seen.astype(jnp.float32)

            start = jnp.zeros((tall(part), samples), jnp.float32)
            mix = lax.fori_loop(0, n, add, start, unroll=UNROLL)
            return mix.astype(jnp.bfloat16).reshape(-1, columns, samples)

        def send(peer):
            grad_out[units(part), peer] = mixed(peer)
            grad_copy(part, peer, me).start()

        for step in range(planes - 1, 0, -1):
            if first if step > 1 else rest:
                q = nearest(step)
                each(0, lambda j: send(q * m + j))
        if rest:
            each(1, lambda j: send(plane * m + j))
            grad_in[units(part), me] = mixed(me)

    def far_pair(q, pair):
        counted = [hits(far[q * m + member(2 * pair + k)]) for k in (0, 1)]
        return jnp.concatenate(counted, axis=1)

    def keep_far():
        for step in range(1, planes):
            q = nearest(step)

            def take(pair):
                kept_own[q, pair] = far_pair(q, pair)

            if keeps:
                pairs(take)

    def collect(which):
        first_unit, count, members = HALVES[which]

        def add(first, second, counted):
            grads = [grad_in[pl.ds(first_unit, count), peer] for peer in (first, second)]
            grads = [piece.reshape(count * columns, samples) for piece in grads]
            total[which] += lax.dot_general(
                counted,
                jnp.concatenate(grads, axis=1),
                (((1,), (1,)), ((), ())),
                preferred_element_type=jnp.float32,
            )

        def plane_ready(q, blocks):
            for part in members:
                if part < parts - 1:
                    arrived = grad_in.at[units(part), pl.ds(0, blocks)]
                    batch(arrived, grad_send.at[part], grad_recv.at[part, q]).wait_recv()

        def ready(peer):
            if parts - 1 in members:
                grad_copy(parts - 1, peer, peer).wait_recv()

        def take_near(pair):
            first, second = (plane * m + member(2 * pair + k) for k in (1, 2))
            ready(first)
            pl.when(2 * pair + 2 < m)(lambda: ready(second))
            if keeps:
                add(first, second, kept[plane, pair])
            else:
                add(first, second, jnp.concatenate(near_pair(plane, pair), axis=1))

        def take_far(q, pair):
            first, second = (q * m + member(2 * pair + k) for k in (0, 1))
            ready(first)
            ready(second)
            add(first, second, kept_own[q, pair] if keeps else far_pair(q, pair))

        plane_ready(plane, m - 1)
        pairs(take_near)
        for step in range(1, planes):
            q = jnp.where(inner, nearest(step % (planes - 1) + 1), nearest(step))
            plane_ready(q, m)
            pairs(lambda pair: take_far(q, pair))

    batch(near.at[pl.ds(0, m - 1)], near_send, near_recv).wait_recv()
    pool(0, plane)
    relay(0, 1)

    @pl.when(inner)
    def _():
        relay(0, 2)
        pool(1, plane)
        relay(1, 1)
        relay(1, 2)
        pool_from(0, 1)
        pool_from(0, 2)
        relay(0, 3)
        relay(2, 1)
        relay(2, 2)
        pool_from(1, 1)
        relay(1, 3)
        pool_from(0, 3)
        pool_from(1, 2)
        pool_from(1, 3)
        pool(2, plane)
        relay(2, 3)
        arrive(0)
        interact(0)
        pool_from(2, 1)
        arrive(1)
        interact(1)
        pool_from(2, 2)
        pool_from(2, 3)

    @pl.when(outer)
    def _():
        pool(1, plane)
        relay(1, 1)
        pool_from(0, 1)
        relay(2, 1)
        pool_from(1, 1)
        relay(0, 2)
        relay(1, 2)
        pool_from(0, 2)
        pool_from(1, 2)
        pool(2, plane)
        relay(0, 3)
        relay(2, 2)
        relay(1, 3)
        pool_from(0, 3)
        pool_from(1, 3)
        pool_from(2, 1)
        pool_from(2, 2)
        arrive(0)
        interact(0, rest=False)
        relay(2, 3)
        pool_from(2, 3)
        arrive(1)
        interact(1, rest=False)
        interact(0, first=False)
        interact(1, first=False)

    arrive(2)
    interact(2)
    batch(far.at[pl.ds(0, n - m)], far_send, far_recv).wait_recv()
    keep_far()
    state_copy.wait()
    pieces = []
    for block in range(touch_count):
        at_block = touched_ref[0, block]
        pair = state_ref[pl.ds(at_block // 2, 1), :]
        pieces.append(jnp.where(lax.rem(at_block, 2) == 0, pair[:, :BLOCK], pair[:, BLOCK:]))
    state_row = jnp.concatenate(pieces, axis=1)
    state_col[...] = jnp.broadcast_to(state_row, (state_col.shape[1], slab_size)).T
    chunk = touch_count // CHUNKS * BLOCK

    def total_copy(which, at):
        span = pl.ds(at * chunk, chunk)
        return pltpu.make_async_remote_copy(
            total.at[which, span],
            total_in.at[which, span],
            pair_sem.at[0, which, at],
            pair_sem.at[1, which, at],
            **partner,
        )

    collect(0)
    for at_chunk in range(CHUNKS):
        total_copy(0, at_chunk).start()
    batch(near.at[pl.ds(0, m - 1)], near_send, near_recv).wait_send()
    batch(far.at[pl.ds(0, n - m)], far_send, far_recv).wait_send()
    batch(slabs.at[pl.ds(0, planes - 1), :, 0], half_send, half_recv.at[0, 0]).wait_send()
    any_slab = slab_recv.at[0, 0]

    @pl.when(inner)
    def _():
        batch(slabs.at[pl.ds(0, 2), :, 0], slab_send.at[0], any_slab).wait_send()
        batch(slabs.at[pl.ds(0, planes - 1), :, 0], slab_send.at[1], any_slab).wait_send()

    @pl.when(outer)
    def _():
        batch(slabs.at[0, :, 0], slab_send.at[0], any_slab).wait_send()

    for part in range(parts):
        sent = pooled_out.at[units(part), :, pl.ds(0, m - 1)]
        batch(sent, pooled_send.at[part], pooled_recv.at[part]).wait_send()

    def grads_sent(part):
        sent = grad_out.at[units(part), pl.ds(0, n - 1)]
        batch(sent, grad_send.at[part], grad_last.at[0]).wait_send()

    grads_sent(0)
    grads_sent(1)
    dither_copy.wait()
    collect(1)
    for at_chunk in range(CHUNKS):
        total_copy(1, at_chunk).start()
    grads_sent(2)
    def update(block, carry):
        at_rows = pl.ds(pl.multiple_of(block * BLOCK, BLOCK), BLOCK)
        grad = [total[h, at_rows, :] + total_in[h, at_rows, :] for h in range(len(HALVES))]
        grad = jnp.concatenate(grad, axis=1)
        state_next = state_col[at_rows, :] + jnp.sum(grad * grad, axis=1, keepdims=True) / width
        state_col[at_rows, :] = state_next
        rate = LEARN_RATE / (jnp.sqrt(state_next) + 1e-08)
        rate = jnp.concatenate([rate] * (width // rate.shape[1]), axis=1)
        moved = slab[at_rows, :].astype(jnp.float32) - grad * rate
        table_in[table_blocks + block] = dither_round(moved, dither_in[at_rows, :])
        return carry

    per_chunk = touch_count // CHUNKS
    for at_chunk in range(CHUNKS):
        for which in range(len(HALVES)):
            total_copy(which, at_chunk).wait_recv()
        lax.fori_loop(at_chunk * per_chunk, (at_chunk + 1) * per_chunk, update, 0, unroll=True)
    state_all = state_ref[...]
    block_at = 2 * lax.broadcasted_iota(jnp.int32, state_all.shape, 0)
    block_at = block_at + lax.broadcasted_iota(jnp.int32, state_all.shape, 1) // BLOCK
    state_row = state_col[...].T[:1, :]
    for block in range(touch_count):
        piece = state_row[:, block * BLOCK : (block + 1) * BLOCK]
        piece = jnp.broadcast_to(jnp.concatenate([piece, piece], axis=1), state_all.shape)
        state_all = jnp.where(block_at == touched_ref[0, block], piece, state_all)
    state_out_ref[...] = state_all
    for which in range(len(HALVES)):
        for at_chunk in range(CHUNKS):
            total_copy(which, at_chunk).wait_send()


def fused_step(n, blocks, offsets, cot, touched, state, table, dither):
    micros, planes, m = blocks.shape[0], blocks.shape[1], blocks.shape[2]
    sample_count = blocks.shape[-1]
    samples = micros * sample_count
    cot_size = math.gcd(n, 16)
    slab_size, width = dither.shape
    columns, parts = width // UNITS, len(PARTS)
    keeps = 2 * n * slab_size * samples <= KEEP_BYTES
    held = (planes, m // 2) if keeps else (1, 1)
    dma = pltpu.SemaphoreType.DMA
    block = (UNITS, n, columns, samples)
    vmem = pl.BlockSpec(memory_space=pltpu.VMEM)
    smem = pl.BlockSpec(memory_space=pltpu.SMEM)
    hbm = pl.BlockSpec(memory_space=pltpu.HBM)
    return pl.pallas_call(
        functools.partial(step_kernel, n),
        out_shape=(
            pltpu.VMEM(state.shape, jnp.float32),
            pltpu.VMEM((table.shape[0] + slab_size // BLOCK,) + table.shape[1:], jnp.bfloat16),
        ),
        in_specs=[hbm, hbm, hbm, smem, hbm, hbm, hbm],
        out_specs=(vmem, vmem),
        scratch_shapes=[
            pltpu.VMEM(blocks.shape, jnp.int32),
            pltpu.VMEM(blocks.shape, jnp.int32),
            pltpu.VMEM(state.shape, jnp.float32),
            pltpu.VMEM(blocks.shape, jnp.int32),
            pltpu.VMEM((micros, cot_size, n, sample_count), jnp.bfloat16),
            pltpu.VMEM((m, micros, planes) + blocks.shape[3:], jnp.int32),
            pltpu.VMEM((n, micros) + blocks.shape[3:], jnp.int32),
            pltpu.VMEM((n * n, samples), jnp.float32),
            pltpu.VMEM((slab_size, width), jnp.int32),
            pltpu.VMEM((slab_size, width), jnp.bfloat16),
            pltpu.VMEM((planes, UNITS, 2, columns // 2, slab_size), jnp.bfloat16),
            pltpu.VMEM((UNITS, planes, m, columns, samples), jnp.bfloat16),
            pltpu.VMEM(block, jnp.bfloat16),
            pltpu.VMEM((n if keeps else 1, 2 * columns, samples), jnp.float32),
            pltpu.VMEM(block, jnp.bfloat16),
            pltpu.VMEM(block, jnp.bfloat16),
            pltpu.VMEM(held + (slab_size, 2 * samples), jnp.bfloat16),
            pltpu.VMEM(held + (slab_size, 2 * samples), jnp.bfloat16),
            pltpu.VMEM((len(HALVES), slab_size, width // len(HALVES)), jnp.float32),
            pltpu.VMEM((len(HALVES), slab_size, width // len(HALVES)), jnp.float32),
            pltpu.VMEM((slab_size, 128), jnp.float32),
            dma((6,)),
            dma((2, len(HALVES), CHUNKS)),
            dma(()),
            dma(()),
            dma(()),
            dma(()),
            dma((2,)),
            dma((parts, planes)),
            dma(()),
            dma((parts, planes)),
            dma((parts,)),
            dma((parts,)),
            dma((parts,)),
            dma((parts - 1, planes)),
            dma((n,)),
        ],
        compiler_params=pltpu.CompilerParams(collective_id=0, has_side_effects=True),
        name="fused_step",
    )(blocks, offsets, cot, touched, state, table, dither)


def write_kernel(touched_ref, state_ref, blocks_ref, out_ref, state_out_ref, place, sem):
    state_copy = pltpu.make_async_copy(state_ref, state_out_ref, sem.at[1])
    state_copy.start()
    blocks, touch_count = out_ref.shape[0], touched_ref.shape[1]
    for block in range(blocks):
        place[block] = block
    for i in range(touch_count):
        place[touched_ref[0, i]] = blocks + i
    for block in range(blocks):
        source = blocks_ref.at[place[block]]
        pltpu.make_async_copy(source, out_ref.at[block], sem.at[0]).start()
    pltpu.make_async_copy(blocks_ref.at[pl.ds(0, blocks)], out_ref, sem.at[0]).wait()
    state_copy.wait()


def write_table(touched, state, blocks, table):
    vmem = pl.BlockSpec(memory_space=pltpu.VMEM)
    hbm = pl.BlockSpec(memory_space=pltpu.HBM)
    held = [pltpu.with_memory_space_constraint(x, pltpu.VMEM) for x in (state, blocks)]
    return pl.pallas_call(
        write_kernel,
        out_shape=(
            jax.ShapeDtypeStruct(table.shape, table.dtype),
            jax.ShapeDtypeStruct(state.shape, state.dtype),
        ),
        in_specs=[pl.BlockSpec(memory_space=pltpu.SMEM), vmem, vmem],
        out_specs=(hbm, hbm),
        scratch_shapes=[pltpu.SMEM((table.shape[0],), jnp.int32), pltpu.SemaphoreType.DMA((2,))],
        compiler_params=pltpu.CompilerParams(vmem_limit_bytes=4 << 20),
        name="write_table",
    )(touched, *held)


def per_device(
    lookup_block, lookup_offset, interaction_grad, table, adagrad_state, touched_blocks, dither
):
    micro_count, sample_count, feature_count, bag_count = lookup_block.shape
    n = lax.axis_size("mp")
    row_count, emb_width = table.shape
    split = (micro_count, PLANES, feature_count // PLANES, bag_count, sample_count)
    blocks = lookup_block.transpose(0, 2, 3, 1).reshape(split)
    offsets = lookup_offset.transpose(0, 2, 3, 1).reshape(split)
    cot = interaction_grad.transpose(0, 2, 3, 1)
    table_blocks = table.reshape(row_count // BLOCK, BLOCK, emb_width)
    state = adagrad_state.reshape(row_count // (2 * BLOCK), 2 * BLOCK)
    new_state, held_blocks = fused_step(
        n, blocks, offsets, cot, touched_blocks, state, table_blocks, dither[0]
    )
    new_table, new_state = write_table(touched_blocks, new_state, held_blocks, table_blocks)
    return (new_table.reshape(row_count, emb_width), new_state.reshape(row_count))


def solution(mesh):
    return jax.shard_map(
        per_device,
        mesh=mesh,
        in_specs=(
            P(None, ("rep", "mp"), None, None),
            P(None, ("rep", "mp"), None, None),
            P(None, ("rep", "mp"), None, None),
            P("mp", None),
            P("mp"),
            P("mp", None),
            P("mp", None, None),
        ),
        out_specs=(P("mp", None), P("mp")),
        check_vma=False,
    )
```

```python
import functools
import math

import jax
import jax.numpy as jnp
from jax import lax
from jax.experimental import pallas as pl
from jax.experimental.pallas import tpu as pltpu
from jax.sharding import PartitionSpec as P

BLOCK = 64
PLANES = 4
UNITS = 4
UNROLL = 16
CHUNKS = 2
PARTS = ((0, 1), (1, 1), (2, 2))
HALVES = ((0, 2, (0, 1)), (2, 2, (2,)))
LEARN_RATE = 0.1
POOL_DECAY = 0.5
DITHER_UNIT = 2.0 ** (-15)
SMALLEST = 2.0 ** (-14)
KEEP_BYTES = 8 << 20
MESH = pl.DeviceIdType.MESH


def dither_round(weights, dither_bits):
    magnitude = jnp.maximum(jnp.abs(weights), SMALLEST)
    exponent = jnp.floor(jnp.log2(magnitude)) - 7.0
    spacing, per_spacing = jnp.exp2(exponent), jnp.exp2(-exponent)
    grid_level = jnp.floor(weights * per_spacing + dither_bits.astype(jnp.float32) * DITHER_UNIT)
    return (grid_level * spacing).astype(jnp.bfloat16)


def plane_order(planes, plane, step):
    picked = jnp.int32(0)
    for own in range(planes):
        near_first = sorted(range(planes), key=lambda q: (abs(q - own), (q - own) * (2 * own - planes)))
        picked = jnp.where(plane == own, near_first[step], picked)
    return picked


def step_kernel(
    n,
    block_hbm,
    offset_hbm,
    cot_ref,
    touched_ref,
    state_hbm,
    table_ref,
    dither_ref,
    state_out_ref,
    table_in,
    block_ref,
    offset_ref,
    state_ref,
    rows_ref,
    cot_in,
    near,
    far,
    w_ref,
    dither_in,
    slab,
    slabs,
    pooled_out,
    pooled_in,
    wide,
    grad_out,
    grad_in,
    kept,
    kept_own,
    total,
    total_in,
    state_col,
    local_sem,
    pair_sem,
    near_send,
    near_recv,
    far_send,
    far_recv,
    slab_send,
    slab_recv,
    half_send,
    half_recv,
    pooled_send,
    pooled_recv,
    grad_send,
    grad_recv,
    grad_last,
):
    me = lax.axis_index("mp")
    rep = lax.axis_index("rep")
    planes, parts = slabs.shape[0], len(PARTS)
    m = n // planes
    plane = me // m
    local = lax.rem(me, m)
    samples = w_ref.shape[1]
    bags = rows_ref.shape[3]
    slab_size, width = slab.shape
    columns = width // UNITS
    touch_count = slab_size // BLOCK
    keeps = kept.shape[0] == planes

    def at(peer):
        return {"device_id": (rep, peer), "device_id_type": MESH}

    partner = {"device_id": (1 - rep, me), "device_id_type": MESH}

    def each(first, body):
        def run(step, carry):
            body(lax.rem(local + step, m))
            return carry

        lax.fori_loop(first, m, run, 0)

    def others(body):
        def run(step, carry):
            body(lax.rem(me + step, n))
            return carry

        lax.fori_loop(1, n, run, 0)

    def outside(body, first=0, last=n - m):
        def run(step, carry):
            body(lax.rem(plane + 1 + step // m, planes), lax.rem(local + step, m))
            return carry

        lax.fori_loop(first, last, run, 0)

    def nearest(step):
        return plane_order(planes, plane, step)

    def units(part):
        first, count = PARTS[part]
        return pl.ds(first, count)

    def tall(part):
        return PARTS[part][1] * columns

    barrier = pltpu.get_barrier_semaphore()
    others(lambda peer: pl.semaphore_signal(barrier, inc=1, **at(peer)))
    pl.semaphore_signal(barrier, inc=1, **partner)
    table_blocks = table_ref.shape[0]
    held_table = table_in.at[pl.ds(0, table_blocks)]
    table_copy = pltpu.make_async_copy(table_ref, held_table, local_sem.at[0])
    table_copy.start()
    block_copy = pltpu.make_async_copy(block_hbm, block_ref, local_sem.at[1])
    block_copy.start()
    offset_copy = pltpu.make_async_copy(offset_hbm, offset_ref, local_sem.at[2])
    offset_copy.start()
    state_copy = pltpu.make_async_copy(state_hbm, state_ref, local_sem.at[3])
    state_copy.start()
    dither_copy = pltpu.make_async_copy(dither_ref, dither_in, local_sem.at[4])
    dither_copy.start()
    block_copy.wait()
    offset_copy.wait()
    rows_ref[...] = block_ref[...] * BLOCK + offset_ref[...]
    near[local] = rows_ref[:, :, local]
    table_copy.wait()
    for block in range(touch_count):
        slab[block * BLOCK : (block + 1) * BLOCK, :] = table_in[touched_ref[0, block]]
    turned = slab[...].astype(jnp.float32).T.astype(jnp.bfloat16)
    slabs[plane] = turned.reshape(slabs.shape[1:])
    pl.semaphore_wait(barrier, n)

    def near_copy(j, slot):
        return pltpu.make_async_remote_copy(
            rows_ref.at[:, :, j],
            near.at[slot],
            near_send,
            near_recv,
            **at(plane * m + j),
        )

    def far_copy(q, j, slot):
        return pltpu.make_async_remote_copy(
            rows_ref.at[:, q, j],
            far.at[slot],
            far_send,
            far_recv,
            **at(q * m + j),
        )

    def slab_copy(part, q, slot, peer):
        return pltpu.make_async_remote_copy(
            slabs.at[q, units(part), rep],
            slabs.at[q, units(part), rep],
            slab_send.at[slot],
            slab_recv.at[part, q],
            **at(peer),
        )

    def half_copy(part, q, which):
        return pltpu.make_async_remote_copy(
            slabs.at[q, units(part), which],
            slabs.at[q, units(part), which],
            half_send,
            half_recv.at[part, q],
            **partner,
        )

    has_up, has_down = plane + 1 < planes, plane > 0
    inner = jnp.logical_and(has_up, has_down)
    outer = jnp.logical_not(inner)
    up, down = lax.rem(me + m, n), lax.rem(me + n - m, n)

    def own_slab(part, act):
        @pl.when(has_up)
        def _():
            act(slab_copy(part, plane, 0, up))

        @pl.when(has_down)
        def _():
            act(slab_copy(part, plane, 0, down))

    def passed_slab(part, q, act):
        @pl.when(jnp.logical_and(q < plane, has_up))
        def _():
            act(slab_copy(part, q, 1, up))

        @pl.when(jnp.logical_and(q > plane, has_down))
        def _():
            act(slab_copy(part, q, 1, down))

    each(1, lambda j: near_copy(j, local).start())
    own_slab(0, lambda copy: copy.start())
    outside(lambda q, j: far_copy(q, j, me).start())
    cot_size = cot_in.shape[1]

    def spread(chunk, carry):
        cot_copy = pltpu.make_async_copy(
            cot_ref.at[:, pl.ds(chunk * cot_size, cot_size)], cot_in, local_sem.at[5]
        )
        cot_copy.start()
        cot_copy.wait()
        for i in range(cot_size):
            pieces = [cot_in[micro, i].astype(jnp.float32) for micro in range(cot_in.shape[0])]
            at_row = pl.multiple_of((chunk * cot_size + i) * n, n)
            w_ref[pl.ds(at_row, n), :] = jnp.concatenate(pieces, axis=-1)
        return carry

    lax.fori_loop(0, n // cot_size, spread, 0)
    place = lax.broadcasted_iota(jnp.int32, (n, samples), 0)

    def fold(f, carry):
        along = pl.ds(pl.multiple_of(f * n, n), n)
        across = pl.ds(f, n, stride=n)
        row, column = w_ref[along, :], w_ref[across, :]
        both = row + column + jnp.where(place == f, POOL_DECAY, 0.0)
        w_ref[along, :] = jnp.where(place >= f, both, row)
        w_ref[across, :] = jnp.where(place >= f, both, column)
        return carry

    lax.fori_loop(0, n, fold, 0)
    for part in range(1, parts):
        own_slab(part, lambda copy: copy.start())
    total[...] = jnp.zeros_like(total)

    sublanes = 16
    place_of = lax.broadcasted_iota(jnp.int32, (BLOCK, samples), 0)
    place_of = place_of.astype(jnp.float32).astype(jnp.bfloat16)
    one = jnp.ones((sublanes, samples), jnp.bfloat16)
    none = jnp.zeros_like(one)

    def hits(micros):
        rows = jnp.concatenate([micros[i] for i in range(micros.shape[0])], axis=-1)
        block_of = (rows // BLOCK).astype(jnp.float32)
        offset_of = lax.rem(rows, BLOCK).astype(jnp.float32)

        def wide(values, lookup):
            row = jnp.broadcast_to(values[lookup : lookup + 1, :], (sublanes, samples))
            return row.astype(jnp.bfloat16)

        spans = [slice(at, at + sublanes) for at in range(0, BLOCK, sublanes)]
        offsets = [wide(offset_of, lookup) for lookup in range(bags)]
        same = [[jnp.where(offset == place_of[span], one, none) for span in spans] for offset in offsets]
        in_block = [wide(block_of, lookup) for lookup in range(bags)]
        pieces = []
        for block in range(slab_size // BLOCK):
            chosen = [row == jnp.full_like(row, block) for row in in_block]
            for at in range(len(spans)):
                terms = [jnp.where(chosen[k], same[k][at], none) for k in range(bags)]
                while len(terms) > 1:
                    terms = [sum(terms[k + 1 : k + 2], terms[k]) for k in range(0, len(terms), 2)]
                pieces.append(terms[0])
        return jnp.concatenate(pieces, axis=0)

    def pooled_copy(part, q, j, slot):
        return pltpu.make_async_remote_copy(
            pooled_out.at[units(part), q, j],
            pooled_in.at[units(part), q * m + slot],
            pooled_send.at[part],
            pooled_recv.at[part],
            **at(plane * m + j),
        )

    def grad_copy(part, peer, slot):
        return pltpu.make_async_remote_copy(
            grad_out.at[units(part), peer],
            grad_in.at[units(part), slot],
            grad_send.at[part],
            grad_last.at[slot] if part == parts - 1 else grad_recv.at[part, slot // m],
            **at(peer),
        )

    def member(at):
        return lax.rem(local + at, m)

    def pairs(body):
        def run(pair, carry):
            body(pair)
            return carry

        lax.fori_loop(0, m // 2, run, 0)

    def near_pair(q, pair):
        return [hits(near[member(2 * pair + k), :, q]) for k in (1, 2)]

    def pool(part, q):
        rows_of = slabs[q, units(part)].reshape(tall(part), slab_size)

        def both(pair):
            if keeps and part > 0:
                counted = kept[q, pair]
            else:
                counted = jnp.concatenate(near_pair(q, pair), axis=1)
                if keeps:
                    kept[q, pair] = counted
            summed = jnp.dot(rows_of, counted, preferred_element_type=jnp.float32)
            summed = summed.astype(jnp.bfloat16).reshape(-1, columns, 2 * samples)
            first, second = member(2 * pair + 1), member(2 * pair + 2)
            pooled_out[units(part), q, first] = summed[:, :, :samples]
            pooled_copy(part, q, first, local).start()
            pooled_out[units(part), q, second] = summed[:, :, samples:]

            @pl.when(2 * pair + 2 < m)
            def _():
                pooled_copy(part, q, second, local).start()

        pairs(both)
        pooled_in[units(part), q * m + local] = pooled_out[units(part), q, local]

    def relay(part, step):
        q = nearest(step)
        slab_copy(part, q, 1, up).wait_recv()
        passed_slab(part, q, lambda copy: copy.start())
        half_copy(part, q, rep).start()

    def pool_from(part, step):
        q = nearest(step)
        half_copy(part, q, 1 - rep).wait_recv()
        pool(part, q)

    def batch(ref, send_sem, recv_sem):
        return pltpu.make_async_remote_copy(ref, ref, send_sem, recv_sem, **partner)

    def arrive(part):
        arrived = pooled_in.at[units(part), pl.ds(0, planes * (m - 1))]
        batch(arrived, pooled_send.at[part], pooled_recv.at[part]).wait_recv()
        widen(part)

    def wide_rows(part):
        start = PARTS[part][0] * columns % wide.shape[1]
        return slice(start, start + tall(part))

    def widen(part):
        if wide.shape[0] == n:

            def run(other, carry):
                seen = pooled_in[units(part), other].reshape(tall(part), samples)
                wide[other, wide_rows(part)] = seen.astype(jnp.float32)
                return carry

            lax.fori_loop(0, n, run, 0, unroll=4)

    def interact(part, first=True, rest=True):
        def mixed(feature):
            def add(other, carry):
                weight = w_ref[pl.ds(feature * n + other, 1), :]
                if wide.shape[0] == n:
                    return carry + weight * wide[other, wide_rows(part)]
                seen = pooled_in[units(part), other].reshape(tall(part), samples)
                return carry + weight * seen.astype(jnp.float32)

            start = jnp.zeros((tall(part), samples), jnp.float32)
            mix = lax.fori_loop(0, n, add, start, unroll=UNROLL)
            return mix.astype(jnp.bfloat16).reshape(-1, columns, samples)

        def send(peer):
            grad_out[units(part), peer] = mixed(peer)
            grad_copy(part, peer, me).start()

        for step in range(planes - 1, 0, -1):
            if first if step > 1 else rest:
                q = jnp.where(outer, nearest(step if step < 2 else planes + 1 - step), nearest(step))
                each(0, lambda j: send(q * m + j))
        if rest:
            each(1, lambda j: send(plane * m + j))
            grad_in[units(part), me] = mixed(me)

    def far_pair(q, pair):
        counted = [hits(far[q * m + member(2 * pair + k)]) for k in (0, 1)]
        return jnp.concatenate(counted, axis=1)

    def keep_far():
        for step in range(1, planes):
            q = nearest(step)

            def take(pair):
                kept_own[q, pair] = far_pair(q, pair)

            if keeps:
                pairs(take)

    def collect(which):
        first_unit, count, members = HALVES[which]

        def add(first, second, counted):
            grads = [grad_in[pl.ds(first_unit, count), peer] for peer in (first, second)]
            grads = [piece.reshape(count * columns, samples) for piece in grads]
            total[which] += lax.dot_general(
                counted,
                jnp.concatenate(grads, axis=1),
                (((1,), (1,)), ((), ())),
                preferred_element_type=jnp.float32,
            )

        def plane_ready(q, blocks):
            for part in members:
                if part < parts - 1:
                    arrived = grad_in.at[units(part), pl.ds(0, blocks)]
                    batch(arrived, grad_send.at[part], grad_recv.at[part, q]).wait_recv()

        def ready(peer):
            if parts - 1 in members:
                grad_copy(parts - 1, peer, peer).wait_recv()

        def take_near(pair):
            first, second = (plane * m + member(2 * pair + k) for k in (1, 2))
            ready(first)
            pl.when(2 * pair + 2 < m)(lambda: ready(second))
            if keeps:
                add(first, second, kept[plane, pair])
            else:
                add(first, second, jnp.concatenate(near_pair(plane, pair), axis=1))

        def take_far(q, pair):
            first, second = (q * m + member(2 * pair + k) for k in (0, 1))
            ready(first)
            ready(second)
            add(first, second, kept_own[q, pair] if keeps else far_pair(q, pair))

        plane_ready(plane, m - 1)
        pairs(take_near)
        for step in range(1, planes):
            q = jnp.where(inner, nearest(step % (planes - 1) + 1), nearest(step))
            plane_ready(q, m)
            pairs(lambda pair: take_far(q, pair))

    batch(near.at[pl.ds(0, m - 1)], near_send, near_recv).wait_recv()
    pool(0, plane)
    relay(0, 1)

    @pl.when(inner)
    def _():
        relay(0, 2)
        pool(1, plane)
        relay(1, 1)
        relay(1, 2)
        pool_from(0, 1)
        pool_from(0, 2)
        relay(0, 3)
        relay(2, 1)
        relay(2, 2)
        pool_from(1, 1)
        relay(1, 3)
        pool_from(0, 3)
        pool_from(1, 2)
        pool_from(1, 3)
        pool(2, plane)
        relay(2, 3)
        arrive(0)
        interact(0)
        pool_from(2, 1)
        arrive(1)
        interact(1)
        pool_from(2, 2)
        pool_from(2, 3)

    @pl.when(outer)
    def _():
        pool(1, plane)
        relay(1, 1)
        pool_from(0, 1)
        relay(2, 1)
        pool_from(1, 1)
        relay(0, 2)
        relay(1, 2)
        pool_from(0, 2)
        pool_from(1, 2)
        pool(2, plane)
        relay(0, 3)
        relay(2, 2)
        relay(1, 3)
        pool_from(0, 3)
        pool_from(1, 3)
        pool_from(2, 1)
        pool_from(2, 2)
        arrive(0)
        interact(0, rest=False)
        relay(2, 3)
        pool_from(2, 3)
        arrive(1)
        interact(1, rest=False)
        interact(0, first=False)
        interact(1, first=False)

    arrive(2)
    interact(2)
    batch(far.at[pl.ds(0, n - m)], far_send, far_recv).wait_recv()
    keep_far()
    state_copy.wait()
    pieces = []
    for block in range(touch_count):
        at_block = touched_ref[0, block]
        pair = state_ref[pl.ds(at_block // 2, 1), :]
        pieces.append(jnp.where(lax.rem(at_block, 2) == 0, pair[:, :BLOCK], pair[:, BLOCK:]))
    state_row = jnp.concatenate(pieces, axis=1)
    state_col[...] = jnp.broadcast_to(state_row, (state_col.shape[1], slab_size)).T
    chunk = touch_count // CHUNKS * BLOCK

    def total_copy(which, at):
        span = pl.ds(at * chunk, chunk)
        return pltpu.make_async_remote_copy(
            total.at[which, span],
            total_in.at[which, span],
            pair_sem.at[0, which, at],
            pair_sem.at[1, which, at],
            **partner,
        )

    collect(0)
    for at_chunk in range(CHUNKS):
        total_copy(0, at_chunk).start()
    batch(near.at[pl.ds(0, m - 1)], near_send, near_recv).wait_send()
    batch(far.at[pl.ds(0, n - m)], far_send, far_recv).wait_send()
    batch(slabs.at[pl.ds(0, planes - 1), :, 0], half_send, half_recv.at[0, 0]).wait_send()
    any_slab = slab_recv.at[0, 0]

    @pl.when(inner)
    def _():
        batch(slabs.at[pl.ds(0, 2), :, 0], slab_send.at[0], any_slab).wait_send()
        batch(slabs.at[pl.ds(0, planes - 1), :, 0], slab_send.at[1], any_slab).wait_send()

    @pl.when(outer)
    def _():
        batch(slabs.at[0, :, 0], slab_send.at[0], any_slab).wait_send()

    for part in range(parts):
        sent = pooled_out.at[units(part), :, pl.ds(0, m - 1)]
        batch(sent, pooled_send.at[part], pooled_recv.at[part]).wait_send()

    def grads_sent(part):
        sent = grad_out.at[units(part), pl.ds(0, n - 1)]
        batch(sent, grad_send.at[part], grad_last.at[0]).wait_send()

    grads_sent(0)
    grads_sent(1)
    dither_copy.wait()
    collect(1)
    for at_chunk in range(CHUNKS):
        total_copy(1, at_chunk).start()
    grads_sent(2)
    def update(block, carry):
        at_rows = pl.ds(pl.multiple_of(block * BLOCK, BLOCK), BLOCK)
        grad = [total[h, at_rows, :] + total_in[h, at_rows, :] for h in range(len(HALVES))]
        grad = jnp.concatenate(grad, axis=1)
        state_next = state_col[at_rows, :] + jnp.sum(grad * grad, axis=1, keepdims=True) / width
        state_col[at_rows, :] = state_next
        rate = LEARN_RATE / (jnp.sqrt(state_next) + 1e-08)
        rate = jnp.concatenate([rate] * (width // rate.shape[1]), axis=1)
        moved = slab[at_rows, :].astype(jnp.float32) - grad * rate
        table_in[table_blocks + block] = dither_round(moved, dither_in[at_rows, :])
        return carry

    per_chunk = touch_count // CHUNKS
    for at_chunk in range(CHUNKS):
        for which in range(len(HALVES)):
            total_copy(which, at_chunk).wait_recv()
        lax.fori_loop(at_chunk * per_chunk, (at_chunk + 1) * per_chunk, update, 0, unroll=True)
    state_all = state_ref[...]
    block_at = 2 * lax.broadcasted_iota(jnp.int32, state_all.shape, 0)
    block_at = block_at + lax.broadcasted_iota(jnp.int32, state_all.shape, 1) // BLOCK
    state_row = state_col[...].T[:1, :]
    for block in range(touch_count):
        piece = state_row[:, block * BLOCK : (block + 1) * BLOCK]
        piece = jnp.broadcast_to(jnp.concatenate([piece, piece], axis=1), state_all.shape)
        state_all = jnp.where(block_at == touched_ref[0, block], piece, state_all)
    state_out_ref[...] = state_all
    for which in range(len(HALVES)):
        for at_chunk in range(CHUNKS):
            total_copy(which, at_chunk).wait_send()


def fused_step(n, blocks, offsets, cot, touched, state, table, dither):
    micros, planes, m = blocks.shape[0], blocks.shape[1], blocks.shape[2]
    sample_count = blocks.shape[-1]
    samples = micros * sample_count
    cot_size = math.gcd(n, 16)
    slab_size, width = dither.shape
    columns, parts = width // UNITS, len(PARTS)
    keeps = 2 * n * slab_size * samples <= KEEP_BYTES
    held = (planes, m // 2) if keeps else (1, 1)
    dma = pltpu.SemaphoreType.DMA
    block = (UNITS, n, columns, samples)
    vmem = pl.BlockSpec(memory_space=pltpu.VMEM)
    smem = pl.BlockSpec(memory_space=pltpu.SMEM)
    hbm = pl.BlockSpec(memory_space=pltpu.HBM)
    return pl.pallas_call(
        functools.partial(step_kernel, n),
        out_shape=(
            pltpu.VMEM(state.shape, jnp.float32),
            pltpu.VMEM((table.shape[0] + slab_size // BLOCK,) + table.shape[1:], jnp.bfloat16),
        ),
        in_specs=[hbm, hbm, hbm, smem, hbm, hbm, hbm],
        out_specs=(vmem, vmem),
        scratch_shapes=[
            pltpu.VMEM(blocks.shape, jnp.int32),
            pltpu.VMEM(blocks.shape, jnp.int32),
            pltpu.VMEM(state.shape, jnp.float32),
            pltpu.VMEM(blocks.shape, jnp.int32),
            pltpu.VMEM((micros, cot_size, n, sample_count), jnp.bfloat16),
            pltpu.VMEM((m, micros, planes) + blocks.shape[3:], jnp.int32),
            pltpu.VMEM((n, micros) + blocks.shape[3:], jnp.int32),
            pltpu.VMEM((n * n, samples), jnp.float32),
            pltpu.VMEM((slab_size, width), jnp.int32),
            pltpu.VMEM((slab_size, width), jnp.bfloat16),
            pltpu.VMEM((planes, UNITS, 2, columns // 2, slab_size), jnp.bfloat16),
            pltpu.VMEM((UNITS, planes, m, columns, samples), jnp.bfloat16),
            pltpu.VMEM(block, jnp.bfloat16),
            pltpu.VMEM((n if keeps else 1, 2 * columns, samples), jnp.float32),
            pltpu.VMEM(block, jnp.bfloat16),
            pltpu.VMEM(block, jnp.bfloat16),
            pltpu.VMEM(held + (slab_size, 2 * samples), jnp.bfloat16),
            pltpu.VMEM(held + (slab_size, 2 * samples), jnp.bfloat16),
            pltpu.VMEM((len(HALVES), slab_size, width // len(HALVES)), jnp.float32),
            pltpu.VMEM((len(HALVES), slab_size, width // len(HALVES)), jnp.float32),
            pltpu.VMEM((slab_size, 128), jnp.float32),
            dma((6,)),
            dma((2, len(HALVES), CHUNKS)),
            dma(()),
            dma(()),
            dma(()),
            dma(()),
            dma((2,)),
            dma((parts, planes)),
            dma(()),
            dma((parts, planes)),
            dma((parts,)),
            dma((parts,)),
            dma((parts,)),
            dma((parts - 1, planes)),
            dma((n,)),
        ],
        compiler_params=pltpu.CompilerParams(collective_id=0, has_side_effects=True),
        name="fused_step",
    )(blocks, offsets, cot, touched, state, table, dither)


def write_kernel(touched_ref, state_ref, blocks_ref, out_ref, state_out_ref, place, sem):
    state_copy = pltpu.make_async_copy(state_ref, state_out_ref, sem.at[1])
    state_copy.start()
    blocks, touch_count = out_ref.shape[0], touched_ref.shape[1]
    for block in range(blocks):
        place[block] = block
    for i in range(touch_count):
        place[touched_ref[0, i]] = blocks + i
    for block in range(blocks):
        source = blocks_ref.at[place[block]]
        pltpu.make_async_copy(source, out_ref.at[block], sem.at[0]).start()
    pltpu.make_async_copy(blocks_ref.at[pl.ds(0, blocks)], out_ref, sem.at[0]).wait()
    state_copy.wait()


def write_table(touched, state, blocks, table):
    vmem = pl.BlockSpec(memory_space=pltpu.VMEM)
    hbm = pl.BlockSpec(memory_space=pltpu.HBM)
    held = [pltpu.with_memory_space_constraint(x, pltpu.VMEM) for x in (state, blocks)]
    return pl.pallas_call(
        write_kernel,
        out_shape=(
            jax.ShapeDtypeStruct(table.shape, table.dtype),
            jax.ShapeDtypeStruct(state.shape, state.dtype),
        ),
        in_specs=[pl.BlockSpec(memory_space=pltpu.SMEM), vmem, vmem],
        out_specs=(hbm, hbm),
        scratch_shapes=[pltpu.SMEM((table.shape[0],), jnp.int32), pltpu.SemaphoreType.DMA((2,))],
        compiler_params=pltpu.CompilerParams(vmem_limit_bytes=4 << 20),
        name="write_table",
    )(touched, *held)


def per_device(
    lookup_block, lookup_offset, interaction_grad, table, adagrad_state, touched_blocks, dither
):
    micro_count, sample_count, feature_count, bag_count = lookup_block.shape
    n = lax.axis_size("mp")
    row_count, emb_width = table.shape
    split = (micro_count, PLANES, feature_count // PLANES, bag_count, sample_count)
    blocks = lookup_block.transpose(0, 2, 3, 1).reshape(split)
    offsets = lookup_offset.transpose(0, 2, 3, 1).reshape(split)
    cot = interaction_grad.transpose(0, 2, 3, 1)
    table_blocks = table.reshape(row_count // BLOCK, BLOCK, emb_width)
    state = adagrad_state.reshape(row_count // (2 * BLOCK), 2 * BLOCK)
    new_state, held_blocks = fused_step(
        n, blocks, offsets, cot, touched_blocks, state, table_blocks, dither[0]
    )
    new_table, new_state = write_table(touched_blocks, new_state, held_blocks, table_blocks)
    return (new_table.reshape(row_count, emb_width), new_state.reshape(row_count))


def solution(mesh):
    return jax.shard_map(
        per_device,
        mesh=mesh,
        in_specs=(
            P(None, ("rep", "mp"), None, None),
            P(None, ("rep", "mp"), None, None),
            P(None, ("rep", "mp"), None, None),
            P("mp", None),
            P("mp"),
            P("mp", None),
            P("mp", None, None),
        ),
        out_specs=(P("mp", None), P("mp")),
        check_vma=False,
    )
```
